512 devices in a mesh: frame: 32 (over x, z), patch: 16 (over y, core).
Axes of the slice: x: 4, y: 8, z: 8, core: 2. Of those that a mesh axis runs over, the one named last changes fastest.
Arguments:
- coeffs: float32 [16, 16, 32, 36], P('patch', None, 'frame'), may hold values from -1.8 to 1.8
- shifts: int32 [16, 16, 32, 2], P('patch', None, 'frame'), may hold values from -4 to 4
- pixels: bfloat16 [16, 16, 32, 128, 128], P('patch', None, 'frame'), may hold values from -6 to 6
- pupil_mask: int32 [64, 64], replicated, may hold values from 0 to 1, as said below
- chan_map: int32 [16], replicated, may hold values from 0 to 1, as said below
- intersection: int32 [16, 32], P('patch', 'frame'), may hold values from 4 to 16
Outputs:
- blended: float32 [2, 1536, 3072], P(None, 'patch', 'frame')
- coeff_grad: float32 [16, 16, 32, 36], P('patch', None, 'frame')
The draws below stay inside these ranges and needn't reach their ends.
Inputs may be any that keep to these rules, and one draw needn't show every extreme that they name: pupil_mask is 1 exactly on the cells whose centres lie in the disc of diameter 64 about the grid's centre, outside a central disc whose radius in cells is drawn from 8 to 21, and off one row and one column of cells (support vanes) whose positions are drawn from 0 to 63. `chan_map`: every channel is named by exactly 8 slots.
All inputs are finite; a program needn't handle non-finite values.
Results may differ from the reference program's by a relative error of at most 0.0003.
Values may be sent and summed in bfloat16 or wider, within the bound.
No kernel may reach another device: no remote copies, remote signals or barrier semaphores. Data moves between devices by JAX's collectives and lax.ppermute only.
A program may use at most 64 MiB of HBM per device.

```python
import math
import jax
import jax.numpy as jnp
from jax import lax

N = 128
ZERN = 36
FRAMES = 8
CHANNELS = 2
MARGIN = 16
PUP = 64
TILE = 96
FC = 16
ROWS = 16
COLS = 32


def draw_pupil_mask(key, part):
    hole_radius = jax.random.randint(jax.random.fold_in(key, 11), (), PUP // 8, PUP // 3 + 1)
    vane_row = jax.random.randint(jax.random.fold_in(key, 13), (), 0, PUP)
    vane_col = jax.random.randint(jax.random.fold_in(key, 17), (), 0, PUP)
    counter = jnp.arange(PUP, dtype=jnp.int32)
    doubled = 2 * counter - (PUP - 1)
    radius_sq = doubled[:, None] * doubled[:, None] + doubled[None, :] * doubled[None, :]
    inside = (radius_sq <= PUP * PUP) & (radius_sq >= 4 * hole_radius * hole_radius)
    inside = inside & (counter[:, None] != vane_row) & (counter[None, :] != vane_col)
    return inside.astype(jnp.int32)


def draw_chan_map(key, part):
    shuffled = jax.random.permutation(jax.random.fold_in(key, 5), FC)
    return (shuffled // FRAMES).astype(jnp.int32)


def touch_ends(array, rng, smallest, top_value):
    shape = array.shape
    spot = [jax.random.randint(jax.random.fold_in(rng, axis), (), 0, shape[axis]) for axis in range(len(shape))]
    array = array.at[tuple(spot)].set(smallest)
    longest = shape.index(max(shape))
    spot[longest] = (spot[longest] + 1) % shape[longest]
    return array.at[tuple(spot)].set(top_value)


def block_scale(stream_key, dims, split, smallest, largest):
    def one(dim, shards_of):
        draws = jax.random.uniform(jax.random.fold_in(jax.random.fold_in(stream_key, 6), dim), (shards_of,), jnp.float32, smallest / len(split), largest / len(split))
        return jnp.repeat(jnp.exp(draws), dims[dim] // shards_of).reshape((-1,) + (1,) * (len(dims) - dim - 1))

    factor_of = one(*split[0])
    for cut in split[1:]:
        factor_of = factor_of * one(*cut)
    return factor_of


def noise(own_key, dims, deviation, reach, pieces=(), kind=jnp.bfloat16):
    loudness = block_scale(own_key, dims, pieces, -0.22, 0.18) if pieces else 1.0
    array = jax.random.normal(own_key, dims, jnp.float32) * deviation * loudness
    return jnp.minimum(jnp.maximum(array, -reach), reach).astype(kind)


def setup_inputs(seed: int = 0) -> dict:
    streams_of = jax.random.split(jax.random.key(seed), 7)
    return {
        "coeffs": noise(streams_of[0], (FC, ROWS, COLS, ZERN), 0.3, 1.8, ((0, 16), (2, 32)), jnp.float32),
        "shifts": touch_ends(jax.random.randint(streams_of[1], (FC, ROWS, COLS, 2), -4, 5), jax.random.fold_in(streams_of[1], 1), -4, 4).astype(jnp.int32),
        "pixels": noise(streams_of[2], (FC, ROWS, COLS, N, N), 1.0, 6.0, ((0, 16), (2, 32))),
        "pupil_mask": draw_pupil_mask(jax.random.fold_in(streams_of[6], 71), 0),
        "chan_map": draw_chan_map(jax.random.fold_in(streams_of[6], 71), 0),
        "intersection": touch_ends(jax.random.randint(streams_of[5], (ROWS, COLS), MARGIN // 4, MARGIN + 1), jax.random.fold_in(streams_of[5], 1), MARGIN // 4, MARGIN).astype(jnp.int32),
    }


highest = lax.Precision.HIGHEST
regular_gamma = 0.1
wave_ratio = 0.35

def product(form, left, right):
    return jnp.einsum(form, left, right, precision=highest)

def noll_order(noll_index):
    radial = 0
    remain = noll_index - 1
    while remain > radial:
        radial += 1
        remain -= radial
    azimuth = radial % 2 + 2 * ((remain + (radial + 1) % 2) // 2)
    if noll_index % 2 == 1:
        azimuth = -azimuth
    return (radial, azimuth)

def zernike_basis(mode_count, pupil_side):
    position = (jnp.arange(pupil_side, dtype=jnp.int32).astype(jnp.float32) - (pupil_side - 1) / 2.0) / (pupil_side / 2.0)
    grid_y = position[:, None] + jnp.zeros((1, pupil_side), jnp.float32)
    grid_x = jnp.zeros((pupil_side, 1), jnp.float32) + position[None, :]
    radius = jnp.sqrt(grid_x * grid_x + grid_y * grid_y)
    angle_map = jnp.arctan2(grid_y, grid_x)
    collected = []
    for noll_index in range(2, mode_count + 2):
        radial, azimuth = noll_order(noll_index)
        order_abs = abs(azimuth)
        radial_sum = jnp.zeros_like(radius)
        for power_step in range((radial - order_abs) // 2 + 1):
            factor = math.factorial(radial - power_step) / (math.factorial(power_step) * math.factorial((radial + order_abs) // 2 - power_step) * math.factorial((radial - order_abs) // 2 - power_step))
            if power_step % 2 == 1:
                factor = -factor
            radial_sum = radial_sum + factor * radius ** (radial - 2 * power_step)
        if azimuth == 0:
            shaped = radial_sum * math.sqrt(radial + 1.0)
        elif azimuth > 0:
            shaped = radial_sum * math.sqrt(2.0 * (radial + 1.0)) * jnp.cos(order_abs * angle_map)
        else:
            shaped = radial_sum * math.sqrt(2.0 * (radial + 1.0)) * jnp.sin(order_abs * angle_map)
        collected.append(shaped.reshape(-1))
    return jnp.stack(collected)

def dft_tables(length, width):
    frequency = jnp.arange(length, dtype=jnp.int32)[:, None]
    position = jnp.arange(width, dtype=jnp.int32)[None, :]
    turns = (frequency * position % length).astype(jnp.float32) * (2.0 * math.pi / length)
    return (jnp.cos(turns), -jnp.sin(turns))

def real_transform(image, length):
    full_re, full_im = dft_tables(length, length)
    inner_re = product('bxy,vy->bxv', image, full_re)
    inner_im = product('bxy,vy->bxv', image, full_im)
    out_re = product('ux,bxv->buv', full_re, inner_re) - product('ux,bxv->buv', full_im, inner_im)
    out_im = product('ux,bxv->buv', full_re, inner_im) + product('ux,bxv->buv', full_im, inner_re)
    return (out_re, out_im)

def build_otf(coeff_in, scale_in, shift_in, zernike, mask_flat, length):
    pupil_side = length // 2
    batch_size = coeff_in.shape[0]
    phase_map = jnp.dot(coeff_in, zernike, precision=highest) * scale_in[:, None]
    pupil_re = (mask_flat * jnp.cos(phase_map)).reshape(batch_size, pupil_side, pupil_side)
    pupil_im = (mask_flat * jnp.sin(phase_map)).reshape(batch_size, pupil_side, pupil_side)
    left_re, left_im = dft_tables(length, pupil_side)
    half_re = product('bxy,vy->bxv', pupil_re, left_re) - product('bxy,vy->bxv', pupil_im, left_im)
    half_im = product('bxy,vy->bxv', pupil_re, left_im) + product('bxy,vy->bxv', pupil_im, left_re)
    field_re = product('ux,bxv->buv', left_re, half_re) - product('ux,bxv->buv', left_im, half_im)
    field_im = product('ux,bxv->buv', left_re, half_im) + product('ux,bxv->buv', left_im, half_re)
    intensity = field_re * field_re + field_im * field_im
    point_spread = intensity / lax.optimization_barrier(jnp.sum(intensity, axis=(1, 2), keepdims=True))
    otf_re, otf_im = real_transform(point_spread, length)
    frequency = jnp.arange(length, dtype=jnp.int32).astype(jnp.float32)
    angle_y = 2.0 * math.pi / length * shift_in[:, 0:1] * frequency[None, :]
    angle_x = 2.0 * math.pi / length * shift_in[:, 1:2] * frequency[None, :]
    total_angle = angle_y[:, :, None] + angle_x[:, None, :]
    tilt_re = jnp.cos(total_angle)
    tilt_im = -jnp.sin(total_angle)
    return (otf_re * tilt_re - otf_im * tilt_im, otf_re * tilt_im + otf_im * tilt_re)

def data_spectrum(pixel_in, length, margin):
    position = jnp.arange(length, dtype=jnp.int32)
    distance = jnp.minimum(position, length - 1 - position).astype(jnp.float32)
    taper_row = jnp.where(distance < margin, 0.5 - 0.5 * jnp.cos(math.pi * (distance + 0.5) / margin), 1.0)
    image = pixel_in.astype(jnp.float32) * taper_row[:, None] * taper_row[None, :]
    return real_transform(image, length)

def wiener_object(otf_re, otf_im, spec_re, spec_im, onehot):
    cross_re = otf_re * spec_re + otf_im * spec_im
    cross_im = otf_re * spec_im - otf_im * spec_re
    intensity = otf_re * otf_re + otf_im * otf_im
    num_re = product('kc,kbuv->cbuv', onehot, cross_re)
    num_im = product('kc,kbuv->cbuv', onehot, cross_im)
    denominator = product('kc,kbuv->cbuv', onehot, intensity) + regular_gamma
    return (num_re / denominator, num_im / denominator)

def object_image(obj_re, obj_im, length):
    full_re, full_im = dft_tables(length, length)
    back_re = product('ux,bxv->buv', full_re, obj_re) + product('ux,bxv->buv', full_im, obj_im)
    back_im = product('ux,bxv->buv', full_re, obj_im) - product('ux,bxv->buv', full_im, obj_re)
    return (product('bux,vx->buv', back_re, full_re) + product('bux,vx->buv', back_im, full_im)) / (length * length)

def window_weight(width_in, length):
    position = jnp.arange(length, dtype=jnp.int32)
    distance = (jnp.minimum(position, length - 1 - position) + 1).astype(jnp.float32)
    ramp_row = jnp.minimum(1.0, distance / (width_in.astype(jnp.float32) + 1.0))
    return ramp_row[:, None] * ramp_row[None, :]

def reference(coeffs, shifts, pixels, pupil_mask, chan_map, intersection):
    length = N
    zernike = zernike_basis(ZERN, PUP)
    mask_flat = pupil_mask.reshape(-1).astype(jnp.float32)
    scale_all = 1.0 / (1.0 + wave_ratio * chan_map.astype(jnp.float32))
    onehot = (chan_map[:, None] == jnp.arange(CHANNELS, dtype=jnp.int32)[None, :]).astype(jnp.float32)
    patch_count = ROWS * COLS
    coeff_patch = jnp.transpose(coeffs, (1, 2, 0, 3)).reshape(patch_count, FC, ZERN)
    shift_patch = jnp.transpose(shifts, (1, 2, 0, 3)).reshape(patch_count, FC, 2).astype(jnp.float32)
    pixel_patch = jnp.transpose(pixels, (1, 2, 0, 3, 4)).reshape(patch_count, FC, N, N)
    width_patch = intersection.reshape(patch_count)
    loss_scale = 1.0 / float(length * length * length)

    def one_patch(packed):
        coeff_one, shift_one, pixel_one, width_one = packed
        spec_re, spec_im = data_spectrum(pixel_one, length, MARGIN)
        spec_re = spec_re[:, None]
        spec_im = spec_im[:, None]

        def metric(coeff_in):
            otf_re, otf_im = build_otf(coeff_in, scale_all, shift_one, zernike, mask_flat, length)
            otf_re = otf_re[:, None]
            otf_im = otf_im[:, None]
            obj_re, obj_im = wiener_object(otf_re, otf_im, spec_re, spec_im, onehot)
            obj_re = lax.stop_gradient(obj_re)
            obj_im = lax.stop_gradient(obj_im)
            per_re = product('kc,cbuv->kbuv', onehot, obj_re)
            per_im = product('kc,cbuv->kbuv', onehot, obj_im)
            res_re = spec_re - (per_re * otf_re - per_im * otf_im)
            res_im = spec_im - (per_re * otf_im + per_im * otf_re)
            total = jnp.sum(res_re * res_re + res_im * res_im) + regular_gamma * jnp.sum(obj_re * obj_re + obj_im * obj_im)
            return (total * loss_scale, (obj_re, obj_im))
        grad_one, objects = jax.grad(metric, has_aux=True)(coeff_one)
        image = object_image(objects[0][:, 0], objects[1][:, 0], length)
        weight = window_weight(width_one, length)
        stacked = jnp.concatenate([image * weight[None], weight[None]], axis=0)
        return (grad_one, stacked)
    grads, windows = lax.map(one_patch, (coeff_patch, shift_patch, pixel_patch, width_patch))
    height = ROWS * TILE + 2 * MARGIN
    breadth = COLS * TILE + 2 * MARGIN
    canvas = jnp.zeros((CHANNELS + 1, height, breadth), jnp.float32)

    def place(counter, canvas_in):
        row_at = (counter // COLS * TILE).astype(jnp.int32)
        col_at = (counter % COLS * TILE).astype(jnp.int32)
        start = (jnp.zeros((), jnp.int32), row_at, col_at)
        current = lax.dynamic_slice(canvas_in, start, (CHANNELS + 1, N, N))
        return lax.dynamic_update_slice(canvas_in, current + windows[counter], start)
    canvas = lax.fori_loop(0, patch_count, place, canvas)
    inner = canvas[:, MARGIN:MARGIN + ROWS * TILE, MARGIN:MARGIN + COLS * TILE]
    blended = inner[:CHANNELS] / inner[CHANNELS][None]
    coeff_grad = jnp.transpose(grads.reshape(ROWS, COLS, FC, ZERN), (2, 0, 1, 3))
    return (blended, coeff_grad)
```

```python
import math

import jax
import jax.numpy as jnp
from jax import lax
from jax.sharding import PartitionSpec as P

CHANNELS = 2
MARGIN = 16


highest = lax.Precision.HIGHEST
regular_gamma = 0.1
wave_ratio = 0.35


def padded(cells, sides, width):
    for axis, dim in sides:
        count = lax.axis_size(axis)
        ends = count - 1
        head = lax.slice_in_dim(cells, 0, width, axis=dim)
        tail = lax.slice_in_dim(cells, cells.shape[dim] - width, cells.shape[dim], axis=dim)
        cells = jnp.concatenate(
            [
                lax.ppermute(tail, axis, [(i, (i + 1) % count) for i in range(ends)]),
                cells,
                lax.ppermute(head, axis, [((i + 1) % count, i) for i in range(ends)]),
            ],
            axis=dim,
        )
    return cells


def product(form, left, right):
    return jnp.einsum(form, left, right, precision=highest)


def noll_order(noll_index):
    radial = 0
    remain = noll_index - 1
    while remain > radial:
        radial += 1
        remain -= radial
    azimuth = radial % 2 + 2 * ((remain + (radial + 1) % 2) // 2)
    if noll_index % 2 == 1:
        azimuth = -azimuth
    return (radial, azimuth)


def zernike_basis(mode_count, pupil_side):
    position = (
        jnp.arange(pupil_side, dtype=jnp.int32).astype(jnp.float32) - (pupil_side - 1) / 2.0
    ) / (pupil_side / 2.0)
    grid_y = position[:, None] + jnp.zeros((1, pupil_side), jnp.float32)
    grid_x = jnp.zeros((pupil_side, 1), jnp.float32) + position[None, :]
    radius = jnp.sqrt(grid_x * grid_x + grid_y * grid_y)
    angle_map = jnp.arctan2(grid_y, grid_x)
    collected = []
    for noll_index in range(2, mode_count + 2):
        radial, azimuth = noll_order(noll_index)
        order_abs = abs(azimuth)
        radial_sum = jnp.zeros_like(radius)
        for power_step in range((radial - order_abs) // 2 + 1):
            factor = math.factorial(radial - power_step) / (
                math.factorial(power_step)
                * math.factorial((radial + order_abs) // 2 - power_step)
                * math.factorial((radial - order_abs) // 2 - power_step)
            )
            if power_step % 2 == 1:
                factor = -factor
            radial_sum = radial_sum + factor * radius ** (radial - 2 * power_step)
        if azimuth == 0:
            shaped = radial_sum * math.sqrt(radial + 1.0)
        elif azimuth > 0:
            shaped = radial_sum * math.sqrt(2.0 * (radial + 1.0)) * jnp.cos(order_abs * angle_map)
        else:
            shaped = radial_sum * math.sqrt(2.0 * (radial + 1.0)) * jnp.sin(order_abs * angle_map)
        collected.append(shaped.reshape(-1))
    return jnp.stack(collected)


def dft_tables(length, width):
    frequency = jnp.arange(length, dtype=jnp.int32)[:, None]
    position = jnp.arange(width, dtype=jnp.int32)[None, :]
    turns = (frequency * position % length).astype(jnp.float32) * (2.0 * math.pi / length)
    return (jnp.cos(turns), -jnp.sin(turns))


def complex_tables(length, width):
    table_re, table_im = dft_tables(length, width)
    right_table = jnp.stack([jnp.stack([table_re, table_im]), jnp.stack([-table_im, table_re])])
    left_table = jnp.stack([jnp.stack([table_re, -table_im]), jnp.stack([table_im, table_re])])
    return (right_table, left_table)


def real_transform(image, length):
    right_table, left_table = complex_tables(length, length)
    inner = product("bxy,tvy->tbxv", image, right_table[0])
    return product("tsux,sbxv->tbuv", left_table, inner)


def build_otf(coeff_in, scale_in, shift_in, zernike, mask_flat, length):
    pupil_side = length // 2
    batch_size = coeff_in.shape[0]
    phase_map = jnp.dot(coeff_in, zernike, precision=highest) * scale_in[:, None]
    pupil = jnp.stack([mask_flat * jnp.cos(phase_map), mask_flat * jnp.sin(phase_map)]).reshape(
        2, batch_size, pupil_side, pupil_side
    )
    right_table, left_table = complex_tables(length, pupil_side)
    half = product("sbxy,stvy->tbxv", pupil, right_table)
    field = product("tsux,sbxv->tbuv", left_table, half)
    intensity = field[0] * field[0] + field[1] * field[1]
    point_spread = intensity / jnp.sum(intensity, axis=(1, 2), keepdims=True)
    otf = real_transform(point_spread, length)
    frequency = jnp.arange(length, dtype=jnp.int32).astype(jnp.float32)
    angle_y = 2.0 * math.pi / length * shift_in[:, 0:1] * frequency[None, :]
    angle_x = 2.0 * math.pi / length * shift_in[:, 1:2] * frequency[None, :]
    total_angle = angle_y[:, :, None] + angle_x[:, None, :]
    tilt_re = jnp.cos(total_angle)
    tilt_im = -jnp.sin(total_angle)
    return jnp.stack([otf[0] * tilt_re - otf[1] * tilt_im, otf[0] * tilt_im + otf[1] * tilt_re])


def data_spectrum(pixel_in, length, margin):
    position = jnp.arange(length, dtype=jnp.int32)
    distance = jnp.minimum(position, length - 1 - position).astype(jnp.float32)
    taper_row = jnp.where(
        distance < margin, 0.5 - 0.5 * jnp.cos(math.pi * (distance + 0.5) / margin), 1.0
    )
    image = pixel_in.astype(jnp.float32) * taper_row[:, None] * taper_row[None, :]
    return real_transform(image, length)


def wiener_terms(otf, spec, onehot, length):
    otf_re, otf_im = (otf[0], otf[1])
    spec_re, spec_im = (spec[0], spec[1])
    cross_re = otf_re * spec_re + otf_im * spec_im
    cross_im = otf_re * spec_im - otf_im * spec_re
    intensity = otf_re * otf_re + otf_im * otf_im
    num_re = product("kc,kbuv->cbuv", onehot, cross_re)
    num_im = product("kc,kbuv->cbuv", onehot, cross_im)
    denominator = product("kc,kbuv->cbuv", onehot, intensity) + regular_gamma
    obj_re = num_re / denominator
    obj_im = num_im / denominator
    per_re = product("kc,cbuv->kbuv", onehot, obj_re)
    per_im = product("kc,cbuv->kbuv", onehot, obj_im)
    res_re = spec_re - (per_re * otf_re - per_im * otf_im)
    res_im = spec_im - (per_re * otf_im + per_im * otf_re)
    loss_scale = 1.0 / float(length * length * length)
    grad_re = -2.0 * loss_scale * (res_re * per_re + res_im * per_im)
    grad_im = 2.0 * loss_scale * (res_re * per_im - res_im * per_re)
    return (obj_re, obj_im, jnp.stack([grad_re, grad_im]))


def object_image(obj_re, obj_im, length):
    full_re, full_im = dft_tables(length, length)
    back_re = product("ux,bxv->buv", full_re, obj_re) + product("ux,bxv->buv", full_im, obj_im)
    back_im = product("ux,bxv->buv", full_re, obj_im) - product("ux,bxv->buv", full_im, obj_re)
    return (product("bux,vx->buv", back_re, full_re) + product("bux,vx->buv", back_im, full_im)) / (
        length * length
    )


def window_weight(width_in, length):
    position = jnp.arange(length, dtype=jnp.int32)
    distance = (jnp.minimum(position, length - 1 - position) + 1).astype(jnp.float32)
    ramp_row = jnp.minimum(1.0, distance / (width_in.astype(jnp.float32) + 1.0))
    return ramp_row[:, None] * ramp_row[None, :]


def fold_margins(extended, axis_num, margin):
    span = extended.shape[axis_num] - 4 * margin
    upper_part = lax.slice_in_dim(extended, 0, margin, axis=axis_num)
    middle = lax.slice_in_dim(extended, 2 * margin, 2 * margin + span, axis=axis_num)
    lower_part = lax.slice_in_dim(extended, span + 3 * margin, span + 4 * margin, axis=axis_num)
    pad_upper = [(0, 0)] * extended.ndim
    pad_lower = [(0, 0)] * extended.ndim
    pad_upper[axis_num] = (0, span - margin)
    pad_lower[axis_num] = (span - margin, 0)
    return middle + jnp.pad(upper_part, pad_upper) + jnp.pad(lower_part, pad_lower)


def per_device(coeffs, shifts, pixels, pupil_mask, chan_map, intersection):
    mode_count = coeffs.shape[3]
    length = pixels.shape[3]
    margin = MARGIN
    channels = CHANNELS
    small = jnp.concatenate([coeffs, shifts.astype(jnp.float32)], axis=3)
    small = lax.all_to_all(small, "patch", split_axis=1, concat_axis=0, tiled=True)
    slots = small.shape[0]
    small = small.reshape(slots, mode_count + 2)
    coeff_all = small[:, :mode_count]
    shift_all = small[:, mode_count:]
    frames = lax.all_to_all(pixels, "patch", split_axis=1, concat_axis=0, tiled=True)
    frames = frames.reshape(slots, length, length)
    zernike = zernike_basis(mode_count, length // 2)
    mask_flat = pupil_mask.reshape(-1).astype(jnp.float32)
    scale_all = 1.0 / (1.0 + wave_ratio * chan_map.astype(jnp.float32))
    onehot = (chan_map[:, None] == jnp.arange(channels, dtype=jnp.int32)[None, :]).astype(
        jnp.float32
    )

    def forward(coeff_in):
        return build_otf(coeff_in, scale_all, shift_all, zernike, mask_flat, length)

    otf, pullback = jax.vjp(forward, coeff_all)
    spectra = data_spectrum(frames, length, margin)
    shape = (2, slots, 1, length, length)
    obj_re, obj_im, otf_grad = wiener_terms(otf.reshape(shape), spectra.reshape(shape), onehot, length)
    images = object_image(
        obj_re.reshape(-1, length, length), obj_im.reshape(-1, length, length), length
    )
    grad_all = pullback(otf_grad.reshape(2, slots, length, length))[0]
    coeff_grad = lax.all_to_all(
        grad_all.reshape(slots, 1, 1, mode_count), "patch", split_axis=0, concat_axis=1, tiled=True
    )
    weight = window_weight(intersection[0, 0], length)
    numerator = images * weight[None]
    canvas = jnp.concatenate([numerator, weight[None]], axis=0)
    extended = padded(canvas, (("frame", 2), ("patch", 1)), margin)
    folded = fold_margins(fold_margins(extended, 1, margin), 2, margin)
    blended = folded[:channels] / folded[channels][None]
    return (blended, coeff_grad)


def solution(mesh):
    in_specs = (
        P("patch", None, "frame", None),
        P("patch", None, "frame", None),
        P("patch", None, "frame", None, None),
        P(),
        P(),
        P("patch", "frame"),
    )
    out_specs = (P(None, "patch", "frame"), P("patch", None, "frame", None))
    return jax.shard_map(
        per_device, mesh=mesh, in_specs=in_specs, out_specs=out_specs, check_vma=False
    )
```

```python
import functools
import math

import jax
import jax.numpy as jnp
import ml_dtypes
import numpy as np
from jax import lax
from jax.experimental import pallas as pl
from jax.experimental.pallas import tpu as pltpu
from jax.sharding import PartitionSpec as P

N = 128
PUP = 64
ZERN = 36
SLOTS = 16
PAIRS = SLOTS // 2
CHANNELS = 2
PER = SLOTS // CHANNELS
MARGIN = 16
HALF = 72
TWO = 2 * HALF
DEG = 9
COEF = 40
regular_gamma = 0.1
wave_ratio = 0.35
f32 = jnp.float32
bf16 = jnp.bfloat16
VM = pl.BlockSpec(memory_space=pltpu.VMEM)
SM = pl.BlockSpec(memory_space=pltpu.SMEM)


def noll_order(noll_index):
    radial = 0
    remain = noll_index - 1
    while remain > radial:
        radial += 1
        remain -= radial
    azimuth = radial % 2 + 2 * ((remain + (radial + 1) % 2) // 2)
    if noll_index % 2 == 1:
        azimuth = -azimuth
    return (radial, azimuth)


def zernike_modes():
    position = (np.arange(PUP) - (PUP - 1) / 2.0) / (PUP / 2.0)
    grid_y, grid_x = np.meshgrid(position, position, indexing="ij")
    radius = np.sqrt(grid_x * grid_x + grid_y * grid_y)
    theta = np.arctan2(grid_y, grid_x)
    modes = []
    for noll_index in range(2, ZERN + 2):
        radial, azimuth = noll_order(noll_index)
        order = abs(azimuth)
        total = np.zeros_like(radius)
        for step in range((radial - order) // 2 + 1):
            factor = math.factorial(radial - step) / (
                math.factorial(step)
                * math.factorial((radial + order) // 2 - step)
                * math.factorial((radial - order) // 2 - step)
            )
            total = total + (-1) ** step * factor * radius ** (radial - 2 * step)
        if azimuth == 0:
            modes.append(total * math.sqrt(radial + 1.0))
        elif azimuth > 0:
            modes.append(total * math.sqrt(2.0 * (radial + 1.0)) * np.cos(order * theta))
        else:
            modes.append(total * math.sqrt(2.0 * (radial + 1.0)) * np.sin(order * theta))
    return position, np.stack(modes)


def halves(table):
    high = table.astype(ml_dtypes.bfloat16)
    low = (table - high.astype(np.float64)).astype(ml_dtypes.bfloat16)
    return high, low


def pair_table(table):
    return np.stack(halves(table))


@functools.cache
def tables():
    index = np.arange(N)
    turns = 2.0 * np.pi / N * (np.outer(index, index) % N)
    c, s = np.cos(turns), np.sin(turns)
    cp, sp = c[:, :PUP], s[:, :PUP]
    ch, sh = c[:HALF], s[:HALF]
    distance = np.minimum(index, N - 1 - index)
    taper = np.where(distance < MARGIN, 0.5 - 0.5 * np.cos(np.pi * (distance + 0.5) / MARGIN), 1.0)
    weight = np.where(np.arange(HALF) < 1, 1.0, 2.0)
    weight[N // 2] = 1.0
    weight[N // 2 + 1 :] = 0.0
    out = {}
    out["right_pupil"] = pair_table(np.block([[cp.T, -sp.T], [sp.T, cp.T]]))
    out["left_pupil"] = pair_table(np.block([[cp, sp], [-sp, cp]]))
    out["left_half"] = pair_table(np.block([[ch], [-sh]]))
    out["right_full"] = pair_table(np.block([[c, -s], [s, c]]))
    out["right_back"] = pair_table(np.block([[c, s], [-s, c]]))
    high, low = halves(np.block([[ch], [-sh]]) * taper[None, :])
    out["left_taper"] = np.concatenate([high, low], axis=1)
    high, low = halves(np.concatenate([weight[None] * ch.T, -weight[None] * sh.T], axis=1))
    out["left_back"] = np.concatenate([high, high, low], axis=1)
    out["taper"] = np.tile(taper, 2)[None].astype(np.float32)
    out["weight"] = np.broadcast_to(weight[:, None], (HALF, N)).astype(np.float32)
    position, modes = zernike_modes()
    cheb = np.polynomial.chebyshev.chebvander(position, DEG - 1)
    fit = np.linalg.lstsq(cheb, modes.transpose(1, 0, 2).reshape(PUP, -1), rcond=None)[0]
    fit = fit.reshape(DEG, ZERN, PUP).transpose(1, 0, 2)
    phase = np.zeros((COEF, DEG, PUP))
    phase[:ZERN] = fit
    step = 2.0 * np.pi / N * (PUP / 2.0)
    phase[ZERN, 1] = step
    phase[ZERN + 1, 0] = step * position
    phase = np.concatenate([phase, phase], axis=2)
    out["phase"] = phase.reshape(COEF, DEG * N).astype(np.float32)
    return out, cheb


def split(x):
    high = x.astype(bf16)
    return high, (x - high.astype(f32)).astype(bf16)


def dot(left, right):
    return lax.dot_general(left, right, (((1,), (0,)), ((), ())), preferred_element_type=f32)


def rows3(x):
    high, low = split(x)
    return jnp.concatenate([high, low, high], axis=0)


def table_rows(ref):
    return jnp.concatenate([ref[0], ref[0], ref[1]], axis=0)


def table_lanes(ref):
    return jnp.concatenate([ref[0], ref[0], ref[1]], axis=1)


def swap_halves(y, count):
    top = jnp.concatenate([y[:count, :N], y[count:, :N]], axis=1)
    low = jnp.concatenate([y[:count, N:], y[count:, N:]], axis=1)
    return jnp.concatenate([top, low], axis=0)


def chebyshev_sums(parts, cheb, row):
    even = parts[0]
    for i in range(2, DEG, 2):
        even = even + float(cheb[row, i]) * parts[i]
    odd = float(cheb[row, 1]) * parts[1]
    for i in range(3, DEG, 2):
        odd = odd + float(cheb[row, i]) * parts[i]
    return even, odd


def turn(phase, lane_turns):
    count = jnp.floor(phase * (2.0 / math.pi) + 0.5)
    rest = phase - count * 1.5703125
    rest = rest - count * 4.837512969970703125e-4
    rest = rest - count * 7.549789954891882e-8
    quarter = count.astype(jnp.int32) + lane_turns
    sq = rest * rest
    sine = rest + rest * sq * (
        -1.6666654611e-1 + sq * (8.3321608736e-3 + sq * -1.9515295891e-4)
    )
    cosine = (1.0 - 0.5 * sq) + sq * sq * (
        4.166664568298827e-2 + sq * (-1.388731625493765e-3 + sq * 2.443315711809948e-5)
    )
    odd = (quarter & 1) == 1
    value = jnp.where(odd, sine, cosine)
    value = jnp.where(((quarter + 1) & 2) == 2, -value, value)
    slope = jnp.where(odd, cosine, sine)
    slope = jnp.where((quarter & 2) == 2, slope, -slope)
    return value, slope


def slot_scales(chan_ref, width):
    row = lax.broadcasted_iota(jnp.int32, (SLOTS, width), 0)
    channel = jnp.zeros((SLOTS, width), jnp.int32)
    for slot in range(SLOTS):
        channel = jnp.where(row == slot, chan_ref[slot], channel)
    return 1.0 / (1.0 + wave_ratio * channel.astype(f32))


def transfer_kernel(
    coef_ref, chan_ref, mask_ref, phase_ref, rp_ref, lp_ref, lh_ref, rf_ref,
    otf_ref, field_ref, slope_ref, inv_ref,
    wide_ref, ph_ref, pl_ref, half_re_ref, half_im_ref, yh_ref, yl_ref,
):
    cheb = tables()[1]
    lane = lax.broadcasted_iota(jnp.int32, (SLOTS, COEF), 1)
    coef = coef_ref[...] * jnp.where(lane < ZERN, slot_scales(chan_ref, COEF), 1.0)
    mask = mask_ref[...].astype(f32)
    wide_ref[...] = jnp.concatenate([mask, mask], axis=1)
    parts_all = lax.dot_general(
        coef, phase_ref[...], (((1,), (0,)), ((), ())),
        precision=lax.Precision.HIGHEST, preferred_element_type=f32,
    )
    parts = [parts_all[:, i * N : (i + 1) * N] for i in range(DEG)]
    lane_turns = jnp.where(lax.broadcasted_iota(jnp.int32, (SLOTS, N), 1) < PUP, 0, 3)
    for row in range(PUP // 2):
        even, odd = chebyshev_sums(parts, cheb, row)
        for at, phase in ((row, even + odd), (PUP - 1 - row, even - odd)):
            value, slope = turn(phase, lane_turns)
            mask = wide_ref[at : at + 1, :]
            value = value * mask
            here = slice(at * SLOTS, (at + 1) * SLOTS)
            slope_ref[here, :] = slope * mask
            high, low = split(value)
            ph_ref[here, :] = high
            pl_ref[here, :] = low
    right = table_rows(rp_ref)
    for chunk in range(4):
        here = slice(chunk * 256, (chunk + 1) * 256)
        high = ph_ref[here, :]
        half = dot(jnp.concatenate([high, pl_ref[here, :], high], axis=1), right)
        half_re_ref[here, :] = half[:, :N]
        half_im_ref[here, :] = half[:, N:]
    left = table_lanes(lp_ref)
    left_h = table_lanes(lh_ref)
    for pair in range(PAIRS):
        columns = []
        for part_ref in (half_re_ref, half_im_ref):
            columns.append(
                jnp.concatenate(
                    [
                        part_ref[pl.ds(2 * pair + which, PUP, stride=SLOTS), :]
                        for which in range(2)
                    ],
                    axis=1,
                )
            )
        field = dot(left, rows3(jnp.concatenate(columns, axis=0)))
        field_ref[pair] = field
        power = field[:N] * field[:N] + field[N:] * field[N:]
        y = dot(left_h, rows3(power))
        high, low = split(swap_halves(y, HALF))
        here = slice(pair * TWO, (pair + 1) * TWO)
        yh_ref[here, :] = high
        yl_ref[here, :] = low
    right = table_rows(rf_ref)
    for pair in range(PAIRS):
        here = slice(pair * TWO, (pair + 1) * TWO)
        high = yh_ref[here, :]
        out = dot(jnp.concatenate([high, yl_ref[here, :], high], axis=1), right)
        for which in range(2):
            slot = 2 * pair + which
            block = out[which * HALF : (which + 1) * HALF]
            inverse = 1.0 / block[0:1, 0:1]
            otf_ref[slot * HALF : (slot + 1) * HALF, :] = block * inverse
            inv_ref[slot : slot + 1, :] = jnp.broadcast_to(inverse, (1, N))


def object_kernel(
    width_ref, chan_ref, pix_ref, otf_ref, lt_ref, taper_ref, weight_ref, rf_ref, rb_ref, lb_ref,
    grad_ref, canvas_ref,
    order_ref, yh_ref, yl_ref, spec_ref, object_ref,
):
    at = [jnp.int32(0), jnp.int32(PER)]
    for slot in range(SLOTS):
        first = chan_ref[slot] == 0
        order_ref[jnp.where(first, at[0], at[1])] = slot
        at = [jnp.where(first, at[0] + 1, at[0]), jnp.where(first, at[1], at[1] + 1)]
    left = lt_ref[...]
    taper = taper_ref[...]
    for pair in range(PAIRS):
        image = jnp.concatenate([pix_ref[2 * pair], pix_ref[2 * pair + 1]], axis=1)
        y = dot(left, jnp.concatenate([image, image], axis=0)) * taper
        high, low = split(swap_halves(y, HALF))
        here = slice(pair * TWO, (pair + 1) * TWO)
        yh_ref[here, :] = high
        yl_ref[here, :] = low
    right = table_rows(rf_ref)
    for pair in range(PAIRS):
        here = slice(pair * TWO, (pair + 1) * TWO)
        high = yh_ref[here, :]
        spec_ref[here, :] = dot(jnp.concatenate([high, yl_ref[here, :], high], axis=1), right)
    for channel in range(CHANNELS):
        slots = [order_ref[channel * PER + i] for i in range(PER)]
        inner = [jnp.zeros((8, N), f32) for _ in range(PER)]
        for block in range(HALF // 8):
            where = [pl.ds(pl.multiple_of(slot * HALF + block * 8, 8), 8) for slot in slots]
            h_re = [otf_ref[w, :N] for w in where]
            h_im = [otf_ref[w, N:] for w in where]
            s_re = [spec_ref[w, :N] for w in where]
            s_im = [spec_ref[w, N:] for w in where]
            num_re = num_im = 0.0
            den = regular_gamma
            for i in range(PER):
                num_re = num_re + (h_re[i] * s_re[i] + h_im[i] * s_im[i])
                num_im = num_im + (h_re[i] * s_im[i] - h_im[i] * s_re[i])
                den = den + (h_re[i] * h_re[i] + h_im[i] * h_im[i])
            inverse = 1.0 / den
            o_re = num_re * inverse
            o_im = num_im * inverse
            rows = slice(channel * HALF + block * 8, channel * HALF + block * 8 + 8)
            object_ref[rows, :N] = o_re
            object_ref[rows, N:] = o_im
            weight = weight_ref[block * 8 : block * 8 + 8, :]
            for i in range(PER):
                r_re = s_re[i] - (o_re * h_re[i] - o_im * h_im[i])
                r_im = s_im[i] - (o_re * h_im[i] + o_im * h_re[i])
                g_re = -(r_re * o_re + r_im * o_im)
                g_im = r_re * o_im - r_im * o_re
                inner[i] = inner[i] + weight * (g_re * h_re[i] + g_im * h_im[i])
                grad_ref[where[i], :N] = g_re
                grad_ref[where[i], N:] = g_im
        origin = (lax.broadcasted_iota(jnp.int32, (8, N), 0) == 0) & (
            lax.broadcasted_iota(jnp.int32, (8, N), 1) == 0
        )
        for i in range(PER):
            total = jnp.sum(jnp.sum(inner[i], axis=0, keepdims=True), axis=1, keepdims=True)
            w = pl.ds(pl.multiple_of(slots[i] * HALF, 8), 8)
            grad_ref[w, :N] = grad_ref[w, :N] - jnp.where(origin, total, 0.0)
    high, low = split(object_ref[...] * (1.0 / (N * N)))
    z = dot(jnp.concatenate([high, low, high], axis=1), table_rows(rb_ref))
    image = dot(lb_ref[...], rows3(swap_halves(z, HALF)))
    width = width_ref[0].astype(f32) + 1.0
    row = lax.broadcasted_iota(jnp.int32, (N, N), 0)
    col = lax.broadcasted_iota(jnp.int32, (N, N), 1)

    def ramp(index):
        distance = (jnp.minimum(index, N - 1 - index) + 1).astype(f32)
        return jnp.minimum(1.0, distance / width)

    weight = ramp(row) * ramp(col)
    canvas_ref[0] = image[:, :N] * weight
    canvas_ref[1] = image[:, N:] * weight
    canvas_ref[2] = weight


def gradient_kernel(
    chan_ref, grad_ref, field_ref, slope_ref, inv_ref, phase_ref, rb_ref, lb_ref, rp_ref, lp_ref,
    out_ref,
    z_ref, qh_ref, ql_ref, pupil_ref,
):
    cheb = tables()[1]
    right = table_rows(rb_ref)
    for pair in range(PAIRS):
        here = slice(pair * TWO, (pair + 1) * TWO)
        high, low = split(grad_ref[here, :])
        z_ref[here, :] = dot(jnp.concatenate([high, low, high], axis=1), right)
    left_b = lb_ref[...]
    left = table_lanes(rp_ref)
    for pair in range(PAIRS):
        here = slice(pair * TWO, (pair + 1) * TWO)
        power = dot(left_b, rows3(swap_halves(z_ref[here, :], HALF)))
        field = field_ref[pair]
        back = jnp.concatenate([field[:N] * power, field[N:] * power], axis=0)
        half = dot(left, rows3(back))
        high, low = split(swap_halves(half, PUP))
        here = slice(pair * N, (pair + 1) * N)
        qh_ref[here, :] = high
        ql_ref[here, :] = low
    right = table_rows(lp_ref)
    for pair in range(PAIRS):
        here = slice(pair * N, (pair + 1) * N)
        high = qh_ref[here, :]
        pupil_ref[here, :] = dot(jnp.concatenate([high, ql_ref[here, :], high], axis=1), right)
    sums = [None] * DEG
    for row in range(PUP // 2):
        both = []
        for at in (row, PUP - 1 - row):
            q = pupil_ref[pl.ds(at, SLOTS, stride=PUP), :]
            both.append(q * slope_ref[at * SLOTS : (at + 1) * SLOTS, :])
        parity = (both[0] + both[1], both[0] - both[1])
        for i in range(DEG):
            term = parity[i % 2] * float(cheb[row, i]) if i else parity[0]
            sums[i] = term if sums[i] is None else sums[i] + term
    total = lax.dot_general(
        jnp.concatenate(sums, axis=1), phase_ref[...], (((1,), (1,)), ((), ())),
        precision=lax.Precision.HIGHEST, preferred_element_type=f32,
    )
    factor = 4.0 / float(N * N * N)
    out_ref[...] = total * (slot_scales(chan_ref, COEF) * factor * inv_ref[:, :COEF])


def transfer(coef, chan, mask, tabs, interpret=False):
    rows = SLOTS * HALF
    return pl.pallas_call(
        transfer_kernel,
        out_shape=(
            jax.ShapeDtypeStruct((rows, 2 * N), f32),
            jax.ShapeDtypeStruct((PAIRS, 2 * N, 2 * N), f32),
            jax.ShapeDtypeStruct((PUP * SLOTS, N), f32),
            jax.ShapeDtypeStruct((SLOTS, N), f32),
        ),
        in_specs=[VM, SM] + [VM] * 6,
        out_specs=(VM,) * 4,
        scratch_shapes=[
            pltpu.VMEM((PUP, N), f32),
            pltpu.VMEM((PUP * SLOTS, N), bf16),
            pltpu.VMEM((PUP * SLOTS, N), bf16),
            pltpu.VMEM((PUP * SLOTS, N), f32),
            pltpu.VMEM((PUP * SLOTS, N), f32),
            pltpu.VMEM((rows, 2 * N), bf16),
            pltpu.VMEM((rows, 2 * N), bf16),
        ],
        interpret=interpret,
        name="transfer",
    )(
        coef, chan, mask, tabs["phase"], tabs["right_pupil"], tabs["left_pupil"],
        tabs["left_half"], tabs["right_full"],
    )


def objects(width, chan, pixels, otf, tabs, interpret=False):
    rows = SLOTS * HALF
    return pl.pallas_call(
        object_kernel,
        out_shape=(
            jax.ShapeDtypeStruct((rows, 2 * N), f32),
            jax.ShapeDtypeStruct((CHANNELS + 1, N, N), f32),
        ),
        in_specs=[SM, SM] + [VM] * 8,
        out_specs=(VM,) * 2,
        scratch_shapes=[
            pltpu.SMEM((SLOTS,), jnp.int32),
            pltpu.VMEM((rows, 2 * N), bf16),
            pltpu.VMEM((rows, 2 * N), bf16),
            pltpu.VMEM((rows, 2 * N), f32),
            pltpu.VMEM((TWO, 2 * N), f32),
        ],
        interpret=interpret,
        name="objects",
    )(
        width, chan, pixels, otf, tabs["left_taper"], tabs["taper"], tabs["weight"],
        tabs["right_full"], tabs["right_back"], tabs["left_back"],
    )


def gradient(chan, grad, field, slope, inverse, tabs, interpret=False):
    rows = SLOTS * HALF
    return pl.pallas_call(
        gradient_kernel,
        out_shape=jax.ShapeDtypeStruct((SLOTS, COEF), f32),
        in_specs=[SM] + [VM] * 9,
        out_specs=VM,
        scratch_shapes=[
            pltpu.VMEM((rows, 2 * N), f32),
            pltpu.VMEM((SLOTS * PUP, 2 * N), bf16),
            pltpu.VMEM((SLOTS * PUP, 2 * N), bf16),
            pltpu.VMEM((SLOTS * PUP, N), f32),
        ],
        interpret=interpret,
        name="gradient",
    )(
        chan, grad, field, slope, inverse, tabs["phase"], tabs["right_back"], tabs["left_back"],
        tabs["right_pupil"], tabs["left_pupil"],
    )


def padded(cells, sides, width):
    for axis, dim in sides:
        count = lax.axis_size(axis)
        ends = count - 1
        head = lax.slice_in_dim(cells, 0, width, axis=dim)
        tail = lax.slice_in_dim(cells, cells.shape[dim] - width, cells.shape[dim], axis=dim)
        cells = jnp.concatenate(
            [
                lax.ppermute(tail, axis, [(i, (i + 1) % count) for i in range(ends)]),
                cells,
                lax.ppermute(head, axis, [((i + 1) % count, i) for i in range(ends)]),
            ],
            axis=dim,
        )
    return cells


def fold_margins(extended, axis_num, margin):
    span = extended.shape[axis_num] - 4 * margin
    upper_part = lax.slice_in_dim(extended, 0, margin, axis=axis_num)
    middle = lax.slice_in_dim(extended, 2 * margin, 2 * margin + span, axis=axis_num)
    lower_part = lax.slice_in_dim(extended, span + 3 * margin, span + 4 * margin, axis=axis_num)
    pad_upper = [(0, 0)] * extended.ndim
    pad_lower = [(0, 0)] * extended.ndim
    pad_upper[axis_num] = (0, span - margin)
    pad_lower[axis_num] = (span - margin, 0)
    return middle + jnp.pad(upper_part, pad_upper) + jnp.pad(lower_part, pad_lower)


def per_device(coeffs, shifts, pixels, pupil_mask, chan_map, intersection):
    tabs = {name: jnp.asarray(table) for name, table in tables()[0].items()}
    spare = jnp.zeros(coeffs.shape[:3] + (COEF - ZERN - 2,), f32)
    small = jnp.concatenate([coeffs, shifts.astype(f32), spare], axis=3)
    small = lax.all_to_all(small, "patch", split_axis=1, concat_axis=0, tiled=True)
    frames = lax.all_to_all(pixels, "patch", split_axis=1, concat_axis=0, tiled=True)
    otf, field, slope, inverse = transfer(small.reshape(SLOTS, COEF), chan_map, pupil_mask, tabs)
    grad, canvas = objects(
        intersection.reshape(1), chan_map, frames.reshape(SLOTS, N, N), otf, tabs
    )
    grad = gradient(chan_map, grad, field, slope, inverse, tabs)
    grad = lax.all_to_all(
        grad.reshape(SLOTS, 1, 1, COEF), "patch", split_axis=0, concat_axis=1, tiled=True
    )
    extended = padded(canvas, (("frame", 2), ("patch", 1)), MARGIN)
    folded = fold_margins(fold_margins(extended, 1, MARGIN), 2, MARGIN)
    blended = folded[:CHANNELS] / folded[CHANNELS][None]
    return (blended, grad[..., :ZERN])


def solution(mesh):
    in_specs = (
        P("patch", None, "frame", None),
        P("patch", None, "frame", None),
        P("patch", None, "frame", None, None),
        P(),
        P(),
        P("patch", "frame"),
    )
    out_specs = (P(None, "patch", "frame"), P("patch", None, "frame", None))
    return jax.shard_map(
        per_device, mesh=mesh, in_specs=in_specs, out_specs=out_specs, check_vma=False
    )
```

```python
import functools
import math

import jax
import jax.numpy as jnp
import ml_dtypes
import numpy as np
from jax import lax
from jax.experimental import pallas as pl
from jax.experimental.pallas import tpu as pltpu
from jax.sharding import PartitionSpec as P


N = 128
PUP = 64
ZERN = 36
SLOTS = 16
PAIRS = SLOTS // 2
CHANNELS = 2
PER = SLOTS // CHANNELS
MARGIN = 16
TILE = N - 2 * MARGIN
HALF = 72
TWO = 2 * HALF
DEG = 9
COEF = 40
ROWS = N + 8
regular_gamma = 0.1
wave_ratio = 0.35
f32 = jnp.float32
bf16 = jnp.bfloat16
VM = pl.BlockSpec(memory_space=pltpu.VMEM)
SM = pl.BlockSpec(memory_space=pltpu.SMEM)


def noll_order(noll_index):
    radial = 0
    remain = noll_index - 1
    while remain > radial:
        radial += 1
        remain -= radial
    azimuth = radial % 2 + 2 * ((remain + (radial + 1) % 2) // 2)
    if noll_index % 2 == 1:
        azimuth = -azimuth
    return (radial, azimuth)


def zernike_modes():
    position = (np.arange(PUP) - (PUP - 1) / 2.0) / (PUP / 2.0)
    grid_y, grid_x = np.meshgrid(position, position, indexing="ij")
    radius = np.sqrt(grid_x * grid_x + grid_y * grid_y)
    theta = np.arctan2(grid_y, grid_x)
    modes = []
    for noll_index in range(2, ZERN + 2):
        radial, azimuth = noll_order(noll_index)
        order = abs(azimuth)
        total = np.zeros_like(radius)
        for step in range((radial - order) // 2 + 1):
            factor = math.factorial(radial - step) / (
                math.factorial(step)
                * math.factorial((radial + order) // 2 - step)
                * math.factorial((radial - order) // 2 - step)
            )
            total = total + (-1) ** step * factor * radius ** (radial - 2 * step)
        if azimuth == 0:
            modes.append(total * math.sqrt(radial + 1.0))
        elif azimuth > 0:
            modes.append(total * math.sqrt(2.0 * (radial + 1.0)) * np.cos(order * theta))
        else:
            modes.append(total * math.sqrt(2.0 * (radial + 1.0)) * np.sin(order * theta))
    return position, np.stack(modes)


def halves(table):
    high = table.astype(ml_dtypes.bfloat16)
    low = (table - high.astype(np.float64)).astype(ml_dtypes.bfloat16)
    return high, low


def pair_table(table):
    return np.stack(halves(table))


@functools.cache
def tables():
    index = np.arange(N)
    turns = 2.0 * np.pi / N * (np.outer(index, index) % N)
    c, s = np.cos(turns), np.sin(turns)
    cp, sp = c[:, :PUP], s[:, :PUP]
    ch, sh = c[:HALF], s[:HALF]
    distance = np.minimum(index, N - 1 - index)
    taper = np.where(distance < MARGIN, 0.5 - 0.5 * np.cos(np.pi * (distance + 0.5) / MARGIN), 1.0)
    weight = np.where(np.arange(HALF) < 1, 1.0, 2.0)
    weight[N // 2] = 1.0
    weight[N // 2 + 1 :] = 0.0
    out = {}
    out["right_pupil"] = pair_table(np.block([[cp.T, -sp.T], [sp.T, cp.T]]))
    out["left_pupil"] = pair_table(np.block([[cp, sp], [-sp, cp]]))
    out["left_half"] = pair_table(np.block([[ch], [-sh]]))
    out["right_full"] = pair_table(np.block([[c, -s], [s, c]]))
    out["right_back"] = pair_table(np.block([[c, s], [-s, c]]))
    high, low = halves(np.block([[ch], [-sh]]) * taper[None, :])
    out["left_taper"] = np.concatenate([high, low], axis=1)
    high, low = halves(np.concatenate([weight[None] * ch.T, -weight[None] * sh.T], axis=1))
    out["left_back"] = np.concatenate([high, high, low], axis=1)
    out["taper"] = np.tile(taper, 2)[None].astype(np.float32)
    out["weight"] = np.broadcast_to(weight[:, None], (HALF, N)).astype(np.float32)
    position, modes = zernike_modes()
    cheb = np.polynomial.chebyshev.chebvander(position, DEG - 1)
    fit = np.linalg.lstsq(cheb, modes.transpose(1, 0, 2).reshape(PUP, -1), rcond=None)[0]
    fit = fit.reshape(DEG, ZERN, PUP).transpose(1, 0, 2)
    phase = np.zeros((COEF, DEG, PUP))
    phase[:ZERN] = fit
    step = 2.0 * np.pi / N * (PUP / 2.0)
    phase[ZERN, 1] = step
    phase[ZERN + 1, 0] = step * position
    phase = np.concatenate([phase, phase], axis=2)
    out["phase"] = phase.reshape(COEF, DEG * N).astype(np.float32)
    return out, cheb


def split(x):
    high = x.astype(bf16)
    return high, (x - high.astype(f32)).astype(bf16)


def dot(left, right):
    return lax.dot_general(left, right, (((1,), (0,)), ((), ())), preferred_element_type=f32)


def rows3(x):
    high, low = split(x)
    return jnp.concatenate([high, low, high], axis=0)


def table_rows(ref):
    return jnp.concatenate([ref[0], ref[0], ref[1]], axis=0)


def table_lanes(ref):
    return jnp.concatenate([ref[0], ref[0], ref[1]], axis=1)


def swap_halves(y, count):
    top = jnp.concatenate([y[:count, :N], y[count:, :N]], axis=1)
    low = jnp.concatenate([y[:count, N:], y[count:, N:]], axis=1)
    return jnp.concatenate([top, low], axis=0)


def chebyshev_sums(parts, cheb, row):
    even = parts[0]
    for i in range(2, DEG, 2):
        even = even + float(cheb[row, i]) * parts[i]
    odd = float(cheb[row, 1]) * parts[1]
    for i in range(3, DEG, 2):
        odd = odd + float(cheb[row, i]) * parts[i]
    return even, odd


def turn(phase, lane_turns):
    count = jnp.floor(phase * (2.0 / math.pi) + 0.5)
    rest = phase - count * 1.5703125
    rest = rest - count * 4.837512969970703125e-4
    rest = rest - count * 7.549789954891882e-8
    quarter = count.astype(jnp.int32) + lane_turns
    sq = rest * rest
    sine = rest + rest * sq * (
        -1.6666654611e-1 + sq * (8.3321608736e-3 + sq * -1.9515295891e-4)
    )
    cosine = (1.0 - 0.5 * sq) + sq * sq * (
        4.166664568298827e-2 + sq * (-1.388731625493765e-3 + sq * 2.443315711809948e-5)
    )
    odd = (quarter & 1) == 1
    value = jnp.where(odd, sine, cosine)
    value = jnp.where(((quarter + 1) & 2) == 2, -value, value)
    slope = jnp.where(odd, cosine, sine)
    slope = jnp.where((quarter & 2) == 2, slope, -slope)
    return value, slope


def slot_scales(chan_ref, width):
    row = lax.broadcasted_iota(jnp.int32, (SLOTS, width), 0)
    channel = jnp.zeros((SLOTS, width), jnp.int32)
    for slot in range(SLOTS):
        channel = jnp.where(row == slot, chan_ref[slot], channel)
    return 1.0 / (1.0 + wave_ratio * channel.astype(f32))


def transfer_part(
    data_ref, chan_ref, mask_ref, phase_ref, rp_ref, lp_ref, lh_ref, rf_ref, ready,
    otf_ref, field_ref, slope_ref, inv_ref,
    line_ref, wide_ref, ph_ref, pl_ref, half_re_ref, half_im_ref, yh_ref, yl_ref,
):
    cheb = tables()[1]
    for slot in range(SLOTS):
        line_ref[slot * 8 : slot * 8 + 8, :] = data_ref[slot, N:, :].astype(f32)
    line = line_ref[pl.ds(0, SLOTS, stride=8), :]
    coef = line + (pltpu.roll(line, N - ZERN, 1) + pltpu.roll(line, N - 2 * ZERN, 1))
    lane = lax.broadcasted_iota(jnp.int32, (SLOTS, N), 1)
    shift = pltpu.roll(line, N - 2 * ZERN, 1)
    coef = jnp.where(lane < ZERN, coef * slot_scales(chan_ref, N), shift)[:, :COEF]
    mask = mask_ref[...].astype(f32)
    wide_ref[...] = jnp.concatenate([mask, mask], axis=1)
    parts_all = lax.dot_general(
        coef, phase_ref[...], (((1,), (0,)), ((), ())),
        precision=lax.Precision.HIGHEST, preferred_element_type=f32,
    )
    parts = [parts_all[:, i * N : (i + 1) * N] for i in range(DEG)]
    lane_turns = jnp.where(lax.broadcasted_iota(jnp.int32, (SLOTS, N), 1) < PUP, 0, 3)
    for row in range(PUP // 2):
        even, odd = chebyshev_sums(parts, cheb, row)
        for at, phase in ((row, even + odd), (PUP - 1 - row, even - odd)):
            value, slope = turn(phase, lane_turns)
            mask = wide_ref[at : at + 1, :]
            value = value * mask
            here = slice(at * SLOTS, (at + 1) * SLOTS)
            slope_ref[here, :] = slope * mask
            high, low = split(value)
            ph_ref[here, :] = high
            pl_ref[here, :] = low
    ready()
    right = table_rows(rp_ref)
    for chunk in range(4):
        here = slice(chunk * 256, (chunk + 1) * 256)
        high = ph_ref[here, :]
        half = dot(jnp.concatenate([high, pl_ref[here, :], high], axis=1), right)
        half_re_ref[here, :] = half[:, :N]
        half_im_ref[here, :] = half[:, N:]
    left = table_lanes(lp_ref)
    left_h = table_lanes(lh_ref)
    for pair in range(PAIRS):
        columns = []
        for part_ref in (half_re_ref, half_im_ref):
            columns.append(
                jnp.concatenate(
                    [
                        part_ref[pl.ds(2 * pair + which, PUP, stride=SLOTS), :]
                        for which in range(2)
                    ],
                    axis=1,
                )
            )
        field = dot(left, rows3(jnp.concatenate(columns, axis=0)))
        field_ref[pair] = field
        power = field[:N] * field[:N] + field[N:] * field[N:]
        y = dot(left_h, rows3(power))
        high, low = split(swap_halves(y, HALF))
        here = slice(pair * TWO, (pair + 1) * TWO)
        yh_ref[here, :] = high
        yl_ref[here, :] = low
    right = table_rows(rf_ref)
    for pair in range(PAIRS):
        here = slice(pair * TWO, (pair + 1) * TWO)
        high = yh_ref[here, :]
        out = dot(jnp.concatenate([high, yl_ref[here, :], high], axis=1), right)
        for which in range(2):
            slot = 2 * pair + which
            block = out[which * HALF : (which + 1) * HALF]
            inverse = 1.0 / block[0:1, 0:1]
            otf_ref[slot * HALF : (slot + 1) * HALF, :] = block * inverse
            inv_ref[slot : slot + 1, :] = jnp.broadcast_to(inverse, (1, N))


def object_part(
    width_ref, chan_ref, pix_ref, otf_ref, lt_ref, taper_ref, weight_ref, rf_ref, rb_ref, lb_ref,
    grad_ref, canvas_ref, head_ref, tail_ref,
    order_ref, yh_ref, yl_ref, spec_ref, object_ref,
):
    at = [jnp.int32(0), jnp.int32(PER)]
    for slot in range(SLOTS):
        first = chan_ref[slot] == 0
        order_ref[jnp.where(first, at[0], at[1])] = slot
        at = [jnp.where(first, at[0] + 1, at[0]), jnp.where(first, at[1], at[1] + 1)]
    left = lt_ref[...]
    taper = taper_ref[...]
    for pair in range(PAIRS):
        image = jnp.concatenate([pix_ref[2 * pair, :N, :], pix_ref[2 * pair + 1, :N, :]], axis=1)
        y = dot(left, jnp.concatenate([image, image], axis=0)) * taper
        high, low = split(swap_halves(y, HALF))
        here = slice(pair * TWO, (pair + 1) * TWO)
        yh_ref[here, :] = high
        yl_ref[here, :] = low
    right = table_rows(rf_ref)
    for pair in range(PAIRS):
        here = slice(pair * TWO, (pair + 1) * TWO)
        high = yh_ref[here, :]
        spec_ref[here, :] = dot(jnp.concatenate([high, yl_ref[here, :], high], axis=1), right)
    for channel in range(CHANNELS):
        slots = [order_ref[channel * PER + i] for i in range(PER)]
        inner = [jnp.zeros((8, N), f32) for _ in range(PER)]
        for block in range(HALF // 8):
            where = [pl.ds(pl.multiple_of(slot * HALF + block * 8, 8), 8) for slot in slots]
            h_re = [otf_ref[w, :N] for w in where]
            h_im = [otf_ref[w, N:] for w in where]
            s_re = [spec_ref[w, :N] for w in where]
            s_im = [spec_ref[w, N:] for w in where]
            num_re = num_im = 0.0
            den = regular_gamma
            for i in range(PER):
                num_re = num_re + (h_re[i] * s_re[i] + h_im[i] * s_im[i])
                num_im = num_im + (h_re[i] * s_im[i] - h_im[i] * s_re[i])
                den = den + (h_re[i] * h_re[i] + h_im[i] * h_im[i])
            inverse = 1.0 / den
            o_re = num_re * inverse
            o_im = num_im * inverse
            rows = slice(channel * HALF + block * 8, channel * HALF + block * 8 + 8)
            object_ref[rows, :N] = o_re
            object_ref[rows, N:] = o_im
            weight = weight_ref[block * 8 : block * 8 + 8, :]
            for i in range(PER):
                r_re = s_re[i] - (o_re * h_re[i] - o_im * h_im[i])
                r_im = s_im[i] - (o_re * h_im[i] + o_im * h_re[i])
                g_re = -(r_re * o_re + r_im * o_im)
                g_im = r_re * o_im - r_im * o_re
                inner[i] = inner[i] + weight * (g_re * h_re[i] + g_im * h_im[i])
                grad_ref[where[i], :N] = g_re
                grad_ref[where[i], N:] = g_im
        origin = (lax.broadcasted_iota(jnp.int32, (8, N), 0) == 0) & (
            lax.broadcasted_iota(jnp.int32, (8, N), 1) == 0
        )
        for i in range(PER):
            total = jnp.sum(jnp.sum(inner[i], axis=0, keepdims=True), axis=1, keepdims=True)
            w = pl.ds(pl.multiple_of(slots[i] * HALF, 8), 8)
            grad_ref[w, :N] = grad_ref[w, :N] - jnp.where(origin, total, 0.0)
    high, low = split(object_ref[...] * (1.0 / (N * N)))
    z = dot(jnp.concatenate([high, low, high], axis=1), table_rows(rb_ref))
    image = dot(lb_ref[...], rows3(swap_halves(z, HALF)))
    width = width_ref[0].astype(f32) + 1.0
    row = lax.broadcasted_iota(jnp.int32, (N, N), 0)
    col = lax.broadcasted_iota(jnp.int32, (N, N), 1)

    def ramp(index):
        distance = (jnp.minimum(index, N - 1 - index) + 1).astype(f32)
        return jnp.minimum(1.0, distance / width)

    weight = ramp(row) * ramp(col)
    head_ref[CHANNELS] = weight[:MARGIN]
    tail_ref[CHANNELS] = weight[N - MARGIN :]
    canvas_ref[CHANNELS] = weight
    for channel in range(CHANNELS):
        shown = image[:, channel * N : (channel + 1) * N] * weight
        canvas_ref[channel] = shown
        turned = shown.T
        head_ref[channel] = turned[:MARGIN]
        tail_ref[channel] = turned[N - MARGIN :]


TABLES = ("right_pupil", "left_pupil", "left_half", "right_full", "right_back", "left_back")


def object_kernel(
    width_ref, chan_ref, data_ref, mask_ref, phase_ref, lt_ref, taper_ref, weight_ref,
    rp_hbm, lp_hbm, lh_hbm, rf_hbm, rb_hbm, lb_hbm,
    grad_ref, field_ref, slope_ref, inv_ref, canvas_ref, head_ref, tail_ref,
    rp_ref, lp_ref, lh_ref, rf_ref, rb_ref, lb_ref, sems,
    otf_ref, line_ref, wide_ref, ph_ref, pl_ref, half_re_ref, half_im_ref, yh_ref, yl_ref,
    order_ref, sh_ref, sl_ref, spec_ref, object_ref,
):
    moves = (
        (rp_hbm, rp_ref), (lp_hbm, lp_ref), (lh_hbm, lh_ref),
        (rf_hbm, rf_ref), (rb_hbm, rb_ref), (lb_hbm, lb_ref),
    )
    copies = [
        pltpu.make_async_copy(source, target, sems.at[i])
        for i, (source, target) in enumerate(moves)
    ]
    for copy in copies:
        copy.start()

    def ready():
        for copy in copies:
            copy.wait()

    transfer_part(
        data_ref, chan_ref, mask_ref, phase_ref, rp_ref, lp_ref, lh_ref, rf_ref, ready,
        otf_ref, field_ref, slope_ref, inv_ref,
        line_ref, wide_ref, ph_ref, pl_ref, half_re_ref, half_im_ref, yh_ref, yl_ref,
    )
    object_part(
        width_ref, chan_ref, data_ref, otf_ref, lt_ref, taper_ref, weight_ref, rf_ref, rb_ref,
        lb_ref, grad_ref, canvas_ref, head_ref, tail_ref,
        order_ref, sh_ref, sl_ref, spec_ref, object_ref,
    )


def pack_kernel(coef_ref, shift_ref, pix_ref, out_ref, sem):
    copy = pltpu.make_async_copy(pix_ref, out_ref.at[:, :N, :], sem)
    copy.start()
    coef = jnp.concatenate([coef_ref[...], jnp.zeros((SLOTS, N - ZERN), f32)], axis=1)
    first = coef.astype(bf16).astype(f32)
    rest = coef - first
    second = rest.astype(bf16).astype(f32)
    third = rest - second
    shift = jnp.concatenate([shift_ref[...].astype(f32), jnp.zeros((6, SLOTS), f32)], axis=0)
    shift = jnp.concatenate([shift, jnp.zeros((8, N - SLOTS), f32)], axis=1)
    shift = jnp.concatenate([shift, jnp.zeros((N - 8, N), f32)], axis=0).T[:SLOTS]
    line = first + pltpu.roll(second, ZERN, 1) + pltpu.roll(third, 2 * ZERN, 1)
    line = line + pltpu.roll(shift, 3 * ZERN, 1)
    for slot in range(SLOTS):
        out_ref[slot, N:, :] = jnp.broadcast_to(line[slot : slot + 1], (8, N)).astype(bf16)
    copy.wait()


def pack(coef, shift, pixels):
    return pl.pallas_call(
        pack_kernel,
        out_shape=jax.ShapeDtypeStruct((SLOTS, ROWS, N), bf16),
        in_specs=[VM, VM, pl.BlockSpec(memory_space=pl.ANY)],
        out_specs=VM,
        scratch_shapes=[pltpu.SemaphoreType.DMA],
        name="pack",
        compiler_params=limit(4),
    )(coef, shift, pixels)


def fold_kernel(
    canvas_ref, left_ref, right_ref, grad_ref,
    middle_ref, head_ref, tail_ref, out_ref,
):
    out_ref[...] = grad_ref[...]
    gap = jnp.zeros((TILE - 2 * MARGIN, N), f32)
    rest = jnp.zeros((N - TILE, N), f32)
    for layer in range(CHANNELS + 1):
        sides = jnp.concatenate([left_ref[layer], gap, right_ref[layer], rest], axis=0).T
        total = pltpu.roll(canvas_ref[layer], N - MARGIN, 1) + sides
        head_ref[layer] = total[:MARGIN]
        middle_ref[layer] = total[MARGIN : N - MARGIN]
        tail_ref[layer] = total[N - MARGIN :]


def blend_kernel(middle_ref, upper_ref, lower_ref, out_ref):
    def folded(layer):
        return jnp.concatenate(
            [
                middle_ref[layer, :MARGIN] + upper_ref[layer],
                middle_ref[layer, MARGIN : TILE - MARGIN],
                middle_ref[layer, TILE - MARGIN :] + lower_ref[layer],
            ],
            axis=0,
        )

    weight = folded(CHANNELS)
    for channel in range(CHANNELS):
        out_ref[channel] = (folded(channel) / weight)[:, :TILE]


def gradient_kernel(
    chan_ref, grad_ref, field_ref, slope_ref, inv_ref, phase_ref, rb_ref, lb_ref, rp_ref, lp_ref,
    out_ref,
    z_ref, qh_ref, ql_ref, pupil_ref,
):
    cheb = tables()[1]
    right = table_rows(rb_ref)
    for pair in range(PAIRS):
        here = slice(pair * TWO, (pair + 1) * TWO)
        high, low = split(grad_ref[here, :])
        z_ref[here, :] = dot(jnp.concatenate([high, low, high], axis=1), right)
    left_b = lb_ref[...]
    left = table_lanes(rp_ref)
    for pair in range(PAIRS):
        here = slice(pair * TWO, (pair + 1) * TWO)
        power = dot(left_b, rows3(swap_halves(z_ref[here, :], HALF)))
        field = field_ref[pair]
        back = jnp.concatenate([field[:N] * power, field[N:] * power], axis=0)
        half = dot(left, rows3(back))
        high, low = split(swap_halves(half, PUP))
        here = slice(pair * N, (pair + 1) * N)
        qh_ref[here, :] = high
        ql_ref[here, :] = low
    right = table_rows(lp_ref)
    for pair in range(PAIRS):
        here = slice(pair * N, (pair + 1) * N)
        high = qh_ref[here, :]
        pupil_ref[here, :] = dot(jnp.concatenate([high, ql_ref[here, :], high], axis=1), right)
    sums = [None] * DEG
    for row in range(PUP // 2):
        both = []
        for at in (row, PUP - 1 - row):
            q = pupil_ref[pl.ds(at, SLOTS, stride=PUP), :]
            both.append(q * slope_ref[at * SLOTS : (at + 1) * SLOTS, :])
        parity = (both[0] + both[1], both[0] - both[1])
        for i in range(DEG):
            term = parity[i % 2] * float(cheb[row, i]) if i else parity[0]
            sums[i] = term if sums[i] is None else sums[i] + term
    total = lax.dot_general(
        jnp.concatenate(sums, axis=1), phase_ref[...], (((1,), (1,)), ((), ())),
        precision=lax.Precision.HIGHEST, preferred_element_type=f32,
    )
    factor = 4.0 / float(N * N * N)
    total = total * (slot_scales(chan_ref, COEF) * factor * inv_ref[:, :COEF])
    out_ref[...] = total[:, :ZERN]


def limit(mib):
    return pltpu.CompilerParams(vmem_limit_bytes=mib << 20)


def objects(width, chan, data, mask, tabs, interpret=False):
    rows = SLOTS * HALF
    margin = jax.ShapeDtypeStruct((CHANNELS + 1, MARGIN, N), f32)
    fixed = [tabs[name] for name in TABLES]
    return pl.pallas_call(
        object_kernel,
        out_shape=(
            jax.ShapeDtypeStruct((rows, 2 * N), f32),
            jax.ShapeDtypeStruct((PAIRS, 2 * N, 2 * N), f32),
            jax.ShapeDtypeStruct((PUP * SLOTS, N), f32),
            jax.ShapeDtypeStruct((SLOTS, N), f32),
            jax.ShapeDtypeStruct((CHANNELS + 1, N, N), f32),
            margin,
            margin,
        ),
        in_specs=[SM, SM] + [VM] * 6 + [pl.BlockSpec(memory_space=pltpu.HBM)] * len(TABLES),
        out_specs=(VM,) * 7,
        scratch_shapes=[pltpu.VMEM(table.shape, bf16) for table in fixed]
        + [
            pltpu.SemaphoreType.DMA((len(TABLES),)),
            pltpu.VMEM((rows, 2 * N), f32),
            pltpu.VMEM((SLOTS * 8, N), f32),
            pltpu.VMEM((PUP, N), f32),
            pltpu.VMEM((PUP * SLOTS, N), bf16),
            pltpu.VMEM((PUP * SLOTS, N), bf16),
            pltpu.VMEM((PUP * SLOTS, N), f32),
            pltpu.VMEM((PUP * SLOTS, N), f32),
            pltpu.VMEM((rows, 2 * N), bf16),
            pltpu.VMEM((rows, 2 * N), bf16),
            pltpu.SMEM((SLOTS,), jnp.int32),
            pltpu.VMEM((rows, 2 * N), bf16),
            pltpu.VMEM((rows, 2 * N), bf16),
            pltpu.VMEM((rows, 2 * N), f32),
            pltpu.VMEM((TWO, 2 * N), f32),
        ],
        interpret=interpret,
        name="objects",
        compiler_params=limit(16),
    )(
        width, chan, data, mask, tabs["phase"], tabs["left_taper"], tabs["taper"], tabs["weight"],
        *fixed,
    )


def gradient(chan, grad, field, slope, inverse, tabs, interpret=False):
    rows = SLOTS * HALF
    return pl.pallas_call(
        gradient_kernel,
        out_shape=jax.ShapeDtypeStruct((SLOTS, ZERN), f32),
        in_specs=[SM] + [VM] * 9,
        out_specs=VM,
        scratch_shapes=[
            pltpu.VMEM((rows, 2 * N), f32),
            pltpu.VMEM((SLOTS * PUP, 2 * N), bf16),
            pltpu.VMEM((SLOTS * PUP, 2 * N), bf16),
            pltpu.VMEM((SLOTS * PUP, N), f32),
        ],
        interpret=interpret,
        name="gradient",
        compiler_params=limit(16),
    )(
        chan, grad, field, slope, inverse, tabs["phase"], tabs["right_back"], tabs["left_back"],
        tabs["right_pupil"], tabs["left_pupil"],
    )


def fold(canvas, left, right, grad):
    margin = jax.ShapeDtypeStruct((CHANNELS + 1, MARGIN, N), f32)
    return pl.pallas_call(
        fold_kernel,
        out_shape=(
            jax.ShapeDtypeStruct((CHANNELS + 1, TILE, N), f32),
            margin,
            margin,
            jax.ShapeDtypeStruct((SLOTS, ZERN), f32),
        ),
        in_specs=[VM] * 4,
        out_specs=(VM,) * 4,
        name="fold",
        compiler_params=limit(8),
    )(canvas, left, right, grad)


def blend(middle, upper, lower):
    return pl.pallas_call(
        blend_kernel,
        out_shape=jax.ShapeDtypeStruct((CHANNELS, TILE, TILE), f32),
        in_specs=[VM] * 3,
        out_specs=VM,
        name="blend",
        compiler_params=limit(8),
    )(middle, upper, lower)


def shifted(cells, axis, forward):
    ends = lax.axis_size(axis) - 1
    if forward:
        return lax.ppermute(cells, axis, [(i, i + 1) for i in range(ends)])
    return lax.ppermute(cells, axis, [(i + 1, i) for i in range(ends)])


def per_device(coeffs, shifts, pixels, pupil_mask, chan_map, intersection):
    tabs = {name: jnp.asarray(table) for name, table in tables()[0].items()}
    coef = coeffs.reshape(SLOTS, ZERN)
    shift = shifts.reshape(SLOTS, 2).T
    data = pack(coef, shift, pixels.reshape(SLOTS, N, N)).reshape(1, SLOTS, 1, ROWS, N)
    data = lax.all_to_all(data, "patch", split_axis=1, concat_axis=0, tiled=True)
    grad, field, slope, inverse, canvas, head, tail = objects(
        intersection.reshape(1), chan_map, data.reshape(SLOTS, ROWS, N), pupil_mask, tabs
    )
    left = shifted(tail, "frame", True)
    right = shifted(head, "frame", False)
    grad = gradient(chan_map, grad, field, slope, inverse, tabs)
    middle, head, tail, grad = fold(canvas, left, right, grad)
    upper = shifted(tail, "patch", True)
    lower = shifted(head, "patch", False)
    grad = lax.all_to_all(
        grad.reshape(SLOTS, 1, 1, ZERN), "patch", split_axis=0, concat_axis=1, tiled=True
    )
    blended = blend(middle, upper, lower)
    return (blended, grad)


def solution(mesh):
    in_specs = (
        P("patch", None, "frame", None),
        P("patch", None, "frame", None),
        P("patch", None, "frame", None, None),
        P(),
        P(),
        P("patch", "frame"),
    )
    out_specs = (P(None, "patch", "frame"), P("patch", None, "frame", None))
    return jax.shard_map(
        per_device, mesh=mesh, in_specs=in_specs, out_specs=out_specs, check_vma=False
    )
```

```python
import functools
import math

import jax
import jax.numpy as jnp
import ml_dtypes
import numpy as np
from jax import lax
from jax.experimental import pallas as pl
from jax.experimental.pallas import tpu as pltpu
from jax.sharding import PartitionSpec as P


N = 128
PUP = 64
ZERN = 36
SLOTS = 16
PAIRS = SLOTS // 2
CHANNELS = 2
PER = SLOTS // CHANNELS
MARGIN = 16
TILE = N - 2 * MARGIN
HALF = 72
TWO = 2 * HALF
DEG = 9
COEF = 40
ROWS = N + 8
regular_gamma = 0.1
wave_ratio = 0.35
f32 = jnp.float32
bf16 = jnp.bfloat16
VM = pl.BlockSpec(memory_space=pltpu.VMEM)
SM = pl.BlockSpec(memory_space=pltpu.SMEM)
HB = pl.BlockSpec(memory_space=pltpu.HBM)


def noll_order(noll_index):
    radial = 0
    remain = noll_index - 1
    while remain > radial:
        radial += 1
        remain -= radial
    azimuth = radial % 2 + 2 * ((remain + (radial + 1) % 2) // 2)
    if noll_index % 2 == 1:
        azimuth = -azimuth
    return (radial, azimuth)


def zernike_modes():
    position = (np.arange(PUP) - (PUP - 1) / 2.0) / (PUP / 2.0)
    grid_y, grid_x = np.meshgrid(position, position, indexing="ij")
    radius = np.sqrt(grid_x * grid_x + grid_y * grid_y)
    theta = np.arctan2(grid_y, grid_x)
    modes = []
    for noll_index in range(2, ZERN + 2):
        radial, azimuth = noll_order(noll_index)
        order = abs(azimuth)
        total = np.zeros_like(radius)
        for step in range((radial - order) // 2 + 1):
            factor = math.factorial(radial - step) / (
                math.factorial(step)
                * math.factorial((radial + order) // 2 - step)
                * math.factorial((radial - order) // 2 - step)
            )
            total = total + (-1) ** step * factor * radius ** (radial - 2 * step)
        if azimuth == 0:
            modes.append(total * math.sqrt(radial + 1.0))
        elif azimuth > 0:
            modes.append(total * math.sqrt(2.0 * (radial + 1.0)) * np.cos(order * theta))
        else:
            modes.append(total * math.sqrt(2.0 * (radial + 1.0)) * np.sin(order * theta))
    return position, np.stack(modes)


def halves(table):
    high = table.astype(ml_dtypes.bfloat16)
    low = (table - high.astype(np.float64)).astype(ml_dtypes.bfloat16)
    return high, low


def pair_table(table):
    return np.stack(halves(table))


@functools.cache
def tables():
    index = np.arange(N)
    turns = 2.0 * np.pi / N * (np.outer(index, index) % N)
    c, s = np.cos(turns), np.sin(turns)
    cp, sp = c[:, :PUP], s[:, :PUP]
    ch, sh = c[:HALF], s[:HALF]
    distance = np.minimum(index, N - 1 - index)
    taper = np.where(distance < MARGIN, 0.5 - 0.5 * np.cos(np.pi * (distance + 0.5) / MARGIN), 1.0)
    weight = np.where(np.arange(HALF) < 1, 1.0, 2.0)
    weight[N // 2] = 1.0
    weight[N // 2 + 1 :] = 0.0
    out = {}
    out["right_pupil"] = pair_table(np.block([[cp.T, -sp.T], [sp.T, cp.T]]))
    out["left_pupil"] = pair_table(np.block([[cp, sp], [-sp, cp]]))
    out["left_half"] = pair_table(np.block([[ch], [-sh]]))
    out["right_full"] = pair_table(np.block([[c, -s], [s, c]]))
    out["right_back"] = pair_table(np.block([[c, s], [-s, c]]))
    high, low = halves(np.block([[ch], [-sh]]) * taper[None, :])
    out["left_taper"] = np.concatenate([high, low], axis=1)
    high, low = halves(np.concatenate([weight[None] * ch.T, -weight[None] * sh.T], axis=1))
    out["left_back"] = np.concatenate([high, high, low], axis=1)
    out["taper"] = np.tile(taper, 2)[None].astype(np.float32)
    out["weight"] = np.broadcast_to(weight[:, None], (HALF, N)).astype(np.float32)
    position, modes = zernike_modes()
    cheb = np.polynomial.chebyshev.chebvander(position, DEG - 1)
    fit = np.linalg.lstsq(cheb, modes.transpose(1, 0, 2).reshape(PUP, -1), rcond=None)[0]
    fit = fit.reshape(DEG, ZERN, PUP).transpose(1, 0, 2)
    phase = np.zeros((COEF, DEG, PUP))
    phase[:ZERN] = fit
    step = 2.0 * np.pi / N * (PUP / 2.0)
    phase[ZERN, 1] = step
    phase[ZERN + 1, 0] = step * position
    phase = np.concatenate([phase, phase], axis=2)
    out["phase"] = phase.reshape(COEF, DEG * N).astype(np.float32)
    return out, cheb


def split(x):
    high = x.astype(bf16)
    return high, (x - high.astype(f32)).astype(bf16)


def dot(left, right):
    return lax.dot_general(left, right, (((1,), (0,)), ((), ())), preferred_element_type=f32)


def rows3(x):
    high, low = split(x)
    return jnp.concatenate([high, low, high], axis=0)


def table_rows(ref):
    return jnp.concatenate([ref[0], ref[0], ref[1]], axis=0)


def table_lanes(ref):
    return jnp.concatenate([ref[0], ref[0], ref[1]], axis=1)


def swap_halves(y, count):
    top = jnp.concatenate([y[:count, :N], y[count:, :N]], axis=1)
    low = jnp.concatenate([y[:count, N:], y[count:, N:]], axis=1)
    return jnp.concatenate([top, low], axis=0)


def chebyshev_sums(parts, cheb, row):
    even = parts[0]
    for i in range(2, DEG, 2):
        even = even + float(cheb[row, i]) * parts[i]
    odd = float(cheb[row, 1]) * parts[1]
    for i in range(3, DEG, 2):
        odd = odd + float(cheb[row, i]) * parts[i]
    return even, odd


def turn(phase, lane_turns):
    count = jnp.floor(phase * (2.0 / math.pi) + 0.5)
    rest = phase - count * 1.5703125
    rest = rest - count * 4.837512969970703125e-4
    rest = rest - count * 7.549789954891882e-8
    quarter = count.astype(jnp.int32) + lane_turns
    sq = rest * rest
    sine = rest + rest * sq * (
        -1.6666654611e-1 + sq * (8.3321608736e-3 + sq * -1.9515295891e-4)
    )
    cosine = (1.0 - 0.5 * sq) + sq * sq * (
        4.166664568298827e-2 + sq * (-1.388731625493765e-3 + sq * 2.443315711809948e-5)
    )
    odd = (quarter & 1) == 1
    value = jnp.where(odd, sine, cosine)
    value = jnp.where(((quarter + 1) & 2) == 2, -value, value)
    slope = jnp.where(odd, cosine, sine)
    slope = jnp.where((quarter & 2) == 2, slope, -slope)
    return value, slope


def slot_scales(chan_ref, width):
    row = lax.broadcasted_iota(jnp.int32, (SLOTS, width), 0)
    channel = jnp.zeros((SLOTS, width), jnp.int32)
    for slot in range(SLOTS):
        channel = jnp.where(row == slot, chan_ref[slot], channel)
    return 1.0 / (1.0 + wave_ratio * channel.astype(f32))


def transfer_part(
    data_ref, chan_ref, mask_ref, phase_ref, rp_ref, lp_ref, lh_ref, rf_ref, ready,
    otf_ref, field_ref, slope_ref, inv_ref,
    line_ref, wide_ref, ph_ref, pl_ref, half_re_ref, half_im_ref, yh_ref, yl_ref,
):
    cheb = tables()[1]
    for slot in range(SLOTS):
        line_ref[slot * 8 : slot * 8 + 8, :] = data_ref[slot, N:, :].astype(f32)
    line = line_ref[pl.ds(0, SLOTS, stride=8), :]
    coef = line + (pltpu.roll(line, N - ZERN, 1) + pltpu.roll(line, N - 2 * ZERN, 1))
    lane = lax.broadcasted_iota(jnp.int32, (SLOTS, N), 1)
    shift = pltpu.roll(line, N - 2 * ZERN, 1)
    coef = jnp.where(lane < ZERN, coef * slot_scales(chan_ref, N), shift)[:, :COEF]
    mask = mask_ref[...].astype(f32)
    wide_ref[...] = jnp.concatenate([mask, mask], axis=1)
    parts_all = lax.dot_general(
        coef, phase_ref[...], (((1,), (0,)), ((), ())),
        precision=lax.Precision.HIGHEST, preferred_element_type=f32,
    )
    parts = [parts_all[:, i * N : (i + 1) * N] for i in range(DEG)]
    lane_turns = jnp.where(lax.broadcasted_iota(jnp.int32, (SLOTS, N), 1) < PUP, 0, 3)
    for row in range(PUP // 2):
        even, odd = chebyshev_sums(parts, cheb, row)
        for at, phase in ((row, even + odd), (PUP - 1 - row, even - odd)):
            value, slope = turn(phase, lane_turns)
            mask = wide_ref[at : at + 1, :]
            value = value * mask
            here = slice(at * SLOTS, (at + 1) * SLOTS)
            slope_ref[here, :] = slope * mask
            high, low = split(value)
            ph_ref[here, :] = high
            pl_ref[here, :] = low
    ready()
    right = table_rows(rp_ref)
    for chunk in range(4):
        here = slice(chunk * 256, (chunk + 1) * 256)
        high = ph_ref[here, :]
        half = dot(jnp.concatenate([high, pl_ref[here, :], high], axis=1), right)
        half_re_ref[here, :] = half[:, :N]
        half_im_ref[here, :] = half[:, N:]
    left = table_lanes(lp_ref)
    left_h = table_lanes(lh_ref)
    for pair in range(PAIRS):
        columns = []
        for part_ref in (half_re_ref, half_im_ref):
            columns.append(
                jnp.concatenate(
                    [
                        part_ref[pl.ds(2 * pair + which, PUP, stride=SLOTS), :]
                        for which in range(2)
                    ],
                    axis=1,
                )
            )
        field = dot(left, rows3(jnp.concatenate(columns, axis=0)))
        field_ref[pair] = field
        power = field[:N] * field[:N] + field[N:] * field[N:]
        y = dot(left_h, rows3(power))
        high, low = split(swap_halves(y, HALF))
        here = slice(pair * TWO, (pair + 1) * TWO)
        yh_ref[here, :] = high
        yl_ref[here, :] = low
    right = table_rows(rf_ref)
    for pair in range(PAIRS):
        here = slice(pair * TWO, (pair + 1) * TWO)
        high = yh_ref[here, :]
        out = dot(jnp.concatenate([high, yl_ref[here, :], high], axis=1), right)
        for which in range(2):
            slot = 2 * pair + which
            block = out[which * HALF : (which + 1) * HALF]
            inverse = 1.0 / block[0:1, 0:1]
            otf_ref[slot * HALF : (slot + 1) * HALF, :] = block * inverse
            inv_ref[slot : slot + 1, :] = jnp.broadcast_to(inverse, (1, N))


def object_part(
    width_ref, chan_ref, pix_ref, otf_ref, lt_ref, taper_ref, weight_ref, rf_ref, rb_ref, lb_ref,
    grad_ref, canvas_ref, head_ref, tail_ref,
    order_ref, yh_ref, yl_ref, spec_ref, object_ref,
):
    at = [jnp.int32(0), jnp.int32(PER)]
    for slot in range(SLOTS):
        first = chan_ref[slot] == 0
        order_ref[jnp.where(first, at[0], at[1])] = slot
        at = [jnp.where(first, at[0] + 1, at[0]), jnp.where(first, at[1], at[1] + 1)]
    left = lt_ref[...]
    taper = taper_ref[...]
    for pair in range(PAIRS):
        image = jnp.concatenate([pix_ref[2 * pair, :N, :], pix_ref[2 * pair + 1, :N, :]], axis=1)
        y = dot(left, jnp.concatenate([image, image], axis=0)) * taper
        high, low = split(swap_halves(y, HALF))
        here = slice(pair * TWO, (pair + 1) * TWO)
        yh_ref[here, :] = high
        yl_ref[here, :] = low
    right = table_rows(rf_ref)
    for pair in range(PAIRS):
        here = slice(pair * TWO, (pair + 1) * TWO)
        high = yh_ref[here, :]
        spec_ref[here, :] = dot(jnp.concatenate([high, yl_ref[here, :], high], axis=1), right)
    for channel in range(CHANNELS):
        slots = [order_ref[channel * PER + i] for i in range(PER)]
        inner = [jnp.zeros((8, N), f32) for _ in range(PER)]
        for block in range(HALF // 8):
            where = [pl.ds(pl.multiple_of(slot * HALF + block * 8, 8), 8) for slot in slots]
            h_re = [otf_ref[w, :N] for w in where]
            h_im = [otf_ref[w, N:] for w in where]
            s_re = [spec_ref[w, :N] for w in where]
            s_im = [spec_ref[w, N:] for w in where]
            num_re = num_im = 0.0
            den = regular_gamma
            for i in range(PER):
                num_re = num_re + (h_re[i] * s_re[i] + h_im[i] * s_im[i])
                num_im = num_im + (h_re[i] * s_im[i] - h_im[i] * s_re[i])
                den = den + (h_re[i] * h_re[i] + h_im[i] * h_im[i])
            inverse = 1.0 / den
            o_re = num_re * inverse
            o_im = num_im * inverse
            rows = slice(channel * HALF + block * 8, channel * HALF + block * 8 + 8)
            object_ref[rows, :N] = o_re
            object_ref[rows, N:] = o_im
            weight = weight_ref[block * 8 : block * 8 + 8, :]
            for i in range(PER):
                r_re = s_re[i] - (o_re * h_re[i] - o_im * h_im[i])
                r_im = s_im[i] - (o_re * h_im[i] + o_im * h_re[i])
                g_re = -(r_re * o_re + r_im * o_im)
                g_im = r_re * o_im - r_im * o_re
                inner[i] = inner[i] + weight * (g_re * h_re[i] + g_im * h_im[i])
                grad_ref[where[i], :N] = g_re
                grad_ref[where[i], N:] = g_im
        origin = (lax.broadcasted_iota(jnp.int32, (8, N), 0) == 0) & (
            lax.broadcasted_iota(jnp.int32, (8, N), 1) == 0
        )
        for i in range(PER):
            total = jnp.sum(jnp.sum(inner[i], axis=0, keepdims=True), axis=1, keepdims=True)
            w = pl.ds(pl.multiple_of(slots[i] * HALF, 8), 8)
            grad_ref[w, :N] = grad_ref[w, :N] - jnp.where(origin, total, 0.0)
    high, low = split(object_ref[...] * (1.0 / (N * N)))
    z = dot(jnp.concatenate([high, low, high], axis=1), table_rows(rb_ref))
    image = dot(lb_ref[...], rows3(swap_halves(z, HALF)))
    width = width_ref[0].astype(f32) + 1.0
    row = lax.broadcasted_iota(jnp.int32, (N, N), 0)
    col = lax.broadcasted_iota(jnp.int32, (N, N), 1)

    def ramp(index):
        distance = (jnp.minimum(index, N - 1 - index) + 1).astype(f32)
        return jnp.minimum(1.0, distance / width)

    weight = ramp(row) * ramp(col)
    head_ref[CHANNELS] = weight[:MARGIN]
    tail_ref[CHANNELS] = weight[N - MARGIN :]
    canvas_ref[CHANNELS] = weight
    for channel in range(CHANNELS):
        shown = image[:, channel * N : (channel + 1) * N] * weight
        canvas_ref[channel] = shown
        turned = shown.T
        head_ref[channel] = turned[:MARGIN]
        tail_ref[channel] = turned[N - MARGIN :]


TABLES = ("right_pupil", "left_pupil", "left_half", "right_full", "right_back", "left_back")


def object_kernel(
    width_ref, chan_ref, data_ref, mask_ref, phase_ref, lt_ref, taper_ref, weight_ref,
    rp_hbm, lp_hbm, lh_hbm, rf_hbm, rb_hbm, lb_hbm,
    grad_ref, field_ref, slope_ref, inv_ref, canvas_ref, head_ref, tail_ref,
    rp_ref, lp_ref, lh_ref, rf_ref, rb_ref, lb_ref, sems,
    otf_ref, line_ref, wide_ref, ph_ref, pl_ref, half_re_ref, half_im_ref, yh_ref, yl_ref,
    order_ref, sh_ref, sl_ref, spec_ref, object_ref,
):
    moves = (
        (rp_hbm, rp_ref), (lp_hbm, lp_ref), (lh_hbm, lh_ref),
        (rf_hbm, rf_ref), (rb_hbm, rb_ref), (lb_hbm, lb_ref),
    )
    copies = [
        pltpu.make_async_copy(source, target, sems.at[i])
        for i, (source, target) in enumerate(moves)
    ]
    for copy in copies:
        copy.start()

    def ready():
        for copy in copies:
            copy.wait()

    transfer_part(
        data_ref, chan_ref, mask_ref, phase_ref, rp_ref, lp_ref, lh_ref, rf_ref, ready,
        otf_ref, field_ref, slope_ref, inv_ref,
        line_ref, wide_ref, ph_ref, pl_ref, half_re_ref, half_im_ref, yh_ref, yl_ref,
    )
    object_part(
        width_ref, chan_ref, data_ref, otf_ref, lt_ref, taper_ref, weight_ref, rf_ref, rb_ref,
        lb_ref, grad_ref, canvas_ref, head_ref, tail_ref,
        order_ref, sh_ref, sl_ref, spec_ref, object_ref,
    )


def pack_kernel(coef_hbm, shift_hbm, pix_hbm, out_ref, coef_ref, shift_ref, sems):
    coef_copy = pltpu.make_async_copy(coef_hbm, coef_ref, sems.at[0])
    shift_copy = pltpu.make_async_copy(shift_hbm, shift_ref, sems.at[1])
    pix_copy = pltpu.make_async_copy(pix_hbm, out_ref.at[:, :N, :], sems.at[2])
    coef_copy.start()
    shift_copy.start()
    pix_copy.start()
    coef_copy.wait()
    shift_copy.wait()
    coef = jnp.concatenate([coef_ref[...], jnp.zeros((SLOTS, N - ZERN), f32)], axis=1)
    first = coef.astype(bf16).astype(f32)
    rest = coef - first
    second = rest.astype(bf16).astype(f32)
    third = rest - second
    shift = jnp.concatenate([shift_ref[...].astype(f32), jnp.zeros((6, SLOTS), f32)], axis=0)
    shift = jnp.concatenate([shift, jnp.zeros((8, N - SLOTS), f32)], axis=1)
    shift = jnp.concatenate([shift, jnp.zeros((N - 8, N), f32)], axis=0).T[:SLOTS]
    line = first + pltpu.roll(second, ZERN, 1) + pltpu.roll(third, 2 * ZERN, 1)
    line = line + pltpu.roll(shift, 3 * ZERN, 1)
    for slot in range(SLOTS):
        out_ref[slot, N:, :] = jnp.broadcast_to(line[slot : slot + 1], (8, N)).astype(bf16)
    pix_copy.wait()


def pack(coef, shift, pixels):
    return pl.pallas_call(
        pack_kernel,
        out_shape=jax.ShapeDtypeStruct((SLOTS, ROWS, N), bf16),
        in_specs=[HB] * 3,
        out_specs=VM,
        scratch_shapes=[
            pltpu.VMEM((SLOTS, ZERN), f32),
            pltpu.VMEM((2, SLOTS), jnp.int32),
            pltpu.SemaphoreType.DMA((3,)),
        ],
        name="pack",
        compiler_params=limit(4),
    )(*[pltpu.with_memory_space_constraint(x, pltpu.HBM) for x in (coef, shift, pixels)])


def fold_kernel(
    canvas_ref, left_ref, right_ref,
    middle_ref, head_ref, tail_ref,
):
    gap = jnp.zeros((TILE - 2 * MARGIN, N), f32)
    rest = jnp.zeros((N - TILE, N), f32)
    for layer in range(CHANNELS + 1):
        sides = jnp.concatenate([left_ref[layer], gap, right_ref[layer], rest], axis=0).T
        total = pltpu.roll(canvas_ref[layer], N - MARGIN, 1) + sides
        head_ref[layer] = total[:MARGIN]
        middle_ref[layer] = total[MARGIN : N - MARGIN]
        tail_ref[layer] = total[N - MARGIN :]


def blend_kernel(middle_ref, upper_ref, lower_ref, out_ref):
    def folded(layer):
        return jnp.concatenate(
            [
                middle_ref[layer, :MARGIN] + upper_ref[layer],
                middle_ref[layer, MARGIN : TILE - MARGIN],
                middle_ref[layer, TILE - MARGIN :] + lower_ref[layer],
            ],
            axis=0,
        )

    weight = folded(CHANNELS)
    for channel in range(CHANNELS):
        out_ref[channel] = (folded(channel) / weight)[:, :TILE]


def gradient_kernel(
    chan_ref, grad_ref, field_ref, slope_ref, inv_ref, phase_ref, rb_ref, lb_ref, rp_ref, lp_ref,
    out_ref,
    z_ref, qh_ref, ql_ref, pupil_ref,
):
    cheb = tables()[1]
    right = table_rows(rb_ref)
    for pair in range(PAIRS):
        here = slice(pair * TWO, (pair + 1) * TWO)
        high, low = split(grad_ref[here, :])
        z_ref[here, :] = dot(jnp.concatenate([high, low, high], axis=1), right)
    left_b = lb_ref[...]
    left = table_lanes(rp_ref)
    for pair in range(PAIRS):
        here = slice(pair * TWO, (pair + 1) * TWO)
        power = dot(left_b, rows3(swap_halves(z_ref[here, :], HALF)))
        field = field_ref[pair]
        back = jnp.concatenate([field[:N] * power, field[N:] * power], axis=0)
        half = dot(left, rows3(back))
        high, low = split(swap_halves(half, PUP))
        here = slice(pair * N, (pair + 1) * N)
        qh_ref[here, :] = high
        ql_ref[here, :] = low
    right = table_rows(lp_ref)
    for pair in range(PAIRS):
        here = slice(pair * N, (pair + 1) * N)
        high = qh_ref[here, :]
        pupil_ref[here, :] = dot(jnp.concatenate([high, ql_ref[here, :], high], axis=1), right)
    sums = [None] * DEG
    for row in range(PUP // 2):
        both = []
        for at in (row, PUP - 1 - row):
            q = pupil_ref[pl.ds(at, SLOTS, stride=PUP), :]
            both.append(q * slope_ref[at * SLOTS : (at + 1) * SLOTS, :])
        parity = (both[0] + both[1], both[0] - both[1])
        for i in range(DEG):
            term = parity[i % 2] * float(cheb[row, i]) if i else parity[0]
            sums[i] = term if sums[i] is None else sums[i] + term
    total = lax.dot_general(
        jnp.concatenate(sums, axis=1), phase_ref[...], (((1,), (1,)), ((), ())),
        precision=lax.Precision.HIGHEST, preferred_element_type=f32,
    )
    factor = 4.0 / float(N * N * N)
    total = total * (slot_scales(chan_ref, COEF) * factor * inv_ref[:, :COEF])
    out_ref[...] = total[:, :ZERN]


def limit(mib):
    return pltpu.CompilerParams(vmem_limit_bytes=mib << 20)


def objects(width, chan, data, mask, tabs, interpret=False):
    rows = SLOTS * HALF
    margin = jax.ShapeDtypeStruct((CHANNELS + 1, MARGIN, N), f32)
    fixed = [tabs[name] for name in TABLES]
    return pl.pallas_call(
        object_kernel,
        out_shape=(
            jax.ShapeDtypeStruct((rows, 2 * N), f32),
            jax.ShapeDtypeStruct((PAIRS, 2 * N, 2 * N), f32),
            jax.ShapeDtypeStruct((PUP * SLOTS, N), f32),
            jax.ShapeDtypeStruct((SLOTS, N), f32),
            jax.ShapeDtypeStruct((CHANNELS + 1, N, N), f32),
            margin,
            margin,
        ),
        in_specs=[SM, SM] + [VM] * 6 + [HB] * len(TABLES),
        out_specs=(VM,) * 7,
        scratch_shapes=[pltpu.VMEM(table.shape, bf16) for table in fixed]
        + [
            pltpu.SemaphoreType.DMA((len(TABLES),)),
            pltpu.VMEM((rows, 2 * N), f32),
            pltpu.VMEM((SLOTS * 8, N), f32),
            pltpu.VMEM((PUP, N), f32),
            pltpu.VMEM((PUP * SLOTS, N), bf16),
            pltpu.VMEM((PUP * SLOTS, N), bf16),
            pltpu.VMEM((PUP * SLOTS, N), f32),
            pltpu.VMEM((PUP * SLOTS, N), f32),
            pltpu.VMEM((rows, 2 * N), bf16),
            pltpu.VMEM((rows, 2 * N), bf16),
            pltpu.SMEM((SLOTS,), jnp.int32),
            pltpu.VMEM((rows, 2 * N), bf16),
            pltpu.VMEM((rows, 2 * N), bf16),
            pltpu.VMEM((rows, 2 * N), f32),
            pltpu.VMEM((TWO, 2 * N), f32),
        ],
        interpret=interpret,
        name="objects",
        compiler_params=limit(16),
    )(
        width, chan, data, mask, tabs["phase"], tabs["left_taper"], tabs["taper"], tabs["weight"],
        *fixed,
    )


def gradient(chan, grad, field, slope, inverse, tabs, interpret=False):
    rows = SLOTS * HALF
    return pl.pallas_call(
        gradient_kernel,
        out_shape=jax.ShapeDtypeStruct((SLOTS, ZERN), f32),
        in_specs=[SM] + [VM] * 9,
        out_specs=VM,
        scratch_shapes=[
            pltpu.VMEM((rows, 2 * N), f32),
            pltpu.VMEM((SLOTS * PUP, 2 * N), bf16),
            pltpu.VMEM((SLOTS * PUP, 2 * N), bf16),
            pltpu.VMEM((SLOTS * PUP, N), f32),
        ],
        interpret=interpret,
        name="gradient",
        compiler_params=limit(16),
    )(
        chan, grad, field, slope, inverse, tabs["phase"], tabs["right_back"], tabs["left_back"],
        tabs["right_pupil"], tabs["left_pupil"],
    )


def fold(canvas, left, right):
    margin = jax.ShapeDtypeStruct((CHANNELS + 1, MARGIN, N), f32)
    return pl.pallas_call(
        fold_kernel,
        out_shape=(
            jax.ShapeDtypeStruct((CHANNELS + 1, TILE, N), f32),
            margin,
            margin,
        ),
        in_specs=[VM] * 3,
        out_specs=(VM,) * 3,
        name="fold",
        compiler_params=limit(8),
    )(canvas, left, right)


def blend(middle, upper, lower):
    return pl.pallas_call(
        blend_kernel,
        out_shape=jax.ShapeDtypeStruct((CHANNELS, TILE, TILE), f32),
        in_specs=[VM] * 3,
        out_specs=VM,
        name="blend",
        compiler_params=limit(8),
    )(middle, upper, lower)


def shifted(cells, axis, forward):
    ends = lax.axis_size(axis) - 1
    if forward:
        return lax.ppermute(cells, axis, [(i, i + 1) for i in range(ends)])
    return lax.ppermute(cells, axis, [(i + 1, i) for i in range(ends)])


def per_device(coeffs, shifts, pixels, pupil_mask, chan_map, intersection):
    tabs = {name: jnp.asarray(table) for name, table in tables()[0].items()}
    coef = coeffs.reshape(SLOTS, ZERN)
    shift = shifts.reshape(SLOTS, 2).T
    data = pack(coef, shift, pixels.reshape(SLOTS, N, N)).reshape(1, SLOTS, 1, ROWS, N)
    data = lax.all_to_all(data, "patch", split_axis=1, concat_axis=0, tiled=True)
    grad, field, slope, inverse, canvas, head, tail = objects(
        intersection.reshape(1), chan_map, data.reshape(SLOTS, ROWS, N), pupil_mask, tabs
    )
    left = shifted(tail, "frame", True)
    right = shifted(head, "frame", False)
    grad = gradient(chan_map, grad, field, slope, inverse, tabs)
    grad = lax.all_to_all(
        grad.reshape(SLOTS, 1, 1, ZERN), "patch", split_axis=0, concat_axis=1, tiled=True
    )
    middle, head, tail = fold(canvas, left, right)
    upper = shifted(tail, "patch", True)
    lower = shifted(head, "patch", False)
    blended = blend(middle, upper, lower)
    return (blended, grad)


def solution(mesh):
    in_specs = (
        P("patch", None, "frame", None),
        P("patch", None, "frame", None),
        P("patch", None, "frame", None, None),
        P(),
        P(),
        P("patch", "frame"),
    )
    out_specs = (P(None, "patch", "frame"), P("patch", None, "frame", None))
    return jax.shard_map(
        per_device, mesh=mesh, in_specs=in_specs, out_specs=out_specs, check_vma=False
    )
```

```python
import functools
import math

import jax
import jax.numpy as jnp
import ml_dtypes
import numpy as np
from jax import lax
from jax.experimental import pallas as pl
from jax.experimental.pallas import tpu as pltpu
from jax.sharding import PartitionSpec as P


N = 128
PUP = 64
ZERN = 36
SLOTS = 16
PAIRS = SLOTS // 2
CHANNELS = 2
PER = SLOTS // CHANNELS
MARGIN = 16
TILE = N - 2 * MARGIN
HALF = 72
TWO = 2 * HALF
DEG = 9
DEG_ROWS = 16
BLOCKS = HALF // 8
COEF = 40
ROWS = N + 8
regular_gamma = 0.1
wave_ratio = 0.35
f32 = jnp.float32
bf16 = jnp.bfloat16
VM = pl.BlockSpec(memory_space=pltpu.VMEM)
SM = pl.BlockSpec(memory_space=pltpu.SMEM)
HB = pl.BlockSpec(memory_space=pltpu.HBM)


def noll_order(noll_index):
    radial = 0
    remain = noll_index - 1
    while remain > radial:
        radial += 1
        remain -= radial
    azimuth = radial % 2 + 2 * ((remain + (radial + 1) % 2) // 2)
    if noll_index % 2 == 1:
        azimuth = -azimuth
    return (radial, azimuth)


def zernike_modes():
    position = (np.arange(PUP) - (PUP - 1) / 2.0) / (PUP / 2.0)
    grid_y, grid_x = np.meshgrid(position, position, indexing="ij")
    radius = np.sqrt(grid_x * grid_x + grid_y * grid_y)
    theta = np.arctan2(grid_y, grid_x)
    modes = []
    for noll_index in range(2, ZERN + 2):
        radial, azimuth = noll_order(noll_index)
        order = abs(azimuth)
        total = np.zeros_like(radius)
        for step in range((radial - order) // 2 + 1):
            factor = math.factorial(radial - step) / (
                math.factorial(step)
                * math.factorial((radial + order) // 2 - step)
                * math.factorial((radial - order) // 2 - step)
            )
            total = total + (-1) ** step * factor * radius ** (radial - 2 * step)
        if azimuth == 0:
            modes.append(total * math.sqrt(radial + 1.0))
        elif azimuth > 0:
            modes.append(total * math.sqrt(2.0 * (radial + 1.0)) * np.cos(order * theta))
        else:
            modes.append(total * math.sqrt(2.0 * (radial + 1.0)) * np.sin(order * theta))
    return position, np.stack(modes)


def halves(table):
    high = table.astype(ml_dtypes.bfloat16)
    low = (table - high.astype(np.float64)).astype(ml_dtypes.bfloat16)
    return high, low


def pair_table(table):
    return np.stack(halves(table))


@functools.cache
def tables():
    index = np.arange(N)
    turns = 2.0 * np.pi / N * (np.outer(index, index) % N)
    c, s = np.cos(turns), np.sin(turns)
    cp, sp = c[:, :PUP], s[:, :PUP]
    ch, sh = c[:HALF], s[:HALF]
    distance = np.minimum(index, N - 1 - index)
    taper = np.where(distance < MARGIN, 0.5 - 0.5 * np.cos(np.pi * (distance + 0.5) / MARGIN), 1.0)
    weight = np.where(np.arange(HALF) < 1, 1.0, 2.0)
    weight[N // 2] = 1.0
    weight[N // 2 + 1 :] = 0.0
    out = {}
    out["right_pupil"] = pair_table(np.block([[cp.T, -sp.T], [sp.T, cp.T]]))
    out["left_pupil"] = pair_table(np.block([[cp, sp], [-sp, cp]]))
    out["left_half"] = pair_table(np.block([[ch], [-sh]]))
    out["right_full"] = pair_table(np.block([[c, -s], [s, c]]))
    out["right_back"] = pair_table(np.block([[c, s], [-s, c]]))
    high, low = halves(np.block([[ch], [-sh]]) * taper[None, :])
    out["left_taper"] = np.concatenate([high, low], axis=1)
    high, low = halves(np.concatenate([weight[None] * ch.T, -weight[None] * sh.T], axis=1))
    out["left_back"] = np.concatenate([high, high, low], axis=1)
    out["taper"] = np.tile(taper, 2)[None].astype(np.float32)
    out["weight"] = np.broadcast_to(weight[:, None] / 2.0, (HALF, N)).astype(np.float32)
    position, modes = zernike_modes()
    cheb = np.polynomial.chebyshev.chebvander(position, DEG - 1)
    fit = np.linalg.lstsq(cheb, modes.transpose(1, 0, 2).reshape(PUP, -1), rcond=None)[0]
    fit = fit.reshape(DEG, ZERN, PUP).transpose(1, 0, 2)
    phase = np.zeros((COEF, DEG, PUP))
    phase[:ZERN] = fit
    step = 2.0 * np.pi / N * (PUP / 2.0)
    phase[ZERN, 1] = step
    phase[ZERN + 1, 0] = step * position
    phase = np.concatenate([phase, phase], axis=2)
    out["phase"] = (phase / (2.0 * np.pi)).reshape(COEF, DEG * N).astype(np.float32)
    spread = np.zeros((DEG_ROWS, PUP))
    spread[:DEG] = cheb.T
    high, low = halves(spread)
    out["sums"] = np.concatenate([high, high, low], axis=1)
    return out, cheb


def split(x):
    high = x.astype(bf16)
    return high, (x - high.astype(f32)).astype(bf16)


def dot(left, right):
    return lax.dot_general(left, right, (((1,), (0,)), ((), ())), preferred_element_type=f32)


def rows3(x):
    high, low = split(x)
    return jnp.concatenate([high, low, high], axis=0)


def table_rows(ref):
    return jnp.concatenate([ref[0], ref[0], ref[1]], axis=0)


def table_lanes(ref):
    return jnp.concatenate([ref[0], ref[0], ref[1]], axis=1)


def swap_halves(y, count):
    top = jnp.concatenate([y[:count, :N], y[count:, :N]], axis=1)
    low = jnp.concatenate([y[:count, N:], y[count:, N:]], axis=1)
    return jnp.concatenate([top, low], axis=0)


SINE = (3.141592616, -5.167708583, 2.55005456, -0.5981644139, 0.07742681132)
COSINE = (0.9999999532, -4.934792831, 4.058411353, -1.331876568, 0.2196896111)


def blocked(y):
    pieces = []
    for block in range(BLOCKS):
        rows = slice(block * 8, block * 8 + 8)
        im_rows = slice(HALF + block * 8, HALF + block * 8 + 8)
        for which in range(2):
            lanes = slice(which * N, (which + 1) * N)
            pieces.append(jnp.concatenate([y[rows, lanes], y[im_rows, lanes]], axis=1))
    return jnp.concatenate(pieces, axis=0)


def store_blocked(y, pair, base, yh_ref, yl_ref):
    high, low = split(blocked(y))
    rows = slice(base + pair * 16, base + pair * 16 + 16)
    for block in range(BLOCKS):
        yh_ref[block, rows, :] = high[block * 16 : block * 16 + 16]
        yl_ref[block, rows, :] = low[block * 16 : block * 16 + 16]


def chebyshev_sum(parts, cheb, row):
    total = parts[0]
    for i in range(1, DEG):
        total = total + float(cheb[row, i]) * parts[i]
    return total


def series(factors, square):
    total = factors[-1] * square + factors[-2]
    for factor in factors[-3::-1]:
        total = total * square + factor
    return total


def turned(turns):
    rest = turns - jnp.round(turns)
    square = rest * rest
    sine = rest * series(SINE, square)
    twice = sine + sine
    return 1.0 - twice * sine, twice * series(COSINE, square)


def slot_scales(chan_ref, width):
    row = lax.broadcasted_iota(jnp.int32, (SLOTS, width), 0)
    channel = jnp.zeros((SLOTS, width), jnp.int32)
    for slot in range(SLOTS):
        channel = jnp.where(row == slot, chan_ref[slot], channel)
    return 1.0 / (1.0 + wave_ratio * channel.astype(f32))


def transfer_part(
    data_ref, chan_ref, mask_ref, phase_ref, rp_ref, lp_ref, lh_ref, ready, spectra,
    field_ref, slope_ref,
    line_ref, wide_ref, ph_ref, pl_ref, half_re_ref, half_im_ref, power_ref, yh_ref, yl_ref,
):
    cheb = tables()[1]
    for slot in range(SLOTS):
        line_ref[slot * 8 : slot * 8 + 8, :] = data_ref[slot, N:, :].astype(f32)
    line = line_ref[pl.ds(0, SLOTS, stride=8), :]
    coef = line + (pltpu.roll(line, N - ZERN, 1) + pltpu.roll(line, N - 2 * ZERN, 1))
    lane = lax.broadcasted_iota(jnp.int32, (SLOTS, N), 1)
    shift = pltpu.roll(line, N - 2 * ZERN, 1)
    coef = jnp.where(lane < ZERN, coef * slot_scales(chan_ref, N), shift)[:, :COEF]
    mask = mask_ref[...].astype(f32)
    wide_ref[...] = jnp.concatenate([mask, mask], axis=1)
    parts_all = lax.dot_general(
        coef, phase_ref[...], (((1,), (0,)), ((), ())),
        precision=lax.Precision.HIGHEST, preferred_element_type=f32,
    )
    first = lax.broadcasted_iota(jnp.int32, (SLOTS, N), 1) < PUP
    sign = jnp.where(first, 1.0, -1.0)
    parts = [parts_all[:, i * N : (i + 1) * N] for i in range(DEG)]
    parts = [part * sign if i % 2 else part for i, part in enumerate(parts)]
    for row in range(PUP // 2):
        if row % 4 == 0:
            spectra(row // 4)
        far = PUP - 1 - row
        cosine, sine = turned(chebyshev_sum(parts, cheb, row))
        mask = jnp.where(first, wide_ref[row : row + 1, :], wide_ref[far : far + 1, :])
        cosine = cosine * mask
        sine = sine * mask
        far_cosine = pltpu.roll(cosine, PUP, 1)
        far_sine = pltpu.roll(sine, PUP, 1)
        here = slice(row * SLOTS, (row + 1) * SLOTS)
        there = slice(far * SLOTS, (far + 1) * SLOTS)
        slope_ref[here, :] = jnp.where(first, -sine, far_cosine)
        slope_ref[there, :] = jnp.where(first, -far_sine, cosine)
        high, low = split(jnp.where(first, cosine, far_sine))
        ph_ref[here, :] = high
        pl_ref[here, :] = low
        high, low = split(jnp.where(first, far_cosine, sine))
        ph_ref[there, :] = high
        pl_ref[there, :] = low
    ready()
    right = table_rows(rp_ref)
    for chunk in range(2):
        here = slice(chunk * 512, (chunk + 1) * 512)
        high = ph_ref[here, :]
        half = dot(jnp.concatenate([high, pl_ref[here, :], high], axis=1), right)
        half_re_ref[here, :] = half[:, :N]
        half_im_ref[here, :] = half[:, N:]
    left = table_lanes(lp_ref)
    for pair in range(PAIRS):
        columns = []
        for part_ref in (half_re_ref, half_im_ref):
            columns.append(
                jnp.concatenate(
                    [part_ref[pl.ds(2 * pair + which, PUP, stride=SLOTS), :] for which in range(2)],
                    axis=1,
                )
            )
        field = dot(left, rows3(jnp.concatenate(columns, axis=0)))
        field_ref[pair] = field
        high, low = split(field[:N] * field[:N] + field[N:] * field[N:])
        power_ref[pair, :N] = high
        power_ref[pair, N:] = low
    left = table_lanes(lh_ref)
    for pair in range(PAIRS):
        high = power_ref[pair, :N]
        y = dot(left, jnp.concatenate([high, power_ref[pair, N:], high], axis=0))
        store_blocked(y, pair, 0, yh_ref, yl_ref)


def object_part(
    width_ref, slots, weight_ref, rf_ref, rb_ref, lb_ref,
    grad_ref, inv_ref, canvas_ref, head_ref, tail_ref,
    yh_ref, yl_ref, plane_ref, object_ref, inner_ref,
):
    right = table_rows(rf_ref)
    for block in range(BLOCKS):
        high = yh_ref[block]
        plane_ref[block] = dot(jnp.concatenate([high, yl_ref[block], high], axis=1), right)
        if block == 0:
            for slot in range(SLOTS):
                inverse = 1.0 / plane_ref[0, slot * 8 : slot * 8 + 1, 0:1]
                inv_ref[slot * 8 : slot * 8 + 8, :] = jnp.broadcast_to(inverse, (8, N))
        for channel in range(CHANNELS):
            mine = slots[channel * PER : (channel + 1) * PER]
            where = [pl.ds(pl.multiple_of(slot * 8, 8), 8) for slot in mine]
            there = [pl.ds(pl.multiple_of(SLOTS * 8 + slot * 8, 8), 8) for slot in mine]
            inverse = [inv_ref[w, :] for w in where]
            h_re = [plane_ref[block, where[i], :N] * inverse[i] for i in range(PER)]
            h_im = [plane_ref[block, where[i], N:] * inverse[i] for i in range(PER)]
            s_re = [plane_ref[block, w, :N] for w in there]
            s_im = [plane_ref[block, w, N:] for w in there]
            num_re = num_im = 0.0
            den = regular_gamma
            for i in range(PER):
                num_re = num_re + (h_re[i] * s_re[i] + h_im[i] * s_im[i])
                num_im = num_im + (h_re[i] * s_im[i] - h_im[i] * s_re[i])
                den = den + (h_re[i] * h_re[i] + h_im[i] * h_im[i])
            recip = 1.0 / den
            o_re = num_re * recip
            o_im = num_im * recip
            rows = slice(channel * HALF + block * 8, channel * HALF + block * 8 + 8)
            object_ref[rows, :N] = o_re
            object_ref[rows, N:] = o_im
            scale = o_re * o_re + o_im * o_im
            for i in range(PER):
                g_re = scale * h_re[i] - (s_re[i] * o_re + s_im[i] * o_im)
                g_im = scale * h_im[i] - (s_im[i] * o_re - s_re[i] * o_im)
                match = g_re * h_re[i] + g_im * h_im[i]
                if block in (0, BLOCKS - 1):
                    match = match * weight_ref[block * 8 : block * 8 + 8, :]
                at = channel * PER + i
                inner_ref[at] = match if block == 0 else inner_ref[at] + match
                grad_ref[block, where[i], :N] = g_re
                grad_ref[block, where[i], N:] = g_im
    origin = (lax.broadcasted_iota(jnp.int32, (8, N), 0) == 0) & (
        lax.broadcasted_iota(jnp.int32, (8, N), 1) == 0
    )
    for at in range(SLOTS):
        total = jnp.sum(jnp.sum(inner_ref[at], axis=0, keepdims=True), axis=1, keepdims=True)
        w = pl.ds(pl.multiple_of(slots[at] * 8, 8), 8)
        grad_ref[0, w, :N] = grad_ref[0, w, :N] - jnp.where(origin, 2.0 * total, 0.0)
    high, low = split(object_ref[...] * (1.0 / (N * N)))
    z = dot(jnp.concatenate([high, low, high], axis=1), table_rows(rb_ref))
    image = dot(lb_ref[...], rows3(swap_halves(z, HALF)))
    width = width_ref[0].astype(f32) + 1.0
    row = lax.broadcasted_iota(jnp.int32, (N, N), 0)
    col = lax.broadcasted_iota(jnp.int32, (N, N), 1)

    def ramp(index):
        distance = (jnp.minimum(index, N - 1 - index) + 1).astype(f32)
        return jnp.minimum(1.0, distance / width)

    weight = ramp(row) * ramp(col)
    head_ref[CHANNELS] = weight[:MARGIN]
    tail_ref[CHANNELS] = weight[N - MARGIN :]
    canvas_ref[CHANNELS] = weight
    for channel in range(CHANNELS):
        shown = image[:, channel * N : (channel + 1) * N] * weight
        canvas_ref[channel] = shown
        turned = shown.T
        head_ref[channel] = turned[:MARGIN]
        tail_ref[channel] = turned[N - MARGIN :]


TABLES = ("right_pupil", "left_pupil", "left_half", "right_full", "right_back", "left_back")


def object_kernel(
    width_ref, chan_ref, data_ref, mask_ref, phase_ref, lt_ref, taper_ref, weight_ref,
    rp_hbm, lp_hbm, lh_hbm, rf_hbm, rb_hbm, lb_hbm,
    grad_ref, field_ref, slope_ref, inv_ref, canvas_ref, head_ref, tail_ref,
    rp_ref, lp_ref, lh_ref, rf_ref, rb_ref, lb_ref, sems,
    line_ref, wide_ref, ph_ref, pl_ref, half_re_ref, half_im_ref, power_ref, yh_ref, yl_ref,
    order_ref, plane_ref, object_ref, inner_ref,
):
    moves = (
        (rp_hbm, rp_ref), (lp_hbm, lp_ref), (lh_hbm, lh_ref),
        (rf_hbm, rf_ref), (rb_hbm, rb_ref), (lb_hbm, lb_ref),
    )
    copies = [
        pltpu.make_async_copy(source, target, sems.at[i])
        for i, (source, target) in enumerate(moves)
    ]
    for copy in copies:
        copy.start()

    def ready():
        for copy in copies:
            copy.wait()

    at = [jnp.int32(0), jnp.int32(PER)]
    for slot in range(SLOTS):
        first = chan_ref[slot] == 0
        order_ref[jnp.where(first, at[0], at[1])] = slot
        at = [jnp.where(first, at[0] + 1, at[0]), jnp.where(first, at[1], at[1] + 1)]
    left = lt_ref[...]
    taper = taper_ref[...]

    def spectra(pair):
        image = jnp.concatenate([data_ref[2 * pair, :N, :], data_ref[2 * pair + 1, :N, :]], axis=1)
        y = dot(left, jnp.concatenate([image, image], axis=0)) * taper
        store_blocked(y, pair, SLOTS * 8, yh_ref, yl_ref)

    transfer_part(
        data_ref, chan_ref, mask_ref, phase_ref, rp_ref, lp_ref, lh_ref, ready, spectra,
        field_ref, slope_ref,
        line_ref, wide_ref, ph_ref, pl_ref, half_re_ref, half_im_ref, power_ref, yh_ref, yl_ref,
    )
    object_part(
        width_ref, [order_ref[i] for i in range(SLOTS)], weight_ref, rf_ref, rb_ref, lb_ref,
        grad_ref, inv_ref, canvas_ref, head_ref, tail_ref,
        yh_ref, yl_ref, plane_ref, object_ref, inner_ref,
    )


def pack_kernel(coef_hbm, shift_hbm, pix_hbm, out_ref, coef_ref, shift_ref, sems):
    coef_copy = pltpu.make_async_copy(coef_hbm, coef_ref, sems.at[0])
    shift_copy = pltpu.make_async_copy(shift_hbm, shift_ref, sems.at[1])
    pix_copy = pltpu.make_async_copy(pix_hbm, out_ref.at[:, :N, :], sems.at[2])
    coef_copy.start()
    shift_copy.start()
    pix_copy.start()
    coef_copy.wait()
    shift_copy.wait()
    coef = jnp.concatenate([coef_ref[...], jnp.zeros((SLOTS, N - ZERN), f32)], axis=1)
    first = coef.astype(bf16).astype(f32)
    rest = coef - first
    second = rest.astype(bf16).astype(f32)
    third = rest - second
    shift = jnp.concatenate([shift_ref[...].astype(f32), jnp.zeros((6, SLOTS), f32)], axis=0)
    shift = jnp.concatenate([shift, jnp.zeros((8, N - SLOTS), f32)], axis=1)
    shift = jnp.concatenate([shift, jnp.zeros((N - 8, N), f32)], axis=0).T[:SLOTS]
    line = first + pltpu.roll(second, ZERN, 1) + pltpu.roll(third, 2 * ZERN, 1)
    line = line + pltpu.roll(shift, 3 * ZERN, 1)
    for slot in range(SLOTS):
        out_ref[slot, N:, :] = jnp.broadcast_to(line[slot : slot + 1], (8, N)).astype(bf16)
    pix_copy.wait()


def pack(coef, shift, pixels):
    return pl.pallas_call(
        pack_kernel,
        out_shape=jax.ShapeDtypeStruct((SLOTS, ROWS, N), bf16),
        in_specs=[HB] * 3,
        out_specs=VM,
        scratch_shapes=[
            pltpu.VMEM((SLOTS, ZERN), f32),
            pltpu.VMEM((2, SLOTS), jnp.int32),
            pltpu.SemaphoreType.DMA((3,)),
        ],
        name="pack",
        compiler_params=limit(4),
    )(*[pltpu.with_memory_space_constraint(x, pltpu.HBM) for x in (coef, shift, pixels)])


def fold_kernel(
    canvas_ref, left_ref, right_ref,
    middle_ref, head_ref, tail_ref,
):
    gap = jnp.zeros((TILE - 2 * MARGIN, N), f32)
    rest = jnp.zeros((N - TILE, N), f32)
    for layer in range(CHANNELS + 1):
        sides = jnp.concatenate([left_ref[layer], gap, right_ref[layer], rest], axis=0).T
        total = pltpu.roll(canvas_ref[layer], N - MARGIN, 1) + sides
        head_ref[layer] = total[:MARGIN]
        middle_ref[layer] = total[MARGIN : N - MARGIN]
        tail_ref[layer] = total[N - MARGIN :]


def blend_kernel(middle_ref, upper_ref, lower_ref, out_ref):
    def folded(layer):
        return jnp.concatenate(
            [
                middle_ref[layer, :MARGIN] + upper_ref[layer],
                middle_ref[layer, MARGIN : TILE - MARGIN],
                middle_ref[layer, TILE - MARGIN :] + lower_ref[layer],
            ],
            axis=0,
        )

    weight = folded(CHANNELS)
    for channel in range(CHANNELS):
        out_ref[channel] = (folded(channel) / weight)[:, :TILE]


def gradient_kernel(
    chan_ref, grad_ref, field_ref, slope_ref, inv_ref, phase_ref, rb_ref, lb_ref, rp_ref, lp_ref,
    sums_ref,
    out_ref,
    z_ref, back_ref, qh_ref, ql_ref, pupil_ref, total_ref,
):
    right = table_rows(rb_ref)
    for chunk in range(3):
        here = slice(chunk * 3, (chunk + 1) * 3)
        high, low = split(grad_ref[here].reshape(3 * SLOTS * 8, 2 * N))
        z = dot(jnp.concatenate([high, low, high], axis=1), right)
        z_ref[here] = z.reshape(3, SLOTS * 8, 2 * N)
    left = lb_ref[...]
    for pair in range(PAIRS):
        rows = []
        for part in range(2):
            lanes = slice(part * N, (part + 1) * N)
            for block in range(BLOCKS):
                at = pair * 16
                pieces = [z_ref[block, at + 8 * w : at + 8 * w + 8, lanes] for w in range(2)]
                rows.append(jnp.concatenate(pieces, axis=1))
        power = dot(left, rows3(jnp.concatenate(rows, axis=0)))
        field = field_ref[pair]
        high, low = split(jnp.concatenate([field[:N] * power, field[N:] * power], axis=0))
        back_ref[pair, : 2 * N] = high
        back_ref[pair, 2 * N :] = low
    left = table_lanes(rp_ref)
    for pair in range(PAIRS):
        high = back_ref[pair, : 2 * N]
        half = dot(left, jnp.concatenate([high, back_ref[pair, 2 * N :], high], axis=0))
        high, low = split(swap_halves(half, PUP))
        here = slice(pair * N, (pair + 1) * N)
        qh_ref[here, :] = high
        ql_ref[here, :] = low
    right = table_rows(lp_ref)
    for chunk in range(2):
        here = slice(chunk * 4 * N, (chunk + 1) * 4 * N)
        high = qh_ref[here, :]
        pupil_ref[here, :] = dot(jnp.concatenate([high, ql_ref[here, :], high], axis=1), right)
    left = sums_ref[...]
    for pair in range(PAIRS):
        both = []
        for which in range(2):
            slot = 2 * pair + which
            slope = slope_ref[pl.ds(slot, PUP, stride=SLOTS), :]
            both.append(pupil_ref[slot * PUP : (slot + 1) * PUP, :] * slope)
        out = dot(left, rows3(jnp.concatenate(both, axis=1)))
        for which in range(2):
            here = slice((2 * pair + which) * DEG_ROWS, (2 * pair + which + 1) * DEG_ROWS)
            total_ref[here, :] = out[:, which * N : (which + 1) * N]
    sums = [total_ref[pl.ds(i, SLOTS, stride=DEG_ROWS), :] for i in range(DEG)]
    total = lax.dot_general(
        jnp.concatenate(sums, axis=1), phase_ref[...], (((1,), (1,)), ((), ())),
        precision=lax.Precision.HIGHEST, preferred_element_type=f32,
    )
    factor = 8.0 * math.pi / float(N * N * N)
    inverse = inv_ref[pl.ds(0, SLOTS, stride=8), :]
    total = total * (slot_scales(chan_ref, COEF) * factor * inverse[:, :COEF])
    out_ref[...] = total[:, :ZERN]


def limit(mib):
    return pltpu.CompilerParams(vmem_limit_bytes=mib << 20)


def objects(width, chan, data, mask, tabs, interpret=False):
    margin = jax.ShapeDtypeStruct((CHANNELS + 1, MARGIN, N), f32)
    fixed = [tabs[name] for name in TABLES]
    return pl.pallas_call(
        object_kernel,
        out_shape=(
            jax.ShapeDtypeStruct((BLOCKS, SLOTS * 8, 2 * N), f32),
            jax.ShapeDtypeStruct((PAIRS, 2 * N, 2 * N), f32),
            jax.ShapeDtypeStruct((PUP * SLOTS, N), f32),
            jax.ShapeDtypeStruct((SLOTS * 8, N), f32),
            jax.ShapeDtypeStruct((CHANNELS + 1, N, N), f32),
            margin,
            margin,
        ),
        in_specs=[SM, SM] + [VM] * 6 + [HB] * len(TABLES),
        out_specs=(VM,) * 7,
        scratch_shapes=[pltpu.VMEM(table.shape, bf16) for table in fixed]
        + [
            pltpu.SemaphoreType.DMA((len(TABLES),)),
            pltpu.VMEM((SLOTS * 8, N), f32),
            pltpu.VMEM((PUP, N), f32),
            pltpu.VMEM((PUP * SLOTS, N), bf16),
            pltpu.VMEM((PUP * SLOTS, N), bf16),
            pltpu.VMEM((PUP * SLOTS, N), f32),
            pltpu.VMEM((PUP * SLOTS, N), f32),
            pltpu.VMEM((PAIRS, 2 * N, 2 * N), bf16),
            pltpu.VMEM((BLOCKS, SLOTS * 16, 2 * N), bf16),
            pltpu.VMEM((BLOCKS, SLOTS * 16, 2 * N), bf16),
            pltpu.SMEM((SLOTS,), jnp.int32),
            pltpu.VMEM((BLOCKS, SLOTS * 16, 2 * N), f32),
            pltpu.VMEM((TWO, 2 * N), f32),
            pltpu.VMEM((SLOTS, 8, N), f32),
        ],
        interpret=interpret,
        name="objects",
        compiler_params=limit(16),
    )(
        width, chan, data, mask, tabs["phase"], tabs["left_taper"], tabs["taper"], tabs["weight"],
        *fixed,
    )


def gradient(chan, grad, field, slope, inverse, tabs, interpret=False):
    return pl.pallas_call(
        gradient_kernel,
        out_shape=jax.ShapeDtypeStruct((SLOTS, ZERN), f32),
        in_specs=[SM] + [VM] * 10,
        out_specs=VM,
        scratch_shapes=[
            pltpu.VMEM((BLOCKS, SLOTS * 8, 2 * N), f32),
            pltpu.VMEM((PAIRS, 4 * N, 2 * N), bf16),
            pltpu.VMEM((SLOTS * PUP, 2 * N), bf16),
            pltpu.VMEM((SLOTS * PUP, 2 * N), bf16),
            pltpu.VMEM((SLOTS * PUP, N), f32),
            pltpu.VMEM((SLOTS * DEG_ROWS, N), f32),
        ],
        interpret=interpret,
        name="gradient",
        compiler_params=limit(16),
    )(
        chan, grad, field, slope, inverse, tabs["phase"], tabs["right_back"], tabs["left_back"],
        tabs["right_pupil"], tabs["left_pupil"], tabs["sums"],
    )


def fold(canvas, left, right):
    margin = jax.ShapeDtypeStruct((CHANNELS + 1, MARGIN, N), f32)
    return pl.pallas_call(
        fold_kernel,
        out_shape=(
            jax.ShapeDtypeStruct((CHANNELS + 1, TILE, N), f32),
            margin,
            margin,
        ),
        in_specs=[VM] * 3,
        out_specs=(VM,) * 3,
        name="fold",
        compiler_params=limit(8),
    )(canvas, left, right)


def blend(middle, upper, lower):
    return pl.pallas_call(
        blend_kernel,
        out_shape=jax.ShapeDtypeStruct((CHANNELS, TILE, TILE), f32),
        in_specs=[VM] * 3,
        out_specs=VM,
        name="blend",
        compiler_params=limit(8),
    )(middle, upper, lower)


def shifted(cells, axis, forward):
    ends = lax.axis_size(axis) - 1
    if forward:
        return lax.ppermute(cells, axis, [(i, i + 1) for i in range(ends)])
    return lax.ppermute(cells, axis, [(i + 1, i) for i in range(ends)])


def per_device(coeffs, shifts, pixels, pupil_mask, chan_map, intersection):
    tabs = {name: jnp.asarray(table) for name, table in tables()[0].items()}
    coef = coeffs.reshape(SLOTS, ZERN)
    shift = shifts.reshape(SLOTS, 2).T
    data = pack(coef, shift, pixels.reshape(SLOTS, N, N)).reshape(1, SLOTS, 1, ROWS, N)
    data = lax.all_to_all(data, "patch", split_axis=1, concat_axis=0, tiled=True)
    grad, field, slope, inverse, canvas, head, tail = objects(
        intersection.reshape(1), chan_map, data.reshape(SLOTS, ROWS, N), pupil_mask, tabs
    )
    left = shifted(tail, "frame", True)
    right = shifted(head, "frame", False)
    grad = gradient(chan_map, grad, field, slope, inverse, tabs)
    grad = lax.all_to_all(
        grad.reshape(SLOTS, 1, 1, ZERN), "patch", split_axis=0, concat_axis=1, tiled=True
    )
    middle, head, tail = fold(canvas, left, right)
    upper = shifted(tail, "patch", True)
    lower = shifted(head, "patch", False)
    blended = blend(middle, upper, lower)
    return (blended, grad)


def solution(mesh):
    in_specs = (
        P("patch", None, "frame", None),
        P("patch", None, "frame", None),
        P("patch", None, "frame", None, None),
        P(),
        P(),
        P("patch", "frame"),
    )
    out_specs = (P(None, "patch", "frame"), P("patch", None, "frame", None))
    return jax.shard_map(
        per_device, mesh=mesh, in_specs=in_specs, out_specs=out_specs, check_vma=False
    )
```

```python
import functools
import math

import jax
import jax.numpy as jnp
import ml_dtypes
import numpy as np
from jax import lax
from jax.experimental import pallas as pl
from jax.experimental.pallas import tpu as pltpu
from jax.sharding import PartitionSpec as P


N = 128
PUP = 64
ZERN = 36
SLOTS = 16
PAIRS = SLOTS // 2
CHANNELS = 2
PER = SLOTS // CHANNELS
MARGIN = 16
DEPTH = 8
TILE = N - 2 * MARGIN
HALF = 72
TWO = 2 * HALF
DEG = 9
DEG_ROWS = 16
BLOCKS = HALF // 8
COEF = 40
ROWS = N + 8
regular_gamma = 0.1
wave_ratio = 0.35
f32 = jnp.float32
bf16 = jnp.bfloat16
VM = pl.BlockSpec(memory_space=pltpu.VMEM)
SM = pl.BlockSpec(memory_space=pltpu.SMEM)
HB = pl.BlockSpec(memory_space=pltpu.HBM)


def noll_order(noll_index):
    radial = 0
    remain = noll_index - 1
    while remain > radial:
        radial += 1
        remain -= radial
    azimuth = radial % 2 + 2 * ((remain + (radial + 1) % 2) // 2)
    if noll_index % 2 == 1:
        azimuth = -azimuth
    return (radial, azimuth)


def zernike_modes():
    position = (np.arange(PUP) - (PUP - 1) / 2.0) / (PUP / 2.0)
    grid_y, grid_x = np.meshgrid(position, position, indexing="ij")
    radius = np.sqrt(grid_x * grid_x + grid_y * grid_y)
    theta = np.arctan2(grid_y, grid_x)
    modes = []
    for noll_index in range(2, ZERN + 2):
        radial, azimuth = noll_order(noll_index)
        order = abs(azimuth)
        total = np.zeros_like(radius)
        for step in range((radial - order) // 2 + 1):
            factor = math.factorial(radial - step) / (
                math.factorial(step)
                * math.factorial((radial + order) // 2 - step)
                * math.factorial((radial - order) // 2 - step)
            )
            total = total + (-1) ** step * factor * radius ** (radial - 2 * step)
        if azimuth == 0:
            modes.append(total * math.sqrt(radial + 1.0))
        elif azimuth > 0:
            modes.append(total * math.sqrt(2.0 * (radial + 1.0)) * np.cos(order * theta))
        else:
            modes.append(total * math.sqrt(2.0 * (radial + 1.0)) * np.sin(order * theta))
    return position, np.stack(modes)


def halves(table):
    high = table.astype(ml_dtypes.bfloat16)
    low = (table - high.astype(np.float64)).astype(ml_dtypes.bfloat16)
    return high, low


def pair_table(table):
    return np.stack(halves(table))


@functools.cache
def tables():
    index = np.arange(N)
    turns = 2.0 * np.pi / N * (np.outer(index, index) % N)
    c, s = np.cos(turns), np.sin(turns)
    cp, sp = c[:, :PUP], s[:, :PUP]
    ch, sh = c[:HALF], s[:HALF]
    distance = np.minimum(index, N - 1 - index)
    taper = np.where(distance < MARGIN, 0.5 - 0.5 * np.cos(np.pi * (distance + 0.5) / MARGIN), 1.0)
    weight = np.where(np.arange(HALF) < 1, 1.0, 2.0)
    weight[N // 2] = 1.0
    weight[N // 2 + 1 :] = 0.0
    out = {}
    out["right_pupil"] = pair_table(np.block([[cp.T, -sp.T], [sp.T, cp.T]]))
    out["left_pupil"] = pair_table(np.block([[cp, sp], [-sp, cp]]))
    out["left_half"] = pair_table(np.block([[ch], [-sh]]))
    out["right_full"] = pair_table(np.block([[c, -s], [s, c]]))
    out["right_back"] = pair_table(np.block([[c, s], [-s, c]]))
    high, low = halves(np.block([[ch], [-sh]]) * taper[None, :])
    out["left_taper"] = np.concatenate([high, low], axis=1)
    high, low = halves(np.concatenate([weight[None] * ch.T, -weight[None] * sh.T], axis=1))
    out["left_back"] = np.concatenate([high, high, low], axis=1)
    out["taper"] = np.tile(taper, 2)[None].astype(np.float32)
    out["weight"] = np.broadcast_to(weight[:, None] / 2.0, (HALF, N)).astype(np.float32)
    position, modes = zernike_modes()
    cheb = np.polynomial.chebyshev.chebvander(position, DEG - 1)
    fit = np.linalg.lstsq(cheb, modes.transpose(1, 0, 2).reshape(PUP, -1), rcond=None)[0]
    fit = fit.reshape(DEG, ZERN, PUP).transpose(1, 0, 2)
    phase = np.zeros((COEF, DEG, PUP))
    phase[:ZERN] = fit
    step = 2.0 * np.pi / N * (PUP / 2.0)
    phase[ZERN, 1] = step
    phase[ZERN + 1, 0] = step * position
    phase = np.concatenate([phase, phase], axis=2)
    out["phase"] = (phase / (2.0 * np.pi)).reshape(COEF, DEG * N).astype(np.float32)
    spread = np.zeros((DEG_ROWS, PUP))
    spread[:DEG] = cheb.T
    high, low = halves(spread)
    out["sums"] = np.concatenate([high, high, low], axis=1)
    return out, cheb


def split(x):
    high = x.astype(bf16)
    return high, (x - high.astype(f32)).astype(bf16)


def dot(left, right):
    return lax.dot_general(left, right, (((1,), (0,)), ((), ())), preferred_element_type=f32)


def rows3(x):
    high, low = split(x)
    return jnp.concatenate([high, low, high], axis=0)


def table_rows(ref):
    return jnp.concatenate([ref[0], ref[0], ref[1]], axis=0)


def table_lanes(ref):
    return jnp.concatenate([ref[0], ref[0], ref[1]], axis=1)


def swap_halves(y, count):
    top = jnp.concatenate([y[:count, :N], y[count:, :N]], axis=1)
    low = jnp.concatenate([y[:count, N:], y[count:, N:]], axis=1)
    return jnp.concatenate([top, low], axis=0)


SINE = (3.141592616, -5.167708583, 2.55005456, -0.5981644139, 0.07742681132)
COSINE = (0.9999999532, -4.934792831, 4.058411353, -1.331876568, 0.2196896111)


def blocked(y):
    pieces = []
    for block in range(BLOCKS):
        rows = slice(block * 8, block * 8 + 8)
        im_rows = slice(HALF + block * 8, HALF + block * 8 + 8)
        for which in range(2):
            lanes = slice(which * N, (which + 1) * N)
            pieces.append(jnp.concatenate([y[rows, lanes], y[im_rows, lanes]], axis=1))
    return jnp.concatenate(pieces, axis=0)


def store_blocked(y, pair, base, yh_ref, yl_ref):
    high, low = split(blocked(y))
    rows = slice(base + pair * 16, base + pair * 16 + 16)
    for block in range(BLOCKS):
        yh_ref[block, rows, :] = high[block * 16 : block * 16 + 16]
        yl_ref[block, rows, :] = low[block * 16 : block * 16 + 16]


def chebyshev_sum(parts, cheb, row):
    total = parts[0]
    for i in range(1, DEG):
        total = total + float(cheb[row, i]) * parts[i]
    return total


def series(factors, square):
    total = factors[-1] * square + factors[-2]
    for factor in factors[-3::-1]:
        total = total * square + factor
    return total


def turned(turns):
    rest = turns - jnp.round(turns)
    square = rest * rest
    sine = rest * series(SINE, square)
    twice = sine + sine
    return 1.0 - twice * sine, twice * series(COSINE, square)


def slot_scales(chan_ref, width):
    row = lax.broadcasted_iota(jnp.int32, (SLOTS, width), 0)
    channel = jnp.zeros((SLOTS, width), jnp.int32)
    for slot in range(SLOTS):
        channel = jnp.where(row == slot, chan_ref[slot], channel)
    return 1.0 / (1.0 + wave_ratio * channel.astype(f32))


def transfer_part(
    data_ref, chan_ref, mask_ref, phase_ref, rp_ref, lp_ref, lh_ref, ready, spectra,
    field_ref, slope_ref,
    line_ref, wide_ref, ph_ref, pl_ref, half_re_ref, half_im_ref, power_ref, yh_ref, yl_ref,
):
    cheb = tables()[1]
    for slot in range(SLOTS):
        line_ref[slot * 8 : slot * 8 + 8, :] = data_ref[slot, N:, :].astype(f32)
    line = line_ref[pl.ds(0, SLOTS, stride=8), :]
    coef = line + (pltpu.roll(line, N - ZERN, 1) + pltpu.roll(line, N - 2 * ZERN, 1))
    lane = lax.broadcasted_iota(jnp.int32, (SLOTS, N), 1)
    shift = pltpu.roll(line, N - 2 * ZERN, 1)
    coef = jnp.where(lane < ZERN, coef * slot_scales(chan_ref, N), shift)[:, :COEF]
    mask = mask_ref[...].astype(f32)
    wide_ref[...] = jnp.concatenate([mask, mask], axis=1)
    parts_all = lax.dot_general(
        coef, phase_ref[...], (((1,), (0,)), ((), ())),
        precision=lax.Precision.HIGHEST, preferred_element_type=f32,
    )
    first = lax.broadcasted_iota(jnp.int32, (SLOTS, N), 1) < PUP
    sign = jnp.where(first, 1.0, -1.0)
    parts = [parts_all[:, i * N : (i + 1) * N] for i in range(DEG)]
    parts = [part * sign if i % 2 else part for i, part in enumerate(parts)]
    for row in range(PUP // 2):
        if row % 4 == 0:
            spectra(row // 4)
        far = PUP - 1 - row
        cosine, sine = turned(chebyshev_sum(parts, cheb, row))
        mask = jnp.where(first, wide_ref[row : row + 1, :], wide_ref[far : far + 1, :])
        cosine = cosine * mask
        sine = sine * mask
        far_cosine = pltpu.roll(cosine, PUP, 1)
        far_sine = pltpu.roll(sine, PUP, 1)
        here = slice(row * SLOTS, (row + 1) * SLOTS)
        there = slice(far * SLOTS, (far + 1) * SLOTS)
        slope_ref[here, :] = jnp.where(first, -sine, far_cosine)
        slope_ref[there, :] = jnp.where(first, -far_sine, cosine)
        high, low = split(jnp.where(first, cosine, far_sine))
        ph_ref[here, :] = high
        pl_ref[here, :] = low
        high, low = split(jnp.where(first, far_cosine, sine))
        ph_ref[there, :] = high
        pl_ref[there, :] = low
    ready()
    right = table_rows(rp_ref)
    for chunk in range(2):
        here = slice(chunk * 512, (chunk + 1) * 512)
        high = ph_ref[here, :]
        half = dot(jnp.concatenate([high, pl_ref[here, :], high], axis=1), right)
        half_re_ref[here, :] = half[:, :N]
        half_im_ref[here, :] = half[:, N:]
    left = table_lanes(lp_ref)
    for pair in range(PAIRS):
        columns = []
        for part_ref in (half_re_ref, half_im_ref):
            columns.append(
                jnp.concatenate(
                    [part_ref[pl.ds(2 * pair + which, PUP, stride=SLOTS), :] for which in range(2)],
                    axis=1,
                )
            )
        field = dot(left, rows3(jnp.concatenate(columns, axis=0)))
        field_ref[pair] = field
        high, low = split(field[:N] * field[:N] + field[N:] * field[N:])
        power_ref[pair, :N] = high
        power_ref[pair, N:] = low
    left = table_lanes(lh_ref)
    for pair in range(PAIRS):
        high = power_ref[pair, :N]
        y = dot(left, jnp.concatenate([high, power_ref[pair, N:], high], axis=0))
        store_blocked(y, pair, 0, yh_ref, yl_ref)


def object_part(
    width_ref, slots, weight_ref, rf_ref, rb_ref, lb_ref,
    grad_ref, inv_ref, canvas_ref, head_ref, tail_ref,
    yh_ref, yl_ref, plane_ref, object_ref, inner_ref,
):
    right = table_rows(rf_ref)
    for block in range(BLOCKS):
        high = yh_ref[block]
        plane_ref[block] = dot(jnp.concatenate([high, yl_ref[block], high], axis=1), right)
        if block == 0:
            for slot in range(SLOTS):
                inverse = 1.0 / plane_ref[0, slot * 8 : slot * 8 + 1, 0:1]
                inv_ref[slot * 8 : slot * 8 + 8, :] = jnp.broadcast_to(inverse, (8, N))
        for channel in range(CHANNELS):
            mine = slots[channel * PER : (channel + 1) * PER]
            where = [pl.ds(pl.multiple_of(slot * 8, 8), 8) for slot in mine]
            there = [pl.ds(pl.multiple_of(SLOTS * 8 + slot * 8, 8), 8) for slot in mine]
            inverse = [inv_ref[w, :] for w in where]
            h_re = [plane_ref[block, where[i], :N] * inverse[i] for i in range(PER)]
            h_im = [plane_ref[block, where[i], N:] * inverse[i] for i in range(PER)]
            s_re = [plane_ref[block, w, :N] for w in there]
            s_im = [plane_ref[block, w, N:] for w in there]
            num_re = num_im = 0.0
            den = regular_gamma
            for i in range(PER):
                num_re = num_re + (h_re[i] * s_re[i] + h_im[i] * s_im[i])
                num_im = num_im + (h_re[i] * s_im[i] - h_im[i] * s_re[i])
                den = den + (h_re[i] * h_re[i] + h_im[i] * h_im[i])
            recip = 1.0 / den
            o_re = num_re * recip
            o_im = num_im * recip
            rows = slice(channel * HALF + block * 8, channel * HALF + block * 8 + 8)
            object_ref[rows, :N] = o_re
            object_ref[rows, N:] = o_im
            scale = o_re * o_re + o_im * o_im
            for i in range(PER):
                g_re = scale * h_re[i] - (s_re[i] * o_re + s_im[i] * o_im)
                g_im = scale * h_im[i] - (s_im[i] * o_re - s_re[i] * o_im)
                match = g_re * h_re[i] + g_im * h_im[i]
                if block in (0, BLOCKS - 1):
                    match = match * weight_ref[block * 8 : block * 8 + 8, :]
                at = channel * PER + i
                inner_ref[at] = match if block == 0 else inner_ref[at] + match
                grad_ref[block, where[i], :N] = g_re
                grad_ref[block, where[i], N:] = g_im
    origin = (lax.broadcasted_iota(jnp.int32, (8, N), 0) == 0) & (
        lax.broadcasted_iota(jnp.int32, (8, N), 1) == 0
    )
    for at in range(SLOTS):
        total = jnp.sum(jnp.sum(inner_ref[at], axis=0, keepdims=True), axis=1, keepdims=True)
        w = pl.ds(pl.multiple_of(slots[at] * 8, 8), 8)
        grad_ref[0, w, :N] = grad_ref[0, w, :N] - jnp.where(origin, 2.0 * total, 0.0)
    high, low = split(object_ref[...] * (1.0 / (N * N)))
    z = dot(jnp.concatenate([high, low, high], axis=1), table_rows(rb_ref))
    image = dot(lb_ref[...], rows3(swap_halves(z, HALF)))
    width = width_ref[0].astype(f32) + 1.0
    row = lax.broadcasted_iota(jnp.int32, (N, N), 0)
    col = lax.broadcasted_iota(jnp.int32, (N, N), 1)

    def ramp(index):
        distance = (jnp.minimum(index, N - 1 - index) + 1).astype(f32)
        return jnp.minimum(1.0, distance / width)

    weight = ramp(row) * ramp(col)
    head_ref[CHANNELS] = weight[:MARGIN]
    tail_ref[CHANNELS] = weight[N - MARGIN :]
    canvas_ref[CHANNELS] = weight
    for channel in range(CHANNELS):
        shown = image[:, channel * N : (channel + 1) * N] * weight
        canvas_ref[channel] = shown
        turned = shown.T
        head_ref[channel] = turned[:MARGIN]
        tail_ref[channel] = turned[N - MARGIN :]


TABLES = ("right_pupil", "left_pupil", "left_half", "right_full", "right_back", "left_back")


def object_kernel(
    width_ref, early_ref, chan_ref, data_ref, mask_ref, phase_ref, lt_ref, taper_ref, weight_ref,
    sums_ref, rp_hbm, lp_hbm, lh_hbm, rf_hbm, rb_hbm, lb_hbm,
    grad_ref, field_ref, slope_ref, inv_ref, canvas_ref, head_ref, tail_ref, done_ref,
    rp_ref, lp_ref, lh_ref, rf_ref, rb_ref, lb_ref, sems,
    line_ref, wide_ref, ph_ref, pl_ref, half_re_ref, half_im_ref, power_ref, yh_ref, yl_ref,
    order_ref, plane_ref, object_ref, inner_ref, *scratch,
):
    moves = (
        (rp_hbm, rp_ref), (lp_hbm, lp_ref), (lh_hbm, lh_ref),
        (rf_hbm, rf_ref), (rb_hbm, rb_ref), (lb_hbm, lb_ref),
    )
    copies = [
        pltpu.make_async_copy(source, target, sems.at[i])
        for i, (source, target) in enumerate(moves)
    ]
    for copy in copies:
        copy.start()

    def ready():
        for copy in copies:
            copy.wait()

    at = [jnp.int32(0), jnp.int32(PER)]
    for slot in range(SLOTS):
        first = chan_ref[slot] == 0
        order_ref[jnp.where(first, at[0], at[1])] = slot
        at = [jnp.where(first, at[0] + 1, at[0]), jnp.where(first, at[1], at[1] + 1)]
    left = lt_ref[...]
    taper = taper_ref[...]

    def spectra(pair):
        image = jnp.concatenate([data_ref[2 * pair, :N, :], data_ref[2 * pair + 1, :N, :]], axis=1)
        y = dot(left, jnp.concatenate([image, image], axis=0)) * taper
        store_blocked(y, pair, SLOTS * 8, yh_ref, yl_ref)

    transfer_part(
        data_ref, chan_ref, mask_ref, phase_ref, rp_ref, lp_ref, lh_ref, ready, spectra,
        field_ref, slope_ref,
        line_ref, wide_ref, ph_ref, pl_ref, half_re_ref, half_im_ref, power_ref, yh_ref, yl_ref,
    )
    object_part(
        width_ref, [order_ref[i] for i in range(SLOTS)], weight_ref, rf_ref, rb_ref, lb_ref,
        grad_ref, inv_ref, canvas_ref, head_ref, tail_ref,
        yh_ref, yl_ref, plane_ref, object_ref, inner_ref,
    )
    done_ref[...] = jnp.zeros_like(done_ref)

    @pl.when(early_ref[0] == 1)
    def _():
        gradient_part(
            chan_ref, grad_ref, field_ref, slope_ref, inv_ref, phase_ref,
            rb_ref, lb_ref, rp_ref, lp_ref, sums_ref, done_ref, *scratch,
        )


def pack_kernel(coef_hbm, shift_hbm, pix_hbm, out_hbm, coef_ref, shift_ref, data_ref, sems):
    coef_copy = pltpu.make_async_copy(coef_hbm, coef_ref, sems.at[0])
    shift_copy = pltpu.make_async_copy(shift_hbm, shift_ref, sems.at[1])
    chunks = [pl.ds(i * 4, 4) for i in range(4)]
    loads = [
        pltpu.make_async_copy(pix_hbm.at[c], data_ref.at[c, :N, :], sems.at[2 + i])
        for i, c in enumerate(chunks)
    ]
    stores = [
        pltpu.make_async_copy(data_ref.at[c], out_hbm.at[c], sems.at[6 + i])
        for i, c in enumerate(chunks)
    ]
    coef_copy.start()
    shift_copy.start()
    for load in loads:
        load.start()
    coef_copy.wait()
    shift_copy.wait()
    coef = jnp.concatenate([coef_ref[...], jnp.zeros((SLOTS, N - ZERN), f32)], axis=1)
    first = coef.astype(bf16).astype(f32)
    rest = coef - first
    second = rest.astype(bf16).astype(f32)
    third = rest - second
    shift = jnp.concatenate([shift_ref[...].astype(f32), jnp.zeros((6, SLOTS), f32)], axis=0)
    shift = jnp.concatenate([shift, jnp.zeros((8, N - SLOTS), f32)], axis=1)
    shift = jnp.concatenate([shift, jnp.zeros((N - 8, N), f32)], axis=0).T[:SLOTS]
    line = first + pltpu.roll(second, ZERN, 1) + pltpu.roll(third, 2 * ZERN, 1)
    line = line + pltpu.roll(shift, 3 * ZERN, 1)
    for slot in range(SLOTS):
        data_ref[slot, N:, :] = jnp.broadcast_to(line[slot : slot + 1], (8, N)).astype(bf16)
    for load, store in zip(loads, stores):
        load.wait()
        store.start()
    for store in stores:
        store.wait()


def pack(coef, shift, pixels):
    return pl.pallas_call(
        pack_kernel,
        out_shape=jax.ShapeDtypeStruct((SLOTS, ROWS, N), bf16),
        in_specs=[HB] * 3,
        out_specs=HB,
        scratch_shapes=[
            pltpu.VMEM((SLOTS, ZERN), f32),
            pltpu.VMEM((2, SLOTS), jnp.int32),
            pltpu.VMEM((SLOTS, ROWS, N), bf16),
            pltpu.SemaphoreType.DMA((10,)),
        ],
        name="pack",
        compiler_params=limit(4),
    )(*[pltpu.with_memory_space_constraint(x, pltpu.HBM) for x in (coef, shift, pixels)])


def fold_kernel(
    canvas_ref, left_ref, right_ref,
    middle_ref, head_ref, tail_ref,
):
    gap = jnp.zeros((TILE - 2 * MARGIN, N), f32)
    rest = jnp.zeros((N - TILE, N), f32)
    for layer in range(CHANNELS + 1):
        sides = jnp.concatenate([left_ref[layer], gap, right_ref[layer], rest], axis=0).T
        total = pltpu.roll(canvas_ref[layer], N - MARGIN, 1) + sides
        head_ref[layer] = total[:MARGIN]
        middle_ref[layer] = total[MARGIN : N - MARGIN]
        tail_ref[layer] = total[N - MARGIN :]


def blend_kernel(middle_ref, upper_ref, lower_ref, grad_ref, out_ref, slope_ref):
    slope_ref[...] = grad_ref[...]

    def folded(layer):
        return jnp.concatenate(
            [
                middle_ref[layer, :MARGIN] + upper_ref[layer],
                middle_ref[layer, MARGIN : TILE - MARGIN],
                middle_ref[layer, TILE - MARGIN :] + lower_ref[layer],
            ],
            axis=0,
        )

    weight = folded(CHANNELS)
    for channel in range(CHANNELS):
        out_ref[channel] = (folded(channel) / weight)[:, :TILE]


def gradient_part(
    chan_ref, grad_ref, field_ref, slope_ref, inv_ref, phase_ref, rb_ref, lb_ref, rp_ref, lp_ref,
    sums_ref,
    out_ref,
    z_ref, back_ref, qh_ref, ql_ref, pupil_ref, total_ref,
):
    right = table_rows(rb_ref)
    for chunk in range(3):
        here = slice(chunk * 3, (chunk + 1) * 3)
        high, low = split(grad_ref[here].reshape(3 * SLOTS * 8, 2 * N))
        z = dot(jnp.concatenate([high, low, high], axis=1), right)
        z_ref[here] = z.reshape(3, SLOTS * 8, 2 * N)
    left = lb_ref[...]
    for pair in range(PAIRS):
        rows = []
        for part in range(2):
            lanes = slice(part * N, (part + 1) * N)
            for block in range(BLOCKS):
                at = pair * 16
                pieces = [z_ref[block, at + 8 * w : at + 8 * w + 8, lanes] for w in range(2)]
                rows.append(jnp.concatenate(pieces, axis=1))
        power = dot(left, rows3(jnp.concatenate(rows, axis=0)))
        field = field_ref[pair]
        high, low = split(jnp.concatenate([field[:N] * power, field[N:] * power], axis=0))
        back_ref[pair, : 2 * N] = high
        back_ref[pair, 2 * N :] = low
    left = table_lanes(rp_ref)
    for pair in range(PAIRS):
        high = back_ref[pair, : 2 * N]
        half = dot(left, jnp.concatenate([high, back_ref[pair, 2 * N :], high], axis=0))
        high, low = split(swap_halves(half, PUP))
        here = slice(pair * N, (pair + 1) * N)
        qh_ref[here, :] = high
        ql_ref[here, :] = low
    right = table_rows(lp_ref)
    for chunk in range(2):
        here = slice(chunk * 4 * N, (chunk + 1) * 4 * N)
        high = qh_ref[here, :]
        pupil_ref[here, :] = dot(jnp.concatenate([high, ql_ref[here, :], high], axis=1), right)
    left = sums_ref[...]
    for pair in range(PAIRS):
        both = []
        for which in range(2):
            slot = 2 * pair + which
            slope = slope_ref[pl.ds(slot, PUP, stride=SLOTS), :]
            both.append(pupil_ref[slot * PUP : (slot + 1) * PUP, :] * slope)
        out = dot(left, rows3(jnp.concatenate(both, axis=1)))
        for which in range(2):
            here = slice((2 * pair + which) * DEG_ROWS, (2 * pair + which + 1) * DEG_ROWS)
            total_ref[here, :] = out[:, which * N : (which + 1) * N]
    sums = [total_ref[pl.ds(i, SLOTS, stride=DEG_ROWS), :] for i in range(DEG)]
    total = lax.dot_general(
        jnp.concatenate(sums, axis=1), phase_ref[...], (((1,), (1,)), ((), ())),
        precision=lax.Precision.HIGHEST, preferred_element_type=f32,
    )
    factor = 8.0 * math.pi / float(N * N * N)
    inverse = inv_ref[pl.ds(0, SLOTS, stride=8), :]
    total = total * (slot_scales(chan_ref, COEF) * factor * inverse[:, :COEF])
    out_ref[...] = total[:, :ZERN]


def gradient_kernel(
    early_ref, chan_ref, done_ref, grad_ref, field_ref, slope_ref, inv_ref, phase_ref,
    rb_ref, lb_ref, rp_ref, lp_ref, sums_ref,
    out_ref,
    *scratch,
):
    @pl.when(early_ref[0] == 1)
    def _():
        out_ref[...] = done_ref[...]

    @pl.when(early_ref[0] == 0)
    def _():
        gradient_part(
            chan_ref, grad_ref, field_ref, slope_ref, inv_ref, phase_ref,
            rb_ref, lb_ref, rp_ref, lp_ref, sums_ref, out_ref, *scratch,
        )


GRADIENT_SCRATCH = (
    ((BLOCKS, SLOTS * 8, 2 * N), f32),
    ((PAIRS, 4 * N, 2 * N), bf16),
    ((SLOTS * PUP, 2 * N), bf16),
    ((SLOTS * PUP, 2 * N), bf16),
    ((SLOTS * PUP, N), f32),
    ((SLOTS * DEG_ROWS, N), f32),
)


def limit(mib):
    return pltpu.CompilerParams(vmem_limit_bytes=mib << 20)


def objects(width, early, chan, data, mask, tabs, interpret=False):
    margin = jax.ShapeDtypeStruct((CHANNELS + 1, MARGIN, N), f32)
    fixed = [tabs[name] for name in TABLES]
    return pl.pallas_call(
        object_kernel,
        out_shape=(
            jax.ShapeDtypeStruct((BLOCKS, SLOTS * 8, 2 * N), f32),
            jax.ShapeDtypeStruct((PAIRS, 2 * N, 2 * N), f32),
            jax.ShapeDtypeStruct((PUP * SLOTS, N), f32),
            jax.ShapeDtypeStruct((SLOTS * 8, N), f32),
            jax.ShapeDtypeStruct((CHANNELS + 1, N, N), f32),
            margin,
            margin,
            jax.ShapeDtypeStruct((SLOTS, ZERN), f32),
        ),
        in_specs=[SM] * 3 + [VM] * 7 + [HB] * len(TABLES),
        out_specs=(VM,) * 8,
        scratch_shapes=[pltpu.VMEM(table.shape, bf16) for table in fixed]
        + [
            pltpu.SemaphoreType.DMA((len(TABLES),)),
            pltpu.VMEM((SLOTS * 8, N), f32),
            pltpu.VMEM((PUP, N), f32),
            pltpu.VMEM((PUP * SLOTS, N), bf16),
            pltpu.VMEM((PUP * SLOTS, N), bf16),
            pltpu.VMEM((PUP * SLOTS, N), f32),
            pltpu.VMEM((PUP * SLOTS, N), f32),
            pltpu.VMEM((PAIRS, 2 * N, 2 * N), bf16),
            pltpu.VMEM((BLOCKS, SLOTS * 16, 2 * N), bf16),
            pltpu.VMEM((BLOCKS, SLOTS * 16, 2 * N), bf16),
            pltpu.SMEM((SLOTS,), jnp.int32),
            pltpu.VMEM((BLOCKS, SLOTS * 16, 2 * N), f32),
            pltpu.VMEM((TWO, 2 * N), f32),
            pltpu.VMEM((SLOTS, 8, N), f32),
        ]
        + [pltpu.VMEM(*piece) for piece in GRADIENT_SCRATCH],
        interpret=interpret,
        name="objects",
        compiler_params=limit(22),
    )(
        width, early, chan, data, mask, tabs["phase"], tabs["left_taper"], tabs["taper"],
        tabs["weight"], tabs["sums"], *fixed,
    )


def gradient(early, chan, done, grad, field, slope, inverse, tabs, interpret=False):
    return pl.pallas_call(
        gradient_kernel,
        out_shape=jax.ShapeDtypeStruct((SLOTS, ZERN), f32),
        in_specs=[SM, SM] + [VM] * 11,
        out_specs=VM,
        scratch_shapes=[pltpu.VMEM(*piece) for piece in GRADIENT_SCRATCH],
        interpret=interpret,
        name="gradient",
        compiler_params=limit(16),
    )(
        early, chan, done, grad, field, slope, inverse, tabs["phase"], tabs["right_back"],
        tabs["left_back"], tabs["right_pupil"], tabs["left_pupil"], tabs["sums"],
    )


def fold(canvas, left, right):
    margin = jax.ShapeDtypeStruct((CHANNELS + 1, MARGIN, N), f32)
    return pl.pallas_call(
        fold_kernel,
        out_shape=(
            jax.ShapeDtypeStruct((CHANNELS + 1, TILE, N), f32),
            margin,
            margin,
        ),
        in_specs=[VM] * 3,
        out_specs=(VM,) * 3,
        name="fold",
        compiler_params=limit(8),
    )(canvas, left, right)


def blend(middle, upper, lower, grad):
    return pl.pallas_call(
        blend_kernel,
        out_shape=(
            jax.ShapeDtypeStruct((CHANNELS, TILE, TILE), f32),
            jax.ShapeDtypeStruct((SLOTS, ZERN), f32),
        ),
        in_specs=[VM] * 4,
        out_specs=(VM,) * 2,
        name="blend",
        compiler_params=limit(8),
    )(middle, upper, lower, grad)


def shifted(cells, axis, forward):
    ends = lax.axis_size(axis) - 1
    if forward:
        return lax.ppermute(cells, axis, [(i, i + 1) for i in range(ends)])
    return lax.ppermute(cells, axis, [(i + 1, i) for i in range(ends)])


def per_device(coeffs, shifts, pixels, pupil_mask, chan_map, intersection):
    tabs = {name: jnp.asarray(table) for name, table in tables()[0].items()}
    coef = coeffs.reshape(SLOTS, ZERN)
    shift = shifts.reshape(SLOTS, 2).T
    data = pack(coef, shift, pixels.reshape(SLOTS, N, N)).reshape(1, SLOTS, 1, ROWS, N)
    data = lax.all_to_all(data, "patch", split_axis=1, concat_axis=0, tiled=True)
    early = ((lax.axis_index("frame") % DEPTH) == 0).astype(jnp.int32).reshape(1)
    grad, field, slope, inverse, canvas, head, tail, done = objects(
        intersection.reshape(1), early, chan_map, data.reshape(SLOTS, ROWS, N), pupil_mask, tabs
    )
    left = shifted(tail, "frame", True)
    right = shifted(head, "frame", False)
    grad = gradient(early, chan_map, done, grad, field, slope, inverse, tabs)
    grad = lax.all_to_all(
        grad.reshape(SLOTS, 1, 1, ZERN), "patch", split_axis=0, concat_axis=1, tiled=True
    )
    middle, head, tail = fold(canvas, left, right)
    upper = shifted(tail, "patch", True)
    lower = shifted(head, "patch", False)
    blended, grad = blend(middle, upper, lower, grad.reshape(SLOTS, ZERN))
    return (blended, grad.reshape(coeffs.shape))


def solution(mesh):
    in_specs = (
        P("patch", None, "frame", None),
        P("patch", None, "frame", None),
        P("patch", None, "frame", None, None),
        P(),
        P(),
        P("patch", "frame"),
    )
    out_specs = (P(None, "patch", "frame"), P("patch", None, "frame", None))
    return jax.shard_map(
        per_device, mesh=mesh, in_specs=in_specs, out_specs=out_specs, check_vma=False
    )
```

```python
import functools
import math

import jax
import jax.numpy as jnp
import ml_dtypes
import numpy as np
from jax import lax
from jax.experimental import pallas as pl
from jax.experimental.pallas import tpu as pltpu
from jax.sharding import PartitionSpec as P


N = 128
PUP = 64
ZERN = 36
SLOTS = 16
PAIRS = SLOTS // 2
CHANNELS = 2
PER = SLOTS // CHANNELS
MARGIN = 16
DEPTH = 8
TILE = N - 2 * MARGIN
HALF = 72
TWO = 2 * HALF
DEG = 9
DEG_ROWS = 16
BLOCKS = HALF // 8
COEF = 40
ROWS = N + 8
regular_gamma = 0.1
wave_ratio = 0.35
f32 = jnp.float32
bf16 = jnp.bfloat16
VM = pl.BlockSpec(memory_space=pltpu.VMEM)
SM = pl.BlockSpec(memory_space=pltpu.SMEM)
HB = pl.BlockSpec(memory_space=pltpu.HBM)


def noll_order(noll_index):
    radial = 0
    remain = noll_index - 1
    while remain > radial:
        radial += 1
        remain -= radial
    azimuth = radial % 2 + 2 * ((remain + (radial + 1) % 2) // 2)
    if noll_index % 2 == 1:
        azimuth = -azimuth
    return (radial, azimuth)


def zernike_modes():
    position = (np.arange(PUP) - (PUP - 1) / 2.0) / (PUP / 2.0)
    grid_y, grid_x = np.meshgrid(position, position, indexing="ij")
    radius = np.sqrt(grid_x * grid_x + grid_y * grid_y)
    theta = np.arctan2(grid_y, grid_x)
    modes = []
    for noll_index in range(2, ZERN + 2):
        radial, azimuth = noll_order(noll_index)
        order = abs(azimuth)
        total = np.zeros_like(radius)
        for step in range((radial - order) // 2 + 1):
            factor = math.factorial(radial - step) / (
                math.factorial(step)
                * math.factorial((radial + order) // 2 - step)
                * math.factorial((radial - order) // 2 - step)
            )
            total = total + (-1) ** step * factor * radius ** (radial - 2 * step)
        if azimuth == 0:
            modes.append(total * math.sqrt(radial + 1.0))
        elif azimuth > 0:
            modes.append(total * math.sqrt(2.0 * (radial + 1.0)) * np.cos(order * theta))
        else:
            modes.append(total * math.sqrt(2.0 * (radial + 1.0)) * np.sin(order * theta))
    return position, np.stack(modes)


def halves(table):
    high = table.astype(ml_dtypes.bfloat16)
    low = (table - high.astype(np.float64)).astype(ml_dtypes.bfloat16)
    return high, low


def pair_table(table):
    return np.stack(halves(table))


@functools.cache
def tables():
    index = np.arange(N)
    turns = 2.0 * np.pi / N * (np.outer(index, index) % N)
    c, s = np.cos(turns), np.sin(turns)
    cp, sp = c[:, :PUP], s[:, :PUP]
    ch, sh = c[:HALF], s[:HALF]
    distance = np.minimum(index, N - 1 - index)
    taper = np.where(distance < MARGIN, 0.5 - 0.5 * np.cos(np.pi * (distance + 0.5) / MARGIN), 1.0)
    weight = np.where(np.arange(HALF) < 1, 1.0, 2.0)
    weight[N // 2] = 1.0
    weight[N // 2 + 1 :] = 0.0
    out = {}
    out["right_pupil"] = pair_table(np.block([[cp.T, -sp.T], [sp.T, cp.T]]))
    out["left_pupil"] = pair_table(np.block([[cp, sp], [-sp, cp]]))
    out["left_half"] = pair_table(np.block([[ch], [-sh]]))
    out["right_full"] = pair_table(np.block([[c, -s], [s, c]]))
    out["right_back"] = pair_table(np.block([[c, s], [-s, c]]))
    high, low = halves(np.block([[ch], [-sh]]) * taper[None, :])
    out["left_taper"] = np.concatenate([high, low], axis=1)
    high, low = halves(np.concatenate([weight[None] * ch.T, -weight[None] * sh.T], axis=1))
    out["left_back"] = np.concatenate([high, high, low], axis=1)
    out["taper"] = np.tile(taper, 2)[None].astype(np.float32)
    out["weight"] = np.broadcast_to(weight[:, None] / 2.0, (HALF, N)).astype(np.float32)
    position, modes = zernike_modes()
    cheb = np.polynomial.chebyshev.chebvander(position, DEG - 1)
    fit = np.linalg.lstsq(cheb, modes.transpose(1, 0, 2).reshape(PUP, -1), rcond=None)[0]
    fit = fit.reshape(DEG, ZERN, PUP).transpose(1, 0, 2)
    phase = np.zeros((COEF, DEG, PUP))
    phase[:ZERN] = fit
    step = 2.0 * np.pi / N * (PUP / 2.0)
    phase[ZERN, 1] = step
    phase[ZERN + 1, 0] = step * position
    phase = np.concatenate([phase, phase], axis=2)
    out["phase"] = (phase / (2.0 * np.pi)).reshape(COEF, DEG * N).astype(np.float32)
    spread = np.zeros((DEG_ROWS, PUP))
    spread[:DEG] = cheb.T
    high, low = halves(spread)
    out["sums"] = np.concatenate([high, high, low], axis=1)
    return out, cheb


def split(x):
    high = x.astype(bf16)
    return high, (x - high.astype(f32)).astype(bf16)


def dot(left, right):
    return lax.dot_general(left, right, (((1,), (0,)), ((), ())), preferred_element_type=f32)


def rows3(x):
    high, low = split(x)
    return jnp.concatenate([high, low, high], axis=0)


def table_rows(ref):
    return jnp.concatenate([ref[0], ref[0], ref[1]], axis=0)


def table_lanes(ref):
    return jnp.concatenate([ref[0], ref[0], ref[1]], axis=1)


def swap_halves(y, count):
    top = jnp.concatenate([y[:count, :N], y[count:, :N]], axis=1)
    low = jnp.concatenate([y[:count, N:], y[count:, N:]], axis=1)
    return jnp.concatenate([top, low], axis=0)


SINE = (3.141592616, -5.167708583, 2.55005456, -0.5981644139, 0.07742681132)
COSINE = (0.9999999532, -4.934792831, 4.058411353, -1.331876568, 0.2196896111)


def blocked(y):
    pieces = []
    for block in range(BLOCKS):
        rows = slice(block * 8, block * 8 + 8)
        im_rows = slice(HALF + block * 8, HALF + block * 8 + 8)
        for which in range(2):
            lanes = slice(which * N, (which + 1) * N)
            pieces.append(jnp.concatenate([y[rows, lanes], y[im_rows, lanes]], axis=1))
    return jnp.concatenate(pieces, axis=0)


def store_blocked(y, pair, base, yh_ref, yl_ref):
    high, low = split(blocked(y))
    rows = slice(base + pair * 16, base + pair * 16 + 16)
    for block in range(BLOCKS):
        yh_ref[block, rows, :] = high[block * 16 : block * 16 + 16]
        yl_ref[block, rows, :] = low[block * 16 : block * 16 + 16]


def chebyshev_sum(parts, cheb, row):
    total = parts[0]
    for i in range(1, DEG):
        total = total + float(cheb[row, i]) * parts[i]
    return total


def series(factors, square):
    total = factors[-1] * square + factors[-2]
    for factor in factors[-3::-1]:
        total = total * square + factor
    return total


def turned(turns):
    rest = turns - jnp.round(turns)
    square = rest * rest
    sine = rest * series(SINE, square)
    twice = sine + sine
    return 1.0 - twice * sine, twice * series(COSINE, square)


def slot_scales(chan_ref, width):
    row = lax.broadcasted_iota(jnp.int32, (SLOTS, width), 0)
    channel = jnp.zeros((SLOTS, width), jnp.int32)
    for slot in range(SLOTS):
        channel = jnp.where(row == slot, chan_ref[slot], channel)
    return 1.0 / (1.0 + wave_ratio * channel.astype(f32))


def transfer_part(
    data_ref, chan_ref, mask_ref, phase_ref, rp_ref, lp_ref, lh_ref, ready, spectra,
    field_ref, slope_ref,
    line_ref, wide_ref, ph_ref, pl_ref, half_re_ref, half_im_ref, power_ref, yh_ref, yl_ref,
):
    cheb = tables()[1]
    for slot in range(SLOTS):
        line_ref[slot * 8 : slot * 8 + 8, :] = data_ref[slot, N:, :].astype(f32)
    line = line_ref[pl.ds(0, SLOTS, stride=8), :]
    coef = line + (pltpu.roll(line, N - ZERN, 1) + pltpu.roll(line, N - 2 * ZERN, 1))
    lane = lax.broadcasted_iota(jnp.int32, (SLOTS, N), 1)
    shift = pltpu.roll(line, N - 2 * ZERN, 1)
    coef = jnp.where(lane < ZERN, coef * slot_scales(chan_ref, N), shift)[:, :COEF]
    mask = mask_ref[...].astype(f32)
    wide_ref[...] = jnp.concatenate([mask, mask], axis=1)
    parts_all = lax.dot_general(
        coef, phase_ref[...], (((1,), (0,)), ((), ())),
        precision=lax.Precision.HIGHEST, preferred_element_type=f32,
    )
    first = lax.broadcasted_iota(jnp.int32, (SLOTS, N), 1) < PUP
    sign = jnp.where(first, 1.0, -1.0)
    parts = [parts_all[:, i * N : (i + 1) * N] for i in range(DEG)]
    parts = [part * sign if i % 2 else part for i, part in enumerate(parts)]
    for row in range(PUP // 2):
        if row % 4 == 0:
            spectra(row // 4)
        far = PUP - 1 - row
        cosine, sine = turned(chebyshev_sum(parts, cheb, row))
        mask = jnp.where(first, wide_ref[row : row + 1, :], wide_ref[far : far + 1, :])
        cosine = cosine * mask
        sine = sine * mask
        far_cosine = pltpu.roll(cosine, PUP, 1)
        far_sine = pltpu.roll(sine, PUP, 1)
        here = slice(row * SLOTS, (row + 1) * SLOTS)
        there = slice(far * SLOTS, (far + 1) * SLOTS)
        slope_ref[here, :] = jnp.where(first, -sine, far_cosine)
        slope_ref[there, :] = jnp.where(first, -far_sine, cosine)
        high, low = split(jnp.where(first, cosine, far_sine))
        ph_ref[here, :] = high
        pl_ref[here, :] = low
        high, low = split(jnp.where(first, far_cosine, sine))
        ph_ref[there, :] = high
        pl_ref[there, :] = low
        if row % 8 == 7:
            count = 8 * SLOTS
            near = slice((row - 7) * SLOTS, (row + 1) * SLOTS)
            back = slice(far * SLOTS, (far + 8) * SLOTS)
            high = jnp.concatenate([ph_ref[near, :], ph_ref[back, :]], axis=0)
            low = jnp.concatenate([pl_ref[near, :], pl_ref[back, :]], axis=0)
            if row == 7:
                ready()
            half = dot(jnp.concatenate([high, low, high], axis=1), table_rows(rp_ref))
            half_re_ref[near, :] = half[:count, :N]
            half_im_ref[near, :] = half[:count, N:]
            half_re_ref[back, :] = half[count:, :N]
            half_im_ref[back, :] = half[count:, N:]
    left = table_lanes(lp_ref)
    for pair in range(PAIRS):
        columns = []
        for part_ref in (half_re_ref, half_im_ref):
            columns.append(
                jnp.concatenate(
                    [part_ref[pl.ds(2 * pair + which, PUP, stride=SLOTS), :] for which in range(2)],
                    axis=1,
                )
            )
        field = dot(left, rows3(jnp.concatenate(columns, axis=0)))
        field_ref[pair] = field
        high, low = split(field[:N] * field[:N] + field[N:] * field[N:])
        power_ref[pair, :N] = high
        power_ref[pair, N:] = low
    left = table_lanes(lh_ref)
    for pair in range(PAIRS):
        high = power_ref[pair, :N]
        y = dot(left, jnp.concatenate([high, power_ref[pair, N:], high], axis=0))
        store_blocked(y, pair, 0, yh_ref, yl_ref)


def object_part(
    width_ref, slots, weight_ref, rf_ref, rb_ref, lb_ref,
    grad_ref, inv_ref, canvas_ref, head_ref, tail_ref,
    yh_ref, yl_ref, plane_ref, object_ref, inner_ref,
):
    right = table_rows(rf_ref)

    def transform(block):
        high = yh_ref[block]
        plane_ref[block] = dot(jnp.concatenate([high, yl_ref[block], high], axis=1), right)

    transform(0)
    for block in range(BLOCKS):
        if block + 1 < BLOCKS:
            transform(block + 1)
        if block == 0:
            for slot in range(SLOTS):
                inverse = 1.0 / plane_ref[0, slot * 8 : slot * 8 + 1, 0:1]
                inv_ref[slot * 8 : slot * 8 + 8, :] = jnp.broadcast_to(inverse, (8, N))
        for channel in range(CHANNELS):
            mine = slots[channel * PER : (channel + 1) * PER]
            where = [pl.ds(pl.multiple_of(slot * 8, 8), 8) for slot in mine]
            there = [pl.ds(pl.multiple_of(SLOTS * 8 + slot * 8, 8), 8) for slot in mine]
            inverse = [inv_ref[w, :] for w in where]
            h_re = [plane_ref[block, where[i], :N] * inverse[i] for i in range(PER)]
            h_im = [plane_ref[block, where[i], N:] * inverse[i] for i in range(PER)]
            s_re = [plane_ref[block, w, :N] for w in there]
            s_im = [plane_ref[block, w, N:] for w in there]
            num_re = num_im = 0.0
            den = regular_gamma
            for i in range(PER):
                num_re = num_re + (h_re[i] * s_re[i] + h_im[i] * s_im[i])
                num_im = num_im + (h_re[i] * s_im[i] - h_im[i] * s_re[i])
                den = den + (h_re[i] * h_re[i] + h_im[i] * h_im[i])
            recip = 1.0 / den
            o_re = num_re * recip
            o_im = num_im * recip
            rows = slice(channel * HALF + block * 8, channel * HALF + block * 8 + 8)
            object_ref[rows, :N] = o_re
            object_ref[rows, N:] = o_im
            scale = o_re * o_re + o_im * o_im
            for i in range(PER):
                g_re = scale * h_re[i] - (s_re[i] * o_re + s_im[i] * o_im)
                g_im = scale * h_im[i] - (s_im[i] * o_re - s_re[i] * o_im)
                match = g_re * h_re[i] + g_im * h_im[i]
                if block in (0, BLOCKS - 1):
                    match = match * weight_ref[block * 8 : block * 8 + 8, :]
                at = channel * PER + i
                inner_ref[at] = match if block == 0 else inner_ref[at] + match
                grad_ref[block, where[i], :N] = g_re
                grad_ref[block, where[i], N:] = g_im
    origin = (lax.broadcasted_iota(jnp.int32, (8, N), 0) == 0) & (
        lax.broadcasted_iota(jnp.int32, (8, N), 1) == 0
    )
    for at in range(SLOTS):
        total = jnp.sum(jnp.sum(inner_ref[at], axis=0, keepdims=True), axis=1, keepdims=True)
        w = pl.ds(pl.multiple_of(slots[at] * 8, 8), 8)
        grad_ref[0, w, :N] = grad_ref[0, w, :N] - jnp.where(origin, 2.0 * total, 0.0)
    high, low = split(object_ref[...] * (1.0 / (N * N)))
    z = dot(jnp.concatenate([high, low, high], axis=1), table_rows(rb_ref))
    image = dot(lb_ref[...], rows3(swap_halves(z, HALF)))
    width = width_ref[0].astype(f32) + 1.0
    row = lax.broadcasted_iota(jnp.int32, (N, N), 0)
    col = lax.broadcasted_iota(jnp.int32, (N, N), 1)

    def ramp(index):
        distance = (jnp.minimum(index, N - 1 - index) + 1).astype(f32)
        return jnp.minimum(1.0, distance / width)

    weight = ramp(row) * ramp(col)
    head_ref[CHANNELS] = weight[:MARGIN]
    tail_ref[CHANNELS] = weight[N - MARGIN :]
    canvas_ref[CHANNELS] = weight
    for channel in range(CHANNELS):
        shown = image[:, channel * N : (channel + 1) * N] * weight
        canvas_ref[channel] = shown
        turned = shown.T
        head_ref[channel] = turned[:MARGIN]
        tail_ref[channel] = turned[N - MARGIN :]


TABLES = ("right_pupil", "left_pupil", "left_half", "right_full", "right_back", "left_back")


def object_kernel(
    width_ref, early_ref, chan_ref, data_ref, mask_ref, phase_ref, lt_ref, taper_ref, weight_ref,
    sums_ref, rp_hbm, lp_hbm, lh_hbm, rf_hbm, rb_hbm, lb_hbm,
    grad_ref, field_ref, slope_ref, inv_ref, canvas_ref, head_ref, tail_ref, done_ref,
    rp_ref, lp_ref, lh_ref, rf_ref, rb_ref, lb_ref, sems,
    line_ref, wide_ref, ph_ref, pl_ref, half_re_ref, half_im_ref, power_ref, yh_ref, yl_ref,
    order_ref, plane_ref, object_ref, inner_ref, *scratch,
):
    moves = (
        (rp_hbm, rp_ref), (lp_hbm, lp_ref), (lh_hbm, lh_ref),
        (rf_hbm, rf_ref), (rb_hbm, rb_ref), (lb_hbm, lb_ref),
    )
    copies = [
        pltpu.make_async_copy(source, target, sems.at[i])
        for i, (source, target) in enumerate(moves)
    ]
    for copy in copies:
        copy.start()

    def ready():
        for copy in copies:
            copy.wait()

    at = [jnp.int32(0), jnp.int32(PER)]
    for slot in range(SLOTS):
        first = chan_ref[slot] == 0
        order_ref[jnp.where(first, at[0], at[1])] = slot
        at = [jnp.where(first, at[0] + 1, at[0]), jnp.where(first, at[1], at[1] + 1)]
    left = lt_ref[...]
    taper = taper_ref[...]

    def spectra(pair):
        image = jnp.concatenate([data_ref[2 * pair, :N, :], data_ref[2 * pair + 1, :N, :]], axis=1)
        y = dot(left, jnp.concatenate([image, image], axis=0)) * taper
        store_blocked(y, pair, SLOTS * 8, yh_ref, yl_ref)

    transfer_part(
        data_ref, chan_ref, mask_ref, phase_ref, rp_ref, lp_ref, lh_ref, ready, spectra,
        field_ref, slope_ref,
        line_ref, wide_ref, ph_ref, pl_ref, half_re_ref, half_im_ref, power_ref, yh_ref, yl_ref,
    )
    object_part(
        width_ref, [order_ref[i] for i in range(SLOTS)], weight_ref, rf_ref, rb_ref, lb_ref,
        grad_ref, inv_ref, canvas_ref, head_ref, tail_ref,
        yh_ref, yl_ref, plane_ref, object_ref, inner_ref,
    )
    done_ref[...] = jnp.zeros_like(done_ref)

    @pl.when(early_ref[0] == 1)
    def _():
        gradient_part(
            chan_ref, grad_ref, field_ref, slope_ref, inv_ref, phase_ref,
            rb_ref, lb_ref, rp_ref, lp_ref, sums_ref, done_ref, *scratch,
        )


def pack_kernel(coef_hbm, shift_hbm, pix_hbm, out_hbm, coef_ref, shift_ref, data_ref, line_ref, sems):
    coef_copy = pltpu.make_async_copy(coef_hbm, coef_ref, sems.at[0])
    shift_copy = pltpu.make_async_copy(shift_hbm, shift_ref, sems.at[1])
    chunks = [pl.ds(i * 4, 4) for i in range(4)]
    loads = [
        pltpu.make_async_copy(pix_hbm.at[c], data_ref.at[c], sems.at[2 + i])
        for i, c in enumerate(chunks)
    ]
    stores = [
        pltpu.make_async_copy(data_ref.at[c], out_hbm.at[c, :N, :], sems.at[6 + i])
        for i, c in enumerate(chunks)
    ]
    coef_copy.start()
    shift_copy.start()
    for load in loads:
        load.start()
    for load, store in zip(loads, stores):
        load.wait()
        store.start()
    coef_copy.wait()
    shift_copy.wait()
    coef = jnp.concatenate([coef_ref[...], jnp.zeros((SLOTS, N - ZERN), f32)], axis=1)
    first = coef.astype(bf16).astype(f32)
    rest = coef - first
    second = rest.astype(bf16).astype(f32)
    third = rest - second
    shift = jnp.concatenate([shift_ref[...].astype(f32), jnp.zeros((6, SLOTS), f32)], axis=0)
    shift = jnp.concatenate([shift, jnp.zeros((8, N - SLOTS), f32)], axis=1)
    shift = jnp.concatenate([shift, jnp.zeros((N - 8, N), f32)], axis=0).T[:SLOTS]
    line = first + pltpu.roll(second, ZERN, 1) + pltpu.roll(third, 2 * ZERN, 1)
    line = line + pltpu.roll(shift, 3 * ZERN, 1)
    for slot in range(SLOTS):
        line_ref[slot] = jnp.broadcast_to(line[slot : slot + 1], (8, N)).astype(bf16)
    line_store = pltpu.make_async_copy(line_ref, out_hbm.at[:, N:, :], sems.at[10])
    line_store.start()
    for store in stores:
        store.wait()
    line_store.wait()


def pack(coef, shift, pixels):
    return pl.pallas_call(
        pack_kernel,
        out_shape=jax.ShapeDtypeStruct((SLOTS, ROWS, N), bf16),
        in_specs=[HB] * 3,
        out_specs=HB,
        scratch_shapes=[
            pltpu.VMEM((SLOTS, ZERN), f32),
            pltpu.VMEM((2, SLOTS), jnp.int32),
            pltpu.VMEM((SLOTS, N, N), bf16),
            pltpu.VMEM((SLOTS, ROWS - N, N), bf16),
            pltpu.SemaphoreType.DMA((11,)),
        ],
        name="pack",
        compiler_params=limit(4),
    )(*[pltpu.with_memory_space_constraint(x, pltpu.HBM) for x in (coef, shift, pixels)])


def fold_kernel(
    canvas_ref, left_ref, right_ref,
    middle_ref, head_ref, tail_ref,
):
    gap = jnp.zeros((TILE - 2 * MARGIN, N), f32)
    rest = jnp.zeros((N - TILE, N), f32)
    for layer in range(CHANNELS + 1):
        sides = jnp.concatenate([left_ref[layer], gap, right_ref[layer], rest], axis=0).T
        total = pltpu.roll(canvas_ref[layer], N - MARGIN, 1) + sides
        head_ref[layer] = total[:MARGIN]
        middle_ref[layer] = total[MARGIN : N - MARGIN]
        tail_ref[layer] = total[N - MARGIN :]


def blend_kernel(middle_ref, upper_ref, lower_ref, grad_ref, out_ref, slope_ref):
    slope_ref[...] = grad_ref[...]

    def folded(layer):
        return jnp.concatenate(
            [
                middle_ref[layer, :MARGIN] + upper_ref[layer],
                middle_ref[layer, MARGIN : TILE - MARGIN],
                middle_ref[layer, TILE - MARGIN :] + lower_ref[layer],
            ],
            axis=0,
        )

    weight = folded(CHANNELS)
    for channel in range(CHANNELS):
        out_ref[channel] = (folded(channel) / weight)[:, :TILE]


def gradient_part(
    chan_ref, grad_ref, field_ref, slope_ref, inv_ref, phase_ref, rb_ref, lb_ref, rp_ref, lp_ref,
    sums_ref,
    out_ref,
    z_ref, back_ref, qh_ref, ql_ref, pupil_ref, total_ref,
):
    right = table_rows(rb_ref)
    for block in range(BLOCKS):
        high, low = split(grad_ref[block])
        z_ref[block] = dot(jnp.concatenate([high, low, high], axis=1), right)
    left = lb_ref[...]
    for pair in range(PAIRS):
        rows = []
        for part in range(2):
            lanes = slice(part * N, (part + 1) * N)
            for block in range(BLOCKS):
                at = pair * 16
                pieces = [z_ref[block, at + 8 * w : at + 8 * w + 8, lanes] for w in range(2)]
                rows.append(jnp.concatenate(pieces, axis=1))
        power = dot(left, rows3(jnp.concatenate(rows, axis=0)))
        field = field_ref[pair]
        high, low = split(jnp.concatenate([field[:N] * power, field[N:] * power], axis=0))
        back_ref[pair, : 2 * N] = high
        back_ref[pair, 2 * N :] = low
    left = table_lanes(rp_ref)
    for pair in range(PAIRS):
        high = back_ref[pair, : 2 * N]
        half = dot(left, jnp.concatenate([high, back_ref[pair, 2 * N :], high], axis=0))
        high, low = split(swap_halves(half, PUP))
        here = slice(pair * N, (pair + 1) * N)
        qh_ref[here, :] = high
        ql_ref[here, :] = low
    right = table_rows(lp_ref)
    for chunk in range(2):
        here = slice(chunk * 4 * N, (chunk + 1) * 4 * N)
        high = qh_ref[here, :]
        pupil_ref[here, :] = dot(jnp.concatenate([high, ql_ref[here, :], high], axis=1), right)
    left = sums_ref[...]
    for pair in range(PAIRS):
        both = []
        for which in range(2):
            slot = 2 * pair + which
            slope = slope_ref[pl.ds(slot, PUP, stride=SLOTS), :]
            both.append(pupil_ref[slot * PUP : (slot + 1) * PUP, :] * slope)
        out = dot(left, rows3(jnp.concatenate(both, axis=1)))
        for which in range(2):
            here = slice((2 * pair + which) * DEG_ROWS, (2 * pair + which + 1) * DEG_ROWS)
            total_ref[here, :] = out[:, which * N : (which + 1) * N]
    sums = [total_ref[pl.ds(i, SLOTS, stride=DEG_ROWS), :] for i in range(DEG)]
    total = lax.dot_general(
        jnp.concatenate(sums, axis=1), phase_ref[...], (((1,), (1,)), ((), ())),
        precision=lax.Precision.HIGHEST, preferred_element_type=f32,
    )
    factor = 8.0 * math.pi / float(N * N * N)
    inverse = inv_ref[pl.ds(0, SLOTS, stride=8), :]
    total = total * (slot_scales(chan_ref, COEF) * factor * inverse[:, :COEF])
    out_ref[...] = total[:, :ZERN]


def gradient_kernel(
    early_ref, chan_ref, done_ref, grad_ref, field_ref, slope_ref, inv_ref, phase_ref,
    rb_ref, lb_ref, rp_ref, lp_ref, sums_ref,
    out_ref,
    *scratch,
):
    @pl.when(early_ref[0] == 1)
    def _():
        out_ref[...] = done_ref[...]

    @pl.when(early_ref[0] == 0)
    def _():
        gradient_part(
            chan_ref, grad_ref, field_ref, slope_ref, inv_ref, phase_ref,
            rb_ref, lb_ref, rp_ref, lp_ref, sums_ref, out_ref, *scratch,
        )


GRADIENT_SCRATCH = (
    ((BLOCKS, SLOTS * 8, 2 * N), f32),
    ((PAIRS, 4 * N, 2 * N), bf16),
    ((SLOTS * PUP, 2 * N), bf16),
    ((SLOTS * PUP, 2 * N), bf16),
    ((SLOTS * PUP, N), f32),
    ((SLOTS * DEG_ROWS, N), f32),
)


def limit(mib):
    return pltpu.CompilerParams(vmem_limit_bytes=mib << 20)


def objects(width, early, chan, data, mask, tabs, interpret=False):
    margin = jax.ShapeDtypeStruct((CHANNELS + 1, MARGIN, N), f32)
    fixed = [tabs[name] for name in TABLES]
    return pl.pallas_call(
        object_kernel,
        out_shape=(
            jax.ShapeDtypeStruct((BLOCKS, SLOTS * 8, 2 * N), f32),
            jax.ShapeDtypeStruct((PAIRS, 2 * N, 2 * N), f32),
            jax.ShapeDtypeStruct((PUP * SLOTS, N), f32),
            jax.ShapeDtypeStruct((SLOTS * 8, N), f32),
            jax.ShapeDtypeStruct((CHANNELS + 1, N, N), f32),
            margin,
            margin,
            jax.ShapeDtypeStruct((SLOTS, ZERN), f32),
        ),
        in_specs=[SM] * 3 + [VM] * 7 + [HB] * len(TABLES),
        out_specs=(VM,) * 8,
        scratch_shapes=[pltpu.VMEM(table.shape, bf16) for table in fixed]
        + [
            pltpu.SemaphoreType.DMA((len(TABLES),)),
            pltpu.VMEM((SLOTS * 8, N), f32),
            pltpu.VMEM((PUP, N), f32),
            pltpu.VMEM((PUP * SLOTS, N), bf16),
            pltpu.VMEM((PUP * SLOTS, N), bf16),
            pltpu.VMEM((PUP * SLOTS, N), f32),
            pltpu.VMEM((PUP * SLOTS, N), f32),
            pltpu.VMEM((PAIRS, 2 * N, 2 * N), bf16),
            pltpu.VMEM((BLOCKS, SLOTS * 16, 2 * N), bf16),
            pltpu.VMEM((BLOCKS, SLOTS * 16, 2 * N), bf16),
            pltpu.SMEM((SLOTS,), jnp.int32),
            pltpu.VMEM((BLOCKS, SLOTS * 16, 2 * N), f32),
            pltpu.VMEM((TWO, 2 * N), f32),
            pltpu.VMEM((SLOTS, 8, N), f32),
        ]
        + [pltpu.VMEM(*piece) for piece in GRADIENT_SCRATCH],
        interpret=interpret,
        name="objects",
        compiler_params=limit(22),
    )(
        width, early, chan, data, mask, tabs["phase"], tabs["left_taper"], tabs["taper"],
        tabs["weight"], tabs["sums"], *fixed,
    )


def gradient(early, chan, done, grad, field, slope, inverse, tabs, interpret=False):
    return pl.pallas_call(
        gradient_kernel,
        out_shape=jax.ShapeDtypeStruct((SLOTS, ZERN), f32),
        in_specs=[SM, SM] + [VM] * 11,
        out_specs=VM,
        scratch_shapes=[pltpu.VMEM(*piece) for piece in GRADIENT_SCRATCH],
        interpret=interpret,
        name="gradient",
        compiler_params=limit(16),
    )(
        early, chan, done, grad, field, slope, inverse, tabs["phase"], tabs["right_back"],
        tabs["left_back"], tabs["right_pupil"], tabs["left_pupil"], tabs["sums"],
    )


def fold(canvas, left, right):
    margin = jax.ShapeDtypeStruct((CHANNELS + 1, MARGIN, N), f32)
    return pl.pallas_call(
        fold_kernel,
        out_shape=(
            jax.ShapeDtypeStruct((CHANNELS + 1, TILE, N), f32),
            margin,
            margin,
        ),
        in_specs=[VM] * 3,
        out_specs=(VM,) * 3,
        name="fold",
        compiler_params=limit(8),
    )(canvas, left, right)


def blend(middle, upper, lower, grad):
    return pl.pallas_call(
        blend_kernel,
        out_shape=(
            jax.ShapeDtypeStruct((CHANNELS, TILE, TILE), f32),
            jax.ShapeDtypeStruct((SLOTS, ZERN), f32),
        ),
        in_specs=[VM] * 4,
        out_specs=(VM,) * 2,
        name="blend",
        compiler_params=limit(8),
    )(middle, upper, lower, grad)


def shifted(cells, axis, forward):
    ends = lax.axis_size(axis) - 1
    if forward:
        return lax.ppermute(cells, axis, [(i, i + 1) for i in range(ends)])
    return lax.ppermute(cells, axis, [(i + 1, i) for i in range(ends)])


def per_device(coeffs, shifts, pixels, pupil_mask, chan_map, intersection):
    tabs = {name: jnp.asarray(table) for name, table in tables()[0].items()}
    coef = coeffs.reshape(SLOTS, ZERN)
    shift = shifts.reshape(SLOTS, 2).T
    data = pack(coef, shift, pixels.reshape(SLOTS, N, N)).reshape(1, SLOTS, 1, ROWS, N)
    data = lax.all_to_all(data, "patch", split_axis=1, concat_axis=0, tiled=True)
    early = ((lax.axis_index("frame") % DEPTH) == 0).astype(jnp.int32).reshape(1)
    grad, field, slope, inverse, canvas, head, tail, done = objects(
        intersection.reshape(1), early, chan_map, data.reshape(SLOTS, ROWS, N), pupil_mask, tabs
    )
    left = shifted(tail, "frame", True)
    right = shifted(head, "frame", False)
    grad = gradient(early, chan_map, done, grad, field, slope, inverse, tabs)
    grad = lax.all_to_all(
        grad.reshape(SLOTS, 1, 1, ZERN), "patch", split_axis=0, concat_axis=1, tiled=True
    )
    middle, head, tail = fold(canvas, left, right)
    lower = shifted(head, "patch", False)
    upper = shifted(tail, "patch", True)
    blended, grad = blend(middle, upper, lower, grad.reshape(SLOTS, ZERN))
    return (blended, grad.reshape(coeffs.shape))


def solution(mesh):
    in_specs = (
        P("patch", None, "frame", None),
        P("patch", None, "frame", None),
        P("patch", None, "frame", None, None),
        P(),
        P(),
        P("patch", "frame"),
    )
    out_specs = (P(None, "patch", "frame"), P("patch", None, "frame", None))
    return jax.shard_map(
        per_device, mesh=mesh, in_specs=in_specs, out_specs=out_specs, check_vma=False
    )
```
